32 devices in a mesh: crops: 2 (over y), xy: 4 (over z), gz: 2 (over x), lab: 2 (over core).
Axes of the slice: x: 2, y: 2, z: 4, core: 2. Of those that a mesh axis runs over, the one named last changes fastest.
Arguments:
- image: bfloat16 [16, 32, 64, 128], P('lab', ('crops', 'xy'), 'gz'), parts along dimension 1, may hold values from -6 to 6
- filt: bfloat16 [3, 16, 3, 3, 3], replicated, may hold values from -0.3125 to 0.3125
- planted_colours: int32 [32, 64, 128], P(('crops', 'xy'), 'gz'), parts along dimension 0, may hold values from 0 to 63
- likelihoods: float32 [8, 32, 64, 128], P('lab', ('crops', 'xy'), 'gz'), parts along dimension 1, may hold values from 0 to 1
- loss_slope: float32 [8, 32, 64, 128], P('lab', ('crops', 'xy'), 'gz'), parts along dimension 1, may hold values from -5.25 to 5.25
Outputs:
- grad_image: bfloat16 [16, 32, 64, 128], P('lab', ('crops', 'xy'), 'gz'), parts along dimension 1
- grad_filter: float32 [6, 16, 3, 3, 3], P('crops', 'lab'), parts along dimension 0
The draws below stay inside these ranges and needn't reach their ends.
There are 2 independent parts, one for each index of `crops`. The reference program is written for one: setup_inputs(seed, part) draws one part's arguments, and reference() takes and returns one part's arrays. A program takes and returns all parts, laid end to end along the dimension named above; an argument that names none is the same for every part. Nothing has to cross between parts.
Inputs may be any that keep to these rules, and one draw needn't show every extreme that they name: `planted_colours`: A value below 8 marks a seed of that colour; any other value marks an unseeded cell.
All inputs are finite; a program needn't handle non-finite values.
Results may differ from the reference program's by a relative error of at most 0.015.
Values may be sent and summed in bfloat16 or wider, within the bound.
No kernel may reach another device: no remote copies, remote signals or barrier semaphores. Data moves between devices by JAX's collectives and lax.ppermute only.
A program may use at most 64 MiB of HBM per device.

```python
import math
import jax
import jax.numpy as jnp

CHANNELS = 16
START_COLOURS = 8
ITERS = 3
NY = 128
NX = 16
NZ = 64


def draw_loss_slope(key, part):
    keys = jax.random.split(key, 4)
    shape = (START_COLOURS, NX, NZ, NY)
    first_pos = jnp.arange(NX, dtype=jnp.int32)[None, :, None, None]
    second_pos = jnp.arange(NZ, dtype=jnp.int32)[None, None, :, None]
    region = (2 * first_pos + 1) * NZ + (2 * second_pos + 1) * NX > 2 * NX * NZ
    region = jnp.broadcast_to(region, shape)
    first_frac = jnp.arange(NX, dtype=jnp.float32)[None, :, None, None] / NX
    third_frac = jnp.arange(NY, dtype=jnp.float32)[None, None, None, :] / NY
    phase_one = jax.random.uniform(keys[0], (START_COLOURS, 1, 1, 1), jnp.float32, 0.0, 1.0)
    phase_two = jax.random.uniform(keys[1], (START_COLOURS, 1, 1, 1), jnp.float32, 0.0, 1.0)
    wave = 2.5 * jnp.sin(2.0 * math.pi * (first_frac + phase_one)) * jnp.cos(2.0 * math.pi * (third_frac + phase_two))
    wave = jnp.broadcast_to(wave, shape)
    rough_part = 1.5 * jnp.clip(jax.random.normal(keys[2], shape, jnp.float32), -3.5, 3.5)
    quiet_noise = 0.3 * jnp.clip(jax.random.normal(keys[3], shape, jnp.float32), -3.0, 3.0)
    return jnp.where(region, rough_part, wave + quiet_noise).astype(jnp.float32)


def set_ends(result, stream_key, low, largest):
    dims = result.shape
    place = [jax.random.randint(jax.random.fold_in(stream_key, axis), (), 0, dims[axis]) for axis in range(len(dims))]
    result = result.at[tuple(place)].set(low)
    longest = dims.index(max(dims))
    place[longest] = (place[longest] + 1) % dims[longest]
    return result.at[tuple(place)].set(largest)


def block_scale(own_key, extent, shards, smallest, high):
    def one(dim, shards_of):
        draws = jax.random.uniform(jax.random.fold_in(jax.random.fold_in(own_key, 6), dim), (shards_of,), jnp.float32, smallest / len(shards), high / len(shards))
        return jnp.repeat(jnp.exp(draws), extent[dim] // shards_of).reshape((-1,) + (1,) * (len(extent) - dim - 1))

    gain = one(*shards[0])
    for cut in shards[1:]:
        gain = gain * one(*cut)
    return gain


def gaussian(own_key, extent, width, bound, cuts=(), kind=jnp.bfloat16):
    loudness = block_scale(own_key, extent, cuts, -0.22, 0.18) if cuts else 1.0
    values = jax.random.normal(own_key, extent, jnp.float32) * width * loudness
    return jnp.minimum(jnp.maximum(values, -bound), bound).astype(kind)


def setup_inputs(seed: int = 0, part: int = 0) -> dict:
    key_list = jax.random.split(jax.random.key(seed), 6)
    part_keys = jax.random.split(jax.random.fold_in(key_list[5], part), 6)
    return {
        "image": gaussian(part_keys[0], (CHANNELS, NX, NZ, NY), 1.0, 6.0, ((0, 2), (1, 4), (2, 2))),
        "filt": gaussian(key_list[1], (3, CHANNELS, 3, 3, 3), (CHANNELS * 27) ** -0.5, 0.3125),
        "planted_colours": set_ends(jax.random.randint(part_keys[2], (NX, NZ, NY), 0, 8 * START_COLOURS), jax.random.fold_in(part_keys[2], 1), 0, (8 * START_COLOURS) - 1).astype(jnp.int32),
        "likelihoods": jnp.clip(1.0 * jax.random.uniform(part_keys[3], (START_COLOURS, NX, NZ, NY), jnp.float32) ** block_scale(part_keys[3], (START_COLOURS, NX, NZ, NY), ((0, 2), (1, 4), (2, 2)), -0.2, 0.2), 0.0, 1.0),
        "loss_slope": draw_loss_slope(jax.random.fold_in(jax.random.fold_in(key_list[5], part), 71), part),
    }


def offsets():
    return [(first, second, third) for first in range(3) for second in range(3) for third in range(3)]


def reference(image, filt, planted_colours, likelihoods, loss_slope):
    wide = jnp.pad(image.astype(jnp.float32), ((0, 0), (1, 1), (1, 1), (1, 1)))
    filt_wide = filt.astype(jnp.float32)
    logits = jnp.zeros((3, NX, NZ, NY), jnp.float32)
    for first, second, third in offsets():
        window = wide[:, first:first + NX, second:second + NZ, third:third + NY]
        logits = logits + jnp.einsum("dc,cxzy->dxzy", filt_wide[:, :, first, second, third], window)
    shape = (NX, NZ, NY)
    along_x = jnp.broadcast_to((jnp.arange(NX) < NX - 1)[:, None, None], shape)
    along_z = jnp.broadcast_to((jnp.arange(NZ) < NZ - 1)[None, :, None], shape)
    along_y = jnp.broadcast_to((jnp.arange(NY) < NY - 1)[None, None, :], shape)
    edge_valid = jnp.stack([along_x, along_z, along_y]).astype(jnp.float32)
    squashed = jax.nn.sigmoid(logits)
    weight = (0.05 + squashed) * edge_valid
    lower_x = jnp.pad(weight[0], ((1, 0), (0, 0), (0, 0)))[:-1]
    lower_z = jnp.pad(weight[1], ((0, 0), (1, 0), (0, 0)))[:, :-1]
    lower_y = jnp.pad(weight[2], ((0, 0), (0, 0), (1, 0)))[:, :, :-1]
    free_cell_flags = (planted_colours >= START_COLOURS).astype(jnp.float32)
    class_membership = (planted_colours[None] == jnp.arange(START_COLOURS, dtype=jnp.int32)[:, None, None, None]).astype(jnp.float32)
    entire_grid_state = free_cell_flags[None] * likelihoods + class_membership

    def operate(field):
        padded = jnp.pad(field, ((0, 0), (1, 1), (1, 1), (1, 1)))
        grand_quantity = weight[0] * (field - padded[:, 2:, 1:-1, 1:-1]) + lower_x * (field - padded[:, :-2, 1:-1, 1:-1])
        grand_quantity = grand_quantity + weight[1] * (field - padded[:, 1:-1, 2:, 1:-1]) + lower_z * (field - padded[:, 1:-1, :-2, 1:-1])
        grand_quantity = grand_quantity + weight[2] * (field - padded[:, 1:-1, 1:-1, 2:]) + lower_y * (field - padded[:, 1:-1, 1:-1, :-2])
        return free_cell_flags[None] * grand_quantity

    def inner(left, right):
        return jnp.sum(left * right, axis=(1, 2, 3))[:, None, None, None]

    adjoint = jnp.zeros_like(likelihoods)
    remainder_grid = free_cell_flags[None] * loss_slope
    direction = remainder_grid
    norm_now = inner(remainder_grid, remainder_grid)
    for count in range(ITERS):
        picture_pixels_flat = operate(direction)
        alpha = norm_now / inner(direction, picture_pixels_flat)
        adjoint = adjoint + alpha * direction
        remainder_grid = remainder_grid - alpha * picture_pixels_flat
        norm_next = inner(remainder_grid, remainder_grid)
        direction = remainder_grid + (norm_next / norm_now) * direction
        norm_now = norm_next

    def above(field, axis):
        widths = [(0, 0)] * 4
        widths[axis] = (0, 1)
        padded = jnp.pad(field, widths)
        return lax_slice(padded, axis)

    def lax_slice(padded, axis):
        if axis == 1:
            return padded[:, 1:]
        if axis == 2:
            return padded[:, :, 1:]
        return padded[:, :, :, 1:]

    grads = []
    for axis in (1, 2, 3):
        step_adjoint = adjoint - above(adjoint, axis)
        step_full = entire_grid_state - above(entire_grid_state, axis)
        grads.append(-jnp.sum(step_adjoint * step_full, axis=0))
    edge_grad = jnp.stack(grads)
    logit_grad = (edge_grad * squashed * (1.0 - squashed) * edge_valid).astype(jnp.bfloat16)
    grad_wide = jnp.pad(logit_grad.astype(jnp.float32), ((0, 0), (1, 1), (1, 1), (1, 1)))
    logit_wide = logit_grad.astype(jnp.float32)
    grad_image = jnp.zeros((CHANNELS, NX, NZ, NY), jnp.float32)
    filter_terms = []
    for first, second, third in offsets():
        window = grad_wide[:, 2 - first:2 - first + NX, 2 - second:2 - second + NZ, 2 - third:2 - third + NY]
        grad_image = grad_image + jnp.einsum("dc,dxzy->cxzy", filt_wide[:, :, first, second, third], window)
        image_window = wide[:, first:first + NX, second:second + NZ, third:third + NY]
        filter_terms.append(jnp.einsum("dxzy,cxzy->dc", logit_wide, image_window))
    grad_filter = jnp.stack(filter_terms, axis=-1).reshape(3, CHANNELS, 3, 3, 3)
    return grad_image.astype(jnp.bfloat16), grad_filter
```

```python
import jax
import jax.numpy as jnp
from jax import lax
from jax.sharding import PartitionSpec as P

HALO = 4
SEED = 64.0
SPREAD = 6.3


def pair_routes(count, phase):
    route = []
    for low in range(phase, count - 1, 2):
        route += [(low, low + 1), (low + 1, low)]
    return route


def swap(block, axis, phase):
    return lax.ppermute(block, axis, pair_routes(lax.axis_size(axis), phase))


def neighbours(upward, downward, axis):
    even = lax.axis_index(axis) % 2 == 0
    first = swap(jnp.where(even, upward, downward), axis, 0)
    if lax.axis_size(axis) > 2:
        second = swap(jnp.where(even, downward, upward), axis, 1)
    else:
        second = jnp.zeros_like(first)
    return jnp.where(even, first, second), jnp.where(even, second, first)


def shared_neighbours(upward, downward, axis):
    count = lax.axis_size(axis)
    lab_count = lax.axis_size("lab")
    route = [
        (src * lab_count + lab, dst * lab_count + lab)
        for lab in range(lab_count)
        for src, dst in pair_routes(count, lab % 2)
    ]
    up = (lax.axis_index(axis) + lax.axis_index("lab")) % 2 == 0
    mine = lax.ppermute(jnp.where(up, upward, downward), (axis, "lab"), route)
    other = lax.ppermute(mine, "lab", [(0, 1), (1, 0)])
    return jnp.where(up, mine, other), jnp.where(up, other, mine)


def offsets():
    return [(i, j, k) for i in range(3) for j in range(3) for k in range(3)]


def total(part, axes):
    count = 1
    for axis in axes:
        count *= lax.axis_size(axis)
    copies = jnp.broadcast_to(part[None], (count,) + part.shape)
    return jnp.sum(lax.all_to_all(copies, axes, 0, 0), axis=0)


def up(field, dim):
    return jnp.roll(field, -1, dim)


def down(field, dim):
    return jnp.roll(field, 1, dim)


def wrap(own, above, below, dim):
    return jnp.concatenate([own, above, below], axis=dim)


def local(image, filt, planted, likelihoods, loss_slope):
    channels = image.shape[0]
    labels, rows_x, rows_z, rows_y = likelihoods.shape
    lab = lax.axis_index("lab")
    colour_count = labels * lax.axis_size("lab")
    bf16, f32 = jnp.bfloat16, jnp.float32
    own_filt = lax.dynamic_slice_in_dim(filt, lab * channels, channels, 1)
    free = (planted >= colour_count)[None]
    colours = lab * labels + jnp.arange(labels, dtype=jnp.int32)
    member = (planted[None] == colours[:, None, None, None]).astype(f32)
    full = free.astype(f32) * likelihoods + member
    rhs = jnp.where(free, loss_slope, SEED)

    def grow(own, width, axis, dim):
        size = own.shape[dim]
        last = lax.slice_in_dim(own, size - width, size, axis=dim)
        first = lax.slice_in_dim(own, 0, width, axis=dim)
        return last, first

    def exchange(fields, axis, dim):
        shapes, ups, downs = [], [], []
        for own, width in fields:
            last, first = grow(own.astype(bf16), width, axis, dim)
            shapes.append(last.shape)
            ups.append(last.reshape(-1, rows_y))
            downs.append(first.reshape(-1, rows_y))
        above, below = neighbours(jnp.concatenate(ups), jnp.concatenate(downs), axis)
        out, at = [], 0
        for (own, width), shape in zip(fields, shapes):
            rows = 1
            for n in shape[:-1]:
                rows *= n
            out.append(
                wrap(
                    own,
                    above[at : at + rows].reshape(shape).astype(own.dtype),
                    below[at : at + rows].reshape(shape).astype(own.dtype),
                    dim,
                )
            )
            at += rows
        return out

    image_z, rhs_z, full_z = exchange([(image, 1), (rhs, HALO), (full, 2)], "gz", 2)
    image_w, rhs_w, full_w = exchange([(image_z, 1), (rhs_z, HALO), (full_z, 2)], "xy", 1)

    def window(field, i, j, k):
        shifted = jnp.roll(field, (1 - i, 1 - j), (1, 2))[:, :rows_x, :rows_z]
        padded = jnp.pad(shifted, ((0, 0), (0, 0), (0, 0), (1, 1)))
        return padded[..., k : k + rows_y]

    part = jnp.zeros((3, rows_x, rows_z, rows_y), f32)
    for i, j, k in offsets():
        part = part + jnp.einsum(
            "dc,cxzy->dxzy", own_filt[:, :, i, j, k], window(image_w, i, j, k), preferred_element_type=f32
        )
    logits = part + lax.ppermute(part, "lab", [(0, 1), (1, 0)])

    last, first = grow(logits.astype(bf16), HALO, "gz", 2)
    above, below = neighbours(last, first, "gz")
    logits_z = wrap(logits, above.astype(f32), below.astype(f32), 2)
    last, first = grow(logits_z.astype(bf16), HALO, "xy", 1)
    above, below = shared_neighbours(last, first, "xy")
    logits_w = wrap(logits_z, above.astype(f32), below.astype(f32), 1)

    def place(rows, axis):
        i = jnp.arange(rows + 2 * HALO, dtype=jnp.int32)
        i = jnp.where(i < rows + HALO, i, i - rows - 2 * HALO)
        return i + lax.axis_index(axis) * rows, rows * lax.axis_size(axis)

    at_x, size_x = place(rows_x, "xy")
    at_z, size_z = place(rows_z, "gz")
    at_y = jnp.arange(rows_y, dtype=jnp.int32)
    in_x, in_z = (at_x >= 0) & (at_x < size_x), (at_z >= 0) & (at_z < size_z)
    next_x, next_z = (at_x >= 0) & (at_x < size_x - 1), (at_z >= 0) & (at_z < size_z - 1)
    next_y = at_y < rows_y - 1
    valid = jnp.stack(
        [
            next_x[:, None, None] & in_z[None, :, None] & jnp.ones((1, 1, rows_y), bool),
            in_x[:, None, None] & next_z[None, :, None] & jnp.ones((1, 1, rows_y), bool),
            in_x[:, None, None] & in_z[None, :, None] & next_y[None, None, :],
        ]
    ).astype(f32)
    squashed = jax.nn.sigmoid(logits_w)
    weight = (0.05 + squashed) * valid
    free_w = (rhs_w < SEED / 2).astype(f32)
    v0 = rhs_w * free_w
    fw = free_w[0]

    def operate(v):
        out = 0.0
        for d in range(3):
            flow = weight[d] * (v - up(v, d + 1))
            out = out + flow - down(flow, d + 1)
        return fw * out

    v1 = operate(v0) * (1.0 / SPREAD) - v0
    v2 = 2.0 * (operate(v1) * (1.0 / SPREAD) - v1) - v0
    av2 = operate(v2)

    def dot(a, b):
        return jnp.sum((a * b)[:, :rows_x, :rows_z], axis=(1, 2, 3))

    dots = jnp.stack([dot(v0, v0), dot(v0, v1), dot(v1, v1), dot(v1, v2), dot(v2, v2), dot(v2, av2)])
    dots = jnp.pad(dots, ((0, 2), (0, 128 - labels)))
    g00, g01, g11, g12, g22, k22 = total(dots, ("xy", "gz"))[:6, :labels]
    g02 = 2.0 * g11 - g00
    k00 = SPREAD * (g00 + g01)
    k01 = SPREAD * (g01 + g11)
    k02 = SPREAD * (g02 + g12)
    k11 = SPREAD * (g11 + 0.5 * (g12 + g01))
    k12 = SPREAD * (g12 + 0.5 * (g22 + g02))
    alpha = g00 / k00
    c0 = alpha
    r0 = 1.0 - alpha * SPREAD
    r1 = -alpha * SPREAD
    rr = r0 * r0 * g00 + 2.0 * r0 * r1 * g01 + r1 * r1 * g11
    beta = rr / g00
    p0, p1 = r0 + beta, r1
    alpha = rr / (p0 * p0 * k00 + 2.0 * p0 * p1 * k01 + p1 * p1 * k11)
    c0, c1 = c0 + alpha * p0, alpha * p1
    r0 = r0 - alpha * SPREAD * (p0 + 0.5 * p1)
    r1 = r1 - alpha * SPREAD * (p0 + p1)
    r2 = -alpha * SPREAD * 0.5 * p1
    rr_next = (
        r0 * r0 * g00 + r1 * r1 * g11 + r2 * r2 * g22 + 2.0 * (r0 * r1 * g01 + r0 * r2 * g02 + r1 * r2 * g12)
    )
    beta = rr_next / rr
    p0, p1, p2 = r0 + beta * p0, r1 + beta * p1, r2
    alpha = rr_next / (
        p0 * p0 * k00 + p1 * p1 * k11 + p2 * p2 * k22 + 2.0 * (p0 * p1 * k01 + p0 * p2 * k02 + p1 * p2 * k12)
    )
    c0, c1, c2 = c0 + alpha * p0, c1 + alpha * p1, alpha * p2
    spread = lambda c: c[:, None, None, None]
    lam = spread(c0) * v0 + spread(c1) * v1 + spread(c2) * v2

    def ring(field, dim, rows, width):
        size = field.shape[dim]
        return jnp.concatenate(
            [
                lax.slice_in_dim(field, 0, rows + width, axis=dim),
                lax.slice_in_dim(field, size - width, size, axis=dim),
            ],
            axis=dim,
        )

    def narrow(field, width):
        return ring(ring(field, 1, rows_x, width), 2, rows_z, width)

    lam = narrow(lam, 2)
    parts = []
    for d in range(3):
        parts.append(-jnp.sum((lam - up(lam, d + 1)) * (full_w - up(full_w, d + 1)), axis=0))
    edge = jnp.stack(parts)
    edge = edge + lax.ppermute(edge, "lab", [(0, 1), (1, 0)])
    s = narrow(squashed, 2)
    logit_grad = (edge * s * (1.0 - s) * narrow(valid, 2)).astype(bf16)

    grad_image = jnp.zeros((channels, rows_x, rows_z, rows_y), f32)
    terms = []
    own_grad = logit_grad[:, :rows_x, :rows_z]
    for i, j, k in offsets():
        grad_image = grad_image + jnp.einsum(
            "dc,dxzy->cxzy",
            own_filt[:, :, i, j, k],
            window(logit_grad, 2 - i, 2 - j, 2 - k),
            preferred_element_type=f32,
        )
        terms.append(
            jnp.einsum("dxzy,cxzy->dc", own_grad, window(image_w, i, j, k), preferred_element_type=f32)
        )
    part = jnp.stack(terms, axis=-1).reshape(3 * channels, 27)
    part = jnp.pad(part, ((0, 0), (0, 128 - 27)))
    grad_filter = total(part, ("xy", "gz"))[:, :27].reshape(3, channels, 3, 3, 3)
    return grad_image.astype(bf16), grad_filter


def solution(mesh):
    return jax.shard_map(
        local,
        mesh=mesh,
        in_specs=(
            P("lab", ("crops", "xy"), "gz", None),
            P(),
            P(("crops", "xy"), "gz", None),
            P("lab", ("crops", "xy"), "gz", None),
            P("lab", ("crops", "xy"), "gz", None),
        ),
        out_specs=(P("lab", ("crops", "xy"), "gz", None), P("crops", "lab", None, None, None)),
        check_vma=False,
    )
```

```python
import functools

import jax
import jax.numpy as jnp
from jax import lax
from jax.experimental import pallas as pl
from jax.experimental.pallas import tpu as pltpu
from jax.sharding import PartitionSpec as P

HALO = 4
SEED = 64.0
SPREAD = 6.3
TILE = 8
LANES = 128
BF16, F32 = jnp.bfloat16, jnp.float32
EVEN_X, EVEN_Z, FIRST_X, FIRST_Z, COLOUR, UP = range(6)


def pair_routes(count, phase):
    route = []
    for low in range(phase, count - 1, 2):
        route += [(low, low + 1), (low + 1, low)]
    return route


def swap(block, axis, phase):
    return lax.ppermute(block, axis, pair_routes(lax.axis_size(axis), phase))


def lab_swap(block):
    return lax.ppermute(block, "lab", [(0, 1), (1, 0)])


def split_swap(block, axis):
    labs = lax.axis_size("lab")
    route = [
        (src * labs + lab, dst * labs + lab)
        for lab in range(labs)
        for src, dst in pair_routes(lax.axis_size(axis), lab % 2)
    ]
    return lax.ppermute(block, (axis, "lab"), route)


def everyones(part, axes):
    count = 1
    for axis in axes:
        count *= lax.axis_size(axis)
    return lax.all_to_all(jnp.broadcast_to(part[None], (count,) + part.shape), axes, 0, 0)


def call(kernel, outs, *ins, scratch=(), flops=1_000_000, name=None):
    specs = [pl.BlockSpec(memory_space=pltpu.SMEM)]
    specs += [pl.BlockSpec(memory_space=pltpu.VMEM)] * (len(ins) - 1)
    bytes_moved = sum(a.size * a.dtype.itemsize for a in ins)
    return pl.pallas_call(
        kernel,
        out_shape=outs,
        in_specs=specs,
        out_specs=jax.tree.map(lambda _: pl.BlockSpec(memory_space=pltpu.VMEM), outs),
        scratch_shapes=list(scratch),
        compiler_params=pltpu.CompilerParams(vmem_limit_bytes=40 * 2**20),
        cost_estimate=pl.CostEstimate(flops=flops, bytes_accessed=bytes_moved, transcendentals=0),
        name=name,
    )(*ins)


def shaped(shape, dtype):
    return jax.ShapeDtypeStruct(shape, dtype)


def rows_iota(rows=TILE):
    return lax.broadcasted_iota(jnp.int32, (rows, LANES), 0)


def lanes_iota(rows=TILE):
    return lax.broadcasted_iota(jnp.int32, (rows, LANES), 1)


def fields(planted, likelihood, slope, colours, colour):
    free = planted >= colours
    member = jnp.where(planted == colour, 1.0, 0.0)
    return jnp.where(free, slope, SEED), jnp.where(free, likelihood, member)


def pack_z(colours, flip, info, image, planted, likelihoods, slope, out):
    labels, rows_x, rows_z, _ = likelihoods.shape
    even = info[EVEN_Z] != flip
    place = (rows_iota() + jnp.where(even, 0, 4)) & 7
    last, first = slice(rows_z - TILE, rows_z), slice(0, TILE)

    def at_end(ref, *lead):
        return jnp.where(even, ref[(*lead, last)].astype(ref.dtype), ref[(*lead, first)])

    def channel(c, x):
        return jnp.where(even, image[c, x, last].astype(F32), image[c, x, first].astype(F32))

    def turned(tile, for_even, for_odd):
        return jnp.where(even, pltpu.roll(tile, for_even, 0), pltpu.roll(tile, for_odd, 0))

    for x in range(rows_x):
        seeds = at_end(planted, x)
        for l in range(labels):
            rhs, full = fields(seeds, at_end(likelihoods, l, x), at_end(slope, l, x), colours, info[COLOUR] + l)
            first_channel = turned(channel(2 * l, x), 3, 6)
            second_channel = turned(channel(2 * l + 1, x), 4, 7)
            rest = jnp.where(place == 2, first_channel, second_channel)
            rest = jnp.where(place < 2, turned(full, 2, 4), rest)
            out[x, l] = jnp.where(place >= 4, rhs, rest).astype(BF16)


def sides(even, first, second):
    if second is None:
        return jnp.where(even, first, 0.0), jnp.where(even, 0.0, first)
    return jnp.where(even, first, second), jnp.where(even, second, first)


def assemble_z(colours, two, info, *refs):
    first_z = refs[0]
    second_z = refs[1] if two else None
    image, planted, likelihoods, slope, rhs_out, full_out, image_out, send_a, send_b = refs[1 + two :]
    labels, rows_x, rows_z, _ = likelihoods.shape
    channels = image.shape[0]
    upper = rows_iota() < 4
    for x in range(rows_x):
        for l in range(labels):
            rhs, full = fields(planted[x], likelihoods[l, x], slope[l, x], colours, info[COLOUR] + l)
            above, below = sides(
                info[EVEN_Z] == 1,
                first_z[x, l].astype(F32),
                second_z[x, l].astype(F32) if two else None,
            )
            rhs = jnp.concatenate([rhs, jnp.where(upper, above, below)], axis=0)
            full_tile = jnp.where(upper, pltpu.roll(above, 4, 0), pltpu.roll(below, 6, 0))
            rhs_out[l, x] = rhs
            full_out[l, x] = jnp.concatenate([full, full_tile], axis=0)
            plane = channels + l * rows_x + x
            send_a[plane] = rhs.astype(BF16)
            send_b[plane] = rhs.astype(BF16)
            for c, up, down in ((2 * l, 2, 5), (2 * l + 1, 1, 4)):
                tile = jnp.where(upper, pltpu.roll(above, up, 0), pltpu.roll(below, down, 0))
                image_out[c, x] = jnp.concatenate([image[c, x].astype(F32), tile], axis=0).astype(BF16)
    even = info[EVEN_X] == 1
    high, low = jnp.where(even, rows_x - 1, 0), jnp.where(even, 0, rows_x - 1)
    for c in range(channels):
        send_a[c] = image_out[c, high]
        send_b[c] = image_out[c, low]
    high, low = jnp.where(even, rows_x - 2, 0), jnp.where(even, 0, rows_x - 2)
    for l in range(labels):
        for r in range(2):
            plane = channels + labels * rows_x + 2 * l + r
            send_a[plane] = full_out[l, high + r].astype(BF16)
            send_b[plane] = full_out[l, low + r].astype(BF16)


def band(half, j, o, transposed=False):
    z, lane = rows_iota(), lanes_iota()
    other = lane & 7
    at = (z + 1 - other - 8 * o) if transposed else (other + 8 * o - z + 1)
    mask = at == j
    if half is not None:
        mask = mask & ((lane >> 6) == half)
    return mask


def bands(o, transposed=False):
    if o == 0:
        return (0, 1, 2)
    return (0,) if (o < 0) != transposed else (2,)


def spread_filter(info, first, second, one, two, wide_out, back_out):
    wide = jnp.dot(first[...], one[...], preferred_element_type=F32)
    back = jnp.dot(second[...], two[...], preferred_element_type=F32)
    zero = jnp.zeros((TILE, LANES), F32)
    for o in (-1, 0, 1):
        masks = {(h, j): band(h, j, o) for h in range(2) for j in bands(o)}
        for kd in range(9):
            for pair in range(2):
                for block in range(3):
                    tiles = []
                    for x in (2 * pair, 2 * pair + 1):
                        tile = zero
                        for i in range(3):
                            if (x + i) // 2 == block:
                                for j in bands(o):
                                    row = kd * 9 + i * 3 + j
                                    value = jnp.broadcast_to(wide[row : row + 1], (TILE, LANES))
                                    tile = jnp.where(masks[(x + i) % 2, j], value, tile)
                        tiles.append(tile)
                    at = (kd * 4 + 2 * pair) * TILE
                    wide_out[o + 1, at : at + 16, block * LANES : (block + 1) * LANES] = jnp.concatenate(
                        tiles, axis=0
                    ).astype(BF16)
        masks = {j: band(None, j, o, True) for j in bands(o, True)}
        for c in range(8):
            for pair in range(2):
                for block in range(6):
                    tiles = []
                    for x in (2 * pair, 2 * pair + 1):
                        tile = zero
                        i = x + 2 - block
                        if 0 <= i < 3:
                            for j in bands(o, True):
                                row = c * 9 + i * 3 + j
                                value = jnp.broadcast_to(back[row : row + 1], (TILE, LANES))
                                tile = jnp.where(masks[j], value, tile)
                        tiles.append(tile)
                    at = (c * 4 + 2 * pair) * TILE
                    back_out[o + 1, at : at + 16, block * LANES : (block + 1) * LANES] = jnp.concatenate(
                        tiles, axis=0
                    ).astype(BF16)


def tile_rows(t):
    at = (4 if t < 0 else t) * TILE
    return slice(at, at + TILE)


def convolve(info, image, first, second, matrix, part, stack, sums):
    channels, rows_x = image.shape[0], image.shape[1]
    even = info[EVEN_X] == 1
    for xp in range(rows_x + 2):
        for c in range(0, channels, 2):
            planes = []
            for ch in (c, c + 1):
                if 0 < xp <= rows_x:
                    planes.append(image[ch, xp - 1].astype(F32))
                else:
                    above, below = sides(even, first[ch].astype(F32), second[ch].astype(F32))
                    planes.append(below if xp == 0 else above)
            at = (xp * channels + c) * TILE
            for t in range(-1, 5):
                both = jnp.concatenate([plane[tile_rows(t)] for plane in planes], axis=0)
                stack[at : at + 16, (t + 1) * LANES : (t + 2) * LANES] = both.astype(BF16)
    total = jnp.dot(matrix[0], stack[:, 0:512], preferred_element_type=F32)
    total = total + jnp.dot(matrix[1], stack[:, 128:640], preferred_element_type=F32)
    sums[...] = total + jnp.dot(matrix[2], stack[:, 256:768], preferred_element_type=F32)
    lane = lanes_iota()
    for d in range(3):
        for x in range(rows_x):
            for t in range(4):
                cols = slice(t * LANES, (t + 1) * LANES)

                def piece(k):
                    at = ((k * 3 + d) * rows_x + x) * TILE
                    return sums[at : at + TILE, cols]

                before = jnp.where(lane > 0, pltpu.roll(piece(0), 1, 1), 0.0)
                after = jnp.where(lane < LANES - 1, pltpu.roll(piece(2), LANES - 1, 1), 0.0)
                part[d, x, tile_rows(t)] = piece(1) + before + after


def add_parts(two, info, part, other, logits, send_a, *send_b):
    rows_x, rows_z = part.shape[1], part.shape[2]
    even = info[EVEN_Z] == 1
    for d in range(3):
        for x in range(rows_x):
            total = part[d, x] + other[d, x]
            logits[d, x] = total
            first, last = total[:TILE], total[rows_z - TILE :]
            send_a[d, x] = jnp.where(even, last, first).astype(BF16)
            if two:
                send_b[0][d, x] = jnp.where(even, first, last).astype(BF16)


def extend_logits(two, info, logits, first, *refs):
    second = refs[0] if two else None
    out = refs[-1]
    upper = rows_iota() < 4
    for d in range(3):
        for x in range(logits.shape[1]):
            above, below = sides(
                info[EVEN_Z] == 1, first[d, x].astype(F32), second[d, x].astype(F32) if two else None
            )
            tile = jnp.where(upper, above, below)
            out[d, x] = jnp.concatenate([logits[d, x], tile], axis=0).astype(BF16)


def up(plane, dim):
    return pltpu.roll(plane, plane.shape[dim] - 1, dim)


def down(plane, dim):
    return pltpu.roll(plane, 1, dim)


def krylov(
    size_x, size_z, info, logits, own, mine, other, rhs, first, second, v0, v1, v2, slope_out, dots, weight, free
):
    labels, rows_x, rows, _ = rhs.shape
    rows_z = rows - TILE
    channels = 2 * labels
    is_up, even = info[UP] == 1, info[EVEN_X] == 1
    z = rows_iota(rows)
    z = info[FIRST_Z] + jnp.where(z < rows_z + HALO, z, z - rows)
    inside_z = (z >= 0) & (z < size_z)
    in_z = jnp.where(inside_z, 1.0, 0.0)
    next_z = jnp.where(inside_z & (z < size_z - 1), 1.0, 0.0)
    in_zy = jnp.where(lanes_iota(rows) < LANES - 1, in_z, 0.0)
    for at in range(rows_x + 2 * HALO):
        x = at - HALO
        place = info[FIRST_X] + x
        inside = (place >= 0) & (place < size_x)
        in_x = jnp.where(inside, 1.0, 0.0)
        next_x = jnp.where(inside & (place < size_x - 1), 1.0, 0.0)
        for d in range(3):
            if 0 <= x < rows_x:
                plane = jnp.concatenate([logits[d, x], own[d, x, rows_z:].astype(F32)], axis=0)
            elif x < 0:
                plane = jnp.where(is_up, other[d, x + HALO].astype(F32), mine[d, x + HALO].astype(F32))
            else:
                plane = jnp.where(is_up, mine[d, x - rows_x].astype(F32), other[d, x - rows_x].astype(F32))
            squashed = 1.0 / (1.0 + jnp.exp(-plane))
            valid = (in_z * next_x, next_z * in_x, in_zy * in_x)[d]
            weight[d, at] = (0.05 + squashed) * valid
            if -1 <= x <= rows_x:
                slope_out[d, x + 1] = squashed * (1.0 - squashed) * valid
        for l in range(labels):
            if 0 <= x < rows_x:
                plane = rhs[l, x]
            else:
                index = channels + l * rows_x + (x + HALO if x < 0 else x - rows_x)
                above, below = sides(even, first[index].astype(F32), second[index].astype(F32))
                plane = below if x < 0 else above
            open_cell = plane < SEED / 2
            v0[l, at] = jnp.where(open_cell, plane, 0.0)
            if l == 0:
                free[at] = jnp.where(open_cell, 1.0, 0.0)

    def label(l, carry):
        def operate(v, start, stop):
            flow_before = weight[0, start - 1] * (v[l, start - 1] - v[l, start])
            for at in range(start, stop):
                here = v[l, at]
                flow = weight[0, at] * (here - v[l, at + 1])
                flow_z = weight[1, at] * (here - up(here, 0))
                flow_y = weight[2, at] * (here - up(here, 1))
                result = flow - flow_before + (flow_z - down(flow_z, 0)) + (flow_y - down(flow_y, 1))
                yield at, here, free[at] * result
                flow_before = flow

        for at, here, result in operate(v0, 1, rows_x + 2 * HALO - 1):
            v1[l, at] = result * (1.0 / SPREAD) - here
        for at, here, result in operate(v1, 2, rows_x + 2 * HALO - 2):
            v2[l, at] = result * (2.0 / SPREAD) - 2.0 * here - v0[l, at]
        sums = [jnp.zeros((TILE, LANES), F32)] * 6
        for at, here, result in operate(v2, HALO, HALO + rows_x):
            a, b = v0[l, at], v1[l, at]
            for n, product in enumerate((a * a, a * b, b * b, b * here, here * here, here * result)):
                for t in range(rows_z // TILE):
                    sums[n] = sums[n] + product[tile_rows(t)]
        for n in range(6):
            dots[pl.ds(n * labels + l, 1), :] = jnp.sum(sums[n], axis=0, keepdims=True)
        return carry

    lax.fori_loop(0, labels, label, 0)


def steps(g00, g01, g11, g12, g22, k22):
    g02 = 2.0 * g11 - g00
    k00 = SPREAD * (g00 + g01)
    k01 = SPREAD * (g01 + g11)
    k02 = SPREAD * (g02 + g12)
    k11 = SPREAD * (g11 + 0.5 * (g12 + g01))
    k12 = SPREAD * (g12 + 0.5 * (g22 + g02))
    alpha = g00 / k00
    c0 = alpha
    r0 = 1.0 - alpha * SPREAD
    r1 = -alpha * SPREAD
    rr = r0 * r0 * g00 + 2.0 * r0 * r1 * g01 + r1 * r1 * g11
    beta = rr / g00
    p0, p1 = r0 + beta, r1
    alpha = rr / (p0 * p0 * k00 + 2.0 * p0 * p1 * k01 + p1 * p1 * k11)
    c0, c1 = c0 + alpha * p0, alpha * p1
    r0 = r0 - alpha * SPREAD * (p0 + 0.5 * p1)
    r1 = r1 - alpha * SPREAD * (p0 + p1)
    r2 = -alpha * SPREAD * 0.5 * p1
    rr_next = r0 * r0 * g00 + r1 * r1 * g11 + r2 * r2 * g22
    rr_next = rr_next + 2.0 * (r0 * r1 * g01 + r0 * r2 * g02 + r1 * r2 * g12)
    beta = rr_next / rr
    p0, p1, p2 = r0 + beta * p0, r1 + beta * p1, r2
    curve = p0 * p0 * k00 + p1 * p1 * k11 + p2 * p2 * k22
    curve = curve + 2.0 * (p0 * p1 * k01 + p0 * p2 * k02 + p1 * p2 * k12)
    alpha = rr_next / curve
    return c0 + alpha * p0, c1 + alpha * p1, alpha * p2


def edges(info, parts, v0, v1, v2, full, first, second, out, lam, field):
    labels, rows_x, rows, _ = full.shape
    even = info[EVEN_X] == 1
    total = jnp.sum(parts[...], axis=0)
    total = jnp.broadcast_to(jnp.sum(total, axis=1, keepdims=True), total.shape)
    grams = []
    for t in range(3):
        tile = total[tile_rows(t)]
        grams += [tile, pltpu.roll(tile, 4, 0)]
    c0, c1, c2 = steps(*grams)
    for l in range(labels):
        s0, s1, s2 = (jnp.broadcast_to(c[l : l + 1], (rows, LANES)) for c in (c0, c1, c2))
        for at in range(rows_x + 3):
            source = at + HALO - 1
            lam[l, at] = s0 * v0[l, source] + s1 * v1[l, source] + s2 * v2[l, source]
            x = at - 1
            if 0 <= x < rows_x:
                plane = full[l, x]
            else:
                index = 2 * labels + labels * rows_x + 2 * l + (1 if x < 0 else x - rows_x)
                above, below = sides(even, first[index].astype(F32), second[index].astype(F32))
                plane = below if x < 0 else above
            field[l, at] = plane
    for at in range(rows_x + 2):
        sums = [jnp.zeros((rows, LANES), F32)] * 3
        for l in range(labels):
            a, b = lam[l, at], field[l, at]
            sums[0] = sums[0] - (a - lam[l, at + 1]) * (b - field[l, at + 1])
            sums[1] = sums[1] - (a - up(a, 0)) * (b - up(b, 0))
            sums[2] = sums[2] - (a - up(a, 1)) * (b - up(b, 1))
        for d in range(3):
            out[d, at] = sums[d]


def filter_sums(info, edge, other, slope, stack, one, grads, out, products, rows_out):
    rows_x = edge.shape[1] - 2
    lane = lanes_iota(edge.shape[2])
    for xp in range(rows_x + 2):
        shifted = [[], [], []]
        for d in range(3):
            plane = ((edge[d, xp] + other[d, xp]) * slope[d, xp]).astype(BF16).astype(F32)
            shifted[0].append(jnp.where(lane < LANES - 1, up(plane, 1), 0.0))
            shifted[1].append(plane)
            shifted[2].append(jnp.where(lane > 0, down(plane, 1), 0.0))
        planes = shifted[0] + shifted[1] + shifted[2]
        planes += [jnp.zeros_like(planes[0])] * 7
        for pair in range(8):
            at = (xp * 16 + 2 * pair) * TILE
            for t in range(-1, 5):
                both = jnp.concatenate([plane[tile_rows(t)] for plane in planes[2 * pair : 2 * pair + 2]], axis=0)
                grads[at : at + 16, (t + 1) * LANES : (t + 2) * LANES] = both.astype(BF16)
    own = grads[LANES : LANES * (rows_x + 1), LANES : 5 * LANES]
    for o in range(3):
        products[o] = lax.dot_general(
            own, stack[:, o * LANES : (o + 4) * LANES], (((1,), (1,)), ((), ())), preferred_element_type=F32
        )
    rows_out[...] = jnp.zeros_like(rows_out)
    masks = {(h, j, o): band(h, j, o) for o in (-1, 0, 1) for h in range(2) for j in bands(o)}
    for kd in range(9):
        k, d = kd // 3, kd % 3
        for i in range(3):
            for j in range(3):
                total = jnp.zeros((TILE, LANES), F32)
                for o in (-1, 0, 1):
                    if j in bands(o):
                        for x in range(rows_x):
                            at = (x * 16 + kd) * TILE
                            col = (x + i) // 2 * LANES
                            piece = products[o + 1, at : at + TILE, col : col + LANES]
                            total = total + jnp.where(masks[(x + i) % 2, j, o], piece, 0.0)
                row = i * 9 + j * 3 + k
                rows_out[d, row : row + 1] = jnp.sum(total, axis=0, keepdims=True)
    for d in range(3):
        out[d * TILE : (d + 1) * TILE] = lax.dot_general(
            one[...],
            rows_out[d],
            (((1,), (1,)), ((), ())),
            precision=lax.Precision.HIGHEST,
            preferred_element_type=F32,
        )


def image_sums(info, grads, matrix, out, sums):
    total = jnp.dot(matrix[0], grads[:, 0:512], preferred_element_type=F32)
    total = total + jnp.dot(matrix[1], grads[:, 128:640], preferred_element_type=F32)
    sums[...] = total + jnp.dot(matrix[2], grads[:, 256:768], preferred_element_type=F32)
    channels, rows_x, rows_z, _ = out.shape
    for c in range(channels):
        for x in range(rows_x):
            at = (c * rows_x + x) * TILE
            for t in range(0, rows_z // TILE, 2):
                both = [sums[at : at + TILE, s * LANES : (s + 1) * LANES] for s in (t, t + 1)]
                out[c, x, t * TILE : (t + 2) * TILE] = jnp.concatenate(both, axis=0).astype(BF16)


def local(image, filt, planted, likelihoods, slope):
    channels = image.shape[0]
    labels, rows_x, rows_z, rows_y = likelihoods.shape
    if (channels, labels, rows_x, rows_z, rows_y) != (8, 4, HALO, 4 * TILE, LANES):
        raise ValueError("brick size")
    lab, xy, gz = lax.axis_index("lab"), lax.axis_index("xy"), lax.axis_index("gz")
    colours = labels * lax.axis_size("lab")
    size_x, size_z = rows_x * lax.axis_size("xy"), rows_z * lax.axis_size("gz")
    rows = rows_z + TILE
    two = lax.axis_size("gz") > 2
    info = jnp.stack(
        [1 - xy % 2, 1 - gz % 2, xy * rows_x, gz * rows_z, lab * labels, 1 - (xy + lab) % 2]
    ).astype(jnp.int32)

    inputs = (image, planted, likelihoods, slope)
    faces = []
    for phase in range(1 + two):
        block = call(
            functools.partial(pack_z, colours, phase),
            shaped((rows_x, labels, TILE, LANES), BF16),
            info,
            *inputs,
            name="pack_z",
        )
        faces.append(swap(block, "gz", phase))
    planes = channels + labels * rows_x + 2 * labels
    rhs, full, wide_image, send_a, send_b = call(
        functools.partial(assemble_z, colours, two),
        [
            shaped((labels, rows_x, rows, LANES), F32),
            shaped((labels, rows_x, rows, LANES), F32),
            shaped((channels, rows_x, rows, LANES), BF16),
            shaped((planes, rows, LANES), BF16),
            shaped((planes, rows, LANES), BF16),
        ],
        info,
        *faces,
        *inputs,
        name="assemble_z",
    )
    first = swap(send_a, "xy", 0)
    second = swap(send_b, "xy", 1)

    own_filt = lax.dynamic_slice_in_dim(filt, lab * channels, channels, 1)
    lines = jnp.transpose(own_filt, (4, 0, 2, 3, 1)).reshape(81, channels)
    lines = jnp.pad(lines, ((0, 7), (0, LANES - channels)))
    backs = jnp.transpose(own_filt, (1, 2, 3, 4, 0)).reshape(72, 9)
    backs = jnp.pad(backs, ((0, 0), (0, LANES - 9)))
    lane = jnp.arange(LANES, dtype=jnp.int32)
    by_channel = ((lane[None] >> 3) & 7) == lane[:, None]
    by_edge = (lane[None] >> 3) == lane[:, None]
    matrix, back_matrix = call(
        spread_filter,
        [shaped((3, 288, 384), BF16), shaped((3, 256, 768), BF16)],
        info,
        lines,
        backs,
        by_channel.astype(BF16),
        by_edge.astype(BF16),
        flops=10_000_000,
        name="spread_filter",
    )
    part, stack = call(
        convolve,
        [shaped((3, rows_x, rows_z, LANES), F32), shaped((384, 768), BF16)],
        info,
        wide_image,
        first,
        second,
        matrix,
        scratch=[pltpu.VMEM((288, 512), F32)],
        name="convolve",
    )
    faces_shape = shaped((3, rows_x, TILE, LANES), BF16)
    logits, *sends = call(
        functools.partial(add_parts, two),
        [shaped(part.shape, F32)] + [faces_shape] * (1 + two),
        info,
        part,
        lab_swap(part),
        name="add_parts",
    )
    faces = [swap(block, "gz", phase) for phase, block in enumerate(sends)]
    own = call(
        functools.partial(extend_logits, two),
        shaped((3, rows_x, rows, LANES), BF16),
        info,
        logits,
        *faces,
        name="extend_logits",
    )
    mine = split_swap(own, "xy")
    other = lab_swap(mine)
    extended = (labels, rows_x + 2 * HALO, rows, LANES)
    ring = shaped((3, rows_x + 2, rows, LANES), F32)
    v0, v1, v2, squash_slope, dots = call(
        functools.partial(krylov, size_x, size_z),
        [shaped(extended, F32)] * 3 + [ring, shaped((6 * labels, LANES), F32)],
        info,
        logits,
        own,
        mine,
        other,
        rhs,
        first,
        second,
        scratch=[
            pltpu.VMEM((3,) + extended[1:], F32),
            pltpu.VMEM(extended[1:], F32),
        ],
        name="krylov",
    )
    edge = call(
        edges,
        ring,
        info,
        everyones(dots, ("xy", "gz")),
        v0,
        v1,
        v2,
        full,
        first,
        second,
        scratch=[pltpu.VMEM((labels, rows_x + 3, rows, LANES), F32)] * 2,
        name="edges",
    )
    grads, sums = call(
        filter_sums,
        [shaped((768, 768), BF16), shaped((3 * TILE, LANES), F32)],
        info,
        edge,
        lab_swap(edge),
        squash_slope,
        stack,
        by_channel[:TILE].astype(F32),
        scratch=[pltpu.VMEM((3, 512, 384), F32), pltpu.VMEM((3, LANES, LANES), F32)],
        name="filter_sums",
    )
    grad_image = call(
        image_sums,
        shaped(image.shape, BF16),
        info,
        grads,
        back_matrix,
        scratch=[pltpu.VMEM((256, 512), F32)],
        flops=10_000_000,
        name="image_sums",
    )
    grad_filter = jnp.sum(everyones(sums, ("xy", "gz")), axis=0)
    return grad_image, grad_filter[:, :27].reshape(3, channels, 3, 3, 3)


def solution(mesh):
    return jax.shard_map(
        local,
        mesh=mesh,
        in_specs=(
            P("lab", ("crops", "xy"), "gz", None),
            P(),
            P(("crops", "xy"), "gz", None),
            P("lab", ("crops", "xy"), "gz", None),
            P("lab", ("crops", "xy"), "gz", None),
        ),
        out_specs=(P("lab", ("crops", "xy"), "gz", None), P("crops", "lab", None, None, None)),
        check_vma=False,
    )
```

```python
import functools

import jax
import jax.numpy as jnp
from jax import lax
from jax.experimental import pallas as pl
from jax.experimental.pallas import tpu as pltpu
from jax.sharding import PartitionSpec as P

HALO = 4
SEED = 64.0
SPREAD = 6.3
TILE = 8
LANES = 128
BF16, F32 = jnp.bfloat16, jnp.float32
EVEN_X, EVEN_Z, FIRST_X, FIRST_Z, COLOUR, UP = range(6)


def pair_routes(count, phase):
    route = []
    for low in range(phase, count - 1, 2):
        route += [(low, low + 1), (low + 1, low)]
    return route


def swap(block, axis, phase):
    return lax.ppermute(block, axis, pair_routes(lax.axis_size(axis), phase))


def lab_swap(block):
    return lax.ppermute(block, "lab", [(0, 1), (1, 0)])


def diagonal_swap(block, x_phase, z_phase):
    along_x = pair_routes(lax.axis_size("xy"), x_phase)
    along_z = pair_routes(lax.axis_size("gz"), z_phase)
    count = lax.axis_size("gz")
    route = [(sx * count + sz, dx * count + dz) for sx, dx in along_x for sz, dz in along_z]
    return lax.ppermute(block, ("xy", "gz"), route)


def split_swap(block):
    labs = lax.axis_size("lab")
    route = [
        (src * labs + lab, dst * labs + lab)
        for lab in range(labs)
        for src, dst in pair_routes(lax.axis_size("xy"), lab % 2)
    ]
    return lax.ppermute(block, ("xy", "lab"), route)


def split_diagonal_swap(block, z_phase):
    labs, count = lax.axis_size("lab"), lax.axis_size("gz")
    route = [
        ((sx * count + sz) * labs + lab, (dx * count + dz) * labs + lab)
        for lab in range(labs)
        for sx, dx in pair_routes(lax.axis_size("xy"), lab % 2)
        for sz, dz in pair_routes(count, z_phase)
    ]
    return lax.ppermute(block, ("xy", "gz", "lab"), route)


def everyones(copies, axes):
    return lax.all_to_all(copies, axes, 0, 0)


def call(kernel, outs, *ins, scratch=(), flops=1_000_000, name=None, space=pltpu.VMEM):
    specs = [pl.BlockSpec(memory_space=pltpu.SMEM)]
    specs += [pl.BlockSpec(memory_space=space)] * (len(ins) - 1)
    bytes_moved = sum(a.size * a.dtype.itemsize for a in ins)
    return pl.pallas_call(
        kernel,
        out_shape=outs,
        in_specs=specs,
        out_specs=jax.tree.map(lambda _: pl.BlockSpec(memory_space=pltpu.VMEM), outs),
        scratch_shapes=list(scratch),
        compiler_params=pltpu.CompilerParams(vmem_limit_bytes=40 * 2**20),
        cost_estimate=pl.CostEstimate(flops=flops, bytes_accessed=bytes_moved, transcendentals=0),
        name=name,
    )(*ins)


def shaped(shape, dtype):
    return jax.ShapeDtypeStruct(shape, dtype)


def rows_iota(rows=TILE):
    return lax.broadcasted_iota(jnp.int32, (rows, LANES), 0)


def lanes_iota(rows=TILE):
    return lax.broadcasted_iota(jnp.int32, (rows, LANES), 1)


def fields(planted, likelihood, slope, colours, colour):
    free = planted >= colours
    member = jnp.where(planted == colour, 1.0, 0.0)
    return jnp.where(free, slope, SEED), jnp.where(free, likelihood, member)


def pack(colours, two, info, image_in, planted_in, likelihoods_in, slope_in, image, planted, likelihoods, slope, *refs):
    faces, (send_a, send_b, sems) = refs[: 1 + two], refs[1 + two :]
    pairs = ((planted_in, planted), (slope_in, slope), (likelihoods_in, likelihoods), (image_in, image))
    copies = [pltpu.make_async_copy(src, dst, sems.at[n]) for n, (src, dst) in enumerate(pairs)]
    for copy in copies:
        copy.start()
    for copy in copies:
        copy.wait()
    labels, rows_x, rows_z, _ = likelihoods.shape
    channels = image.shape[0]
    last, first = slice(rows_z - TILE, rows_z), slice(0, TILE)
    for phase, out in enumerate(faces):
        even = info[EVEN_Z] != phase
        place = (rows_iota() + jnp.where(even, 0, 4)) & 7

        def at_end(plane):
            return jnp.where(even, plane[last], plane[first])

        def channel(c, x):
            return jnp.where(even, image[c, x, last].astype(F32), image[c, x, first].astype(F32))

        def turned(tile, for_even, for_odd):
            return jnp.where(even, pltpu.roll(tile, for_even, 0), pltpu.roll(tile, for_odd, 0))

        for x in range(rows_x):
            seeds = jnp.where(even, planted[x, last], planted[x, first])
            for l in range(labels):
                ends = [jnp.where(even, ref[l, x, last], ref[l, x, first]) for ref in (likelihoods, slope)]
                rhs, full = fields(seeds, *ends, colours, info[COLOUR] + l)
                first_channel = turned(channel(2 * l, x), 3, 6)
                second_channel = turned(channel(2 * l + 1, x), 4, 7)
                rest = jnp.where(place == 2, first_channel, second_channel)
                rest = jnp.where(place < 2, turned(full, 2, 4), rest)
                out[x, l] = jnp.where(place >= 4, rhs, rest).astype(BF16)
    even = info[EVEN_X] == 1
    high, low = jnp.where(even, rows_x - 1, 0), jnp.where(even, 0, rows_x - 1)
    for c in range(channels):
        send_a[c] = image[c, high]
        send_b[c] = image[c, low]
    for x in range(rows_x):
        for l in range(labels):
            rhs = jnp.where(planted[x] >= colours, slope[l, x], SEED).astype(BF16)
            send_a[channels + l * rows_x + x] = rhs
            send_b[channels + l * rows_x + x] = rhs
    for l in range(labels):
        for send, at in ((send_a, high), (send_b, low)):
            for r in range(2):
                x = jnp.where(at == 0, 0, rows_x - 2) + r
                _, full = fields(planted[x], likelihoods[l, x], slope[l, x], colours, info[COLOUR] + l)
                send[channels + labels * rows_x + 2 * l + r] = full.astype(BF16)


def sides(even, first, second):
    if second is None:
        return jnp.where(even, first, 0.0), jnp.where(even, 0.0, first)
    return jnp.where(even, first, second), jnp.where(even, second, first)


def ends_z(info, tiles, x, l):
    both = [ref[x, l].astype(F32) for ref in tiles]
    return sides(info[EVEN_Z] == 1, both[0], both[1] if len(both) > 1 else None)


def rhs_tile(above, below):
    return jnp.where(rows_iota() < 4, above, below)


def full_tile(above, below):
    return jnp.where(rows_iota() < 4, pltpu.roll(above, 4, 0), pltpu.roll(below, 6, 0))


def image_tile(above, below, c):
    up, down = (2, 5) if c % 2 == 0 else (1, 4)
    return jnp.where(rows_iota() < 4, pltpu.roll(above, up, 0), pltpu.roll(below, down, 0))


def band(half, j, o, transposed=False):
    z, lane = rows_iota(), lanes_iota()
    other = lane & 7
    at = (z + 1 - other - 8 * o) if transposed else (other + 8 * o - z + 1)
    mask = at == j
    if half is not None:
        mask = mask & ((lane >> 6) == half)
    return mask


def bands(o, transposed=False):
    if o == 0:
        return (0, 1, 2)
    return (0,) if (o < 0) != transposed else (2,)


def spread_filter(info, first, second, one, two, wide_out, back_out):
    wide = jnp.dot(first[...], one[...], preferred_element_type=F32)
    back = jnp.dot(second[...], two[...], preferred_element_type=F32)
    zero = jnp.zeros((TILE, LANES), F32)
    for o in (-1, 0, 1):
        masks = {(h, j): band(h, j, o) for h in range(2) for j in bands(o)}
        for kd in range(9):
            for pair in range(2):
                for block in range(3):
                    tiles = []
                    for x in (2 * pair, 2 * pair + 1):
                        tile = zero
                        for i in range(3):
                            if (x + i) // 2 == block:
                                for j in bands(o):
                                    row = kd * 9 + i * 3 + j
                                    value = jnp.broadcast_to(wide[row : row + 1], (TILE, LANES))
                                    tile = jnp.where(masks[(x + i) % 2, j], value, tile)
                        tiles.append(tile)
                    at = (kd * 4 + 2 * pair) * TILE
                    wide_out[o + 1, at : at + 16, block * LANES : (block + 1) * LANES] = jnp.concatenate(
                        tiles, axis=0
                    ).astype(BF16)
        masks = {j: band(None, j, o, True) for j in bands(o, True)}
        for c in range(8):
            for pair in range(2):
                for block in range(6):
                    tiles = []
                    for x in (2 * pair, 2 * pair + 1):
                        tile = zero
                        i = x + 2 - block
                        if 0 <= i < 3:
                            for j in bands(o, True):
                                row = c * 9 + i * 3 + j
                                value = jnp.broadcast_to(back[row : row + 1], (TILE, LANES))
                                tile = jnp.where(masks[j], value, tile)
                        tiles.append(tile)
                    at = (c * 4 + 2 * pair) * TILE
                    back_out[o + 1, at : at + 16, block * LANES : (block + 1) * LANES] = jnp.concatenate(
                        tiles, axis=0
                    ).astype(BF16)


def tile_rows(t):
    at = (4 if t < 0 else t) * TILE
    return slice(at, at + TILE)


def convolve(two, info, image, first, second, *refs):
    faces, edges_a, edges_b = refs[: 1 + two], refs[1 + two : 2 + 2 * two], refs[2 + 2 * two : 3 + 3 * two]
    matrix, part, stack, sums = refs[3 + 3 * two :]
    channels, rows_x = image.shape[0], image.shape[1]
    even = info[EVEN_X] == 1
    for xp in range(rows_x + 2):
        for c in range(0, channels, 2):
            planes = []
            if 0 < xp <= rows_x:
                ends = [ends_z(info, faces, xp - 1, c // 2)]
            else:
                ends = [ends_z(info, tiles, rows_x - 1 if xp == 0 else 0, c // 2) for tiles in (edges_a, edges_b)]
            for ch in (c, c + 1):
                tiles = [image_tile(*pair, ch) for pair in ends]
                if 0 < xp <= rows_x:
                    planes.append(jnp.concatenate([image[ch, xp - 1].astype(F32), tiles[0]], axis=0))
                else:
                    received = [
                        jnp.concatenate([ref[ch].astype(F32), tile], axis=0)
                        for ref, tile in zip((first, second), tiles)
                    ]
                    above, below = sides(even, *received)
                    planes.append(below if xp == 0 else above)
            at = (xp * channels + c) * TILE
            for t in range(-1, 5):
                both = jnp.concatenate([plane[tile_rows(t)] for plane in planes], axis=0)
                stack[at : at + 16, (t + 1) * LANES : (t + 2) * LANES] = both.astype(BF16)
    total = jnp.dot(matrix[0], stack[:, 0:512], preferred_element_type=F32)
    total = total + jnp.dot(matrix[1], stack[:, 128:640], preferred_element_type=F32)
    sums[...] = total + jnp.dot(matrix[2], stack[:, 256:768], preferred_element_type=F32)
    lane = lanes_iota()
    for d in range(3):
        for x in range(rows_x):
            for t in range(4):
                cols = slice(t * LANES, (t + 1) * LANES)

                def piece(k):
                    at = ((k * 3 + d) * rows_x + x) * TILE
                    return sums[at : at + TILE, cols]

                before = jnp.where(lane > 0, pltpu.roll(piece(0), 1, 1), 0.0)
                after = jnp.where(lane < LANES - 1, pltpu.roll(piece(2), LANES - 1, 1), 0.0)
                part[d, x, tile_rows(t)] = piece(1) + before + after


def add_parts(two, info, part, other, logits, brick, *faces):
    rows_x, rows_z = part.shape[1], part.shape[2]
    for d in range(3):
        for x in range(rows_x):
            total = part[d, x] + other[d, x]
            logits[d, x] = total
            brick[d, x] = total.astype(BF16)
            for phase, face in enumerate(faces):
                even = info[EVEN_Z] != phase
                face[d, x] = jnp.where(even, total[rows_z - TILE :], total[:TILE]).astype(BF16)


def up(plane, dim):
    return pltpu.roll(plane, plane.shape[dim] - 1, dim)


def down(plane, dim):
    return pltpu.roll(plane, 1, dim)


def krylov(colours, size_x, size_z, two, info, planted, slope, logits, mine, other, first, second, *refs):
    groups = [refs[n * (1 + two) : (n + 1) * (1 + two)] for n in range(6)]
    faces, mine_edges, other_edges, rhs_faces, edges_a, edges_b = groups
    v0, v1, v2, slope_out, dots_out, weight, free, dots = refs[6 * (1 + two) :]
    labels, rows_x, rows_z, _ = slope.shape
    rows = rows_z + TILE
    channels = 2 * labels
    is_up, even = info[UP] == 1, info[EVEN_X] == 1
    z = rows_iota(rows)
    z = info[FIRST_Z] + jnp.where(z < rows_z + HALO, z, z - rows)
    inside_z = (z >= 0) & (z < size_z)
    in_z = jnp.where(inside_z, 1.0, 0.0)
    next_z = jnp.where(inside_z & (z < size_z - 1), 1.0, 0.0)
    in_zy = jnp.where(lanes_iota(rows) < LANES - 1, in_z, 0.0)
    for at in range(rows_x + 2 * HALO):
        x = at - HALO
        place = info[FIRST_X] + x
        inside = (place >= 0) & (place < size_x)
        in_x = jnp.where(inside, 1.0, 0.0)
        next_x = jnp.where(inside & (place < size_x - 1), 1.0, 0.0)
        for d in range(3):
            def grown(plane, tiles, source):
                return jnp.concatenate([plane, rhs_tile(*ends_z(info, tiles, d, source))], axis=0)

            if 0 <= x < rows_x:
                plane = grown(logits[d, x], faces, x)
            else:
                source = x % rows_x
                here = grown(mine[d, source].astype(F32), mine_edges, source)
                there = grown(other[d, source].astype(F32), other_edges, source)
                plane = jnp.where(is_up, there, here) if x < 0 else jnp.where(is_up, here, there)
            squashed = 1.0 / (1.0 + jnp.exp(-plane))
            valid = (in_z * next_x, next_z * in_x, in_zy * in_x)[d]
            weight[d, at] = (0.05 + squashed) * valid
            if -1 <= x <= rows_x:
                slope_out[d, x + 1] = squashed * (1.0 - squashed) * valid
        for l in range(labels):
            source = x % rows_x
            if 0 <= x < rows_x:
                plane = jnp.where(planted[x] >= colours, slope[l, x], SEED)
                plane = jnp.concatenate([plane, rhs_tile(*ends_z(info, rhs_faces, x, l))], axis=0)
            else:
                index = channels + l * rows_x + source
                received = [
                    jnp.concatenate([ref[index].astype(F32), rhs_tile(*ends_z(info, tiles, source, l))], axis=0)
                    for ref, tiles in ((first, edges_a), (second, edges_b))
                ]
                above, below = sides(even, *received)
                plane = below if x < 0 else above
            open_cell = plane < SEED / 2
            v0[l, at] = jnp.where(open_cell, plane, 0.0)
            if l == 0:
                free[at] = jnp.where(open_cell, 1.0, 0.0)

    def label(l, carry):
        def operate(v, start, stop):
            flow_before = weight[0, start - 1] * (v[l, start - 1] - v[l, start])
            for at in range(start, stop):
                here = v[l, at]
                flow = weight[0, at] * (here - v[l, at + 1])
                flow_z = weight[1, at] * (here - up(here, 0))
                flow_y = weight[2, at] * (here - up(here, 1))
                result = flow - flow_before + (flow_z - down(flow_z, 0)) + (flow_y - down(flow_y, 1))
                yield at, here, free[at] * result
                flow_before = flow

        for at, here, result in operate(v0, 1, rows_x + 2 * HALO - 1):
            v1[l, at] = result * (1.0 / SPREAD) - here
        for at, here, result in operate(v1, 2, rows_x + 2 * HALO - 2):
            v2[l, at] = result * (2.0 / SPREAD) - 2.0 * here - v0[l, at]
        sums = [jnp.zeros((TILE, LANES), F32)] * 6
        for at, here, result in operate(v2, HALO, HALO + rows_x):
            a, b = v0[l, at], v1[l, at]
            for n, product in enumerate((a * a, a * b, b * b, b * here, here * here, here * result)):
                for t in range(rows_z // TILE):
                    sums[n] = sums[n] + product[tile_rows(t)]
        for n in range(6):
            dots[pl.ds(n * labels + l, 1), :] = jnp.sum(sums[n], axis=0, keepdims=True)
        return carry

    lax.fori_loop(0, labels, label, 0)
    for n in range(dots_out.shape[0]):
        dots_out[n] = dots[...]


def steps(g00, g01, g11, g12, g22, k22):
    g02 = 2.0 * g11 - g00
    k00 = SPREAD * (g00 + g01)
    k01 = SPREAD * (g01 + g11)
    k02 = SPREAD * (g02 + g12)
    k11 = SPREAD * (g11 + 0.5 * (g12 + g01))
    k12 = SPREAD * (g12 + 0.5 * (g22 + g02))
    alpha = g00 / k00
    c0 = alpha
    r0 = 1.0 - alpha * SPREAD
    r1 = -alpha * SPREAD
    rr = r0 * r0 * g00 + 2.0 * r0 * r1 * g01 + r1 * r1 * g11
    beta = rr / g00
    p0, p1 = r0 + beta, r1
    alpha = rr / (p0 * p0 * k00 + 2.0 * p0 * p1 * k01 + p1 * p1 * k11)
    c0, c1 = c0 + alpha * p0, alpha * p1
    r0 = r0 - alpha * SPREAD * (p0 + 0.5 * p1)
    r1 = r1 - alpha * SPREAD * (p0 + p1)
    r2 = -alpha * SPREAD * 0.5 * p1
    rr_next = r0 * r0 * g00 + r1 * r1 * g11 + r2 * r2 * g22
    rr_next = rr_next + 2.0 * (r0 * r1 * g01 + r0 * r2 * g02 + r1 * r2 * g12)
    beta = rr_next / rr
    p0, p1, p2 = r0 + beta * p0, r1 + beta * p1, r2
    curve = p0 * p0 * k00 + p1 * p1 * k11 + p2 * p2 * k22
    curve = curve + 2.0 * (p0 * p1 * k01 + p0 * p2 * k02 + p1 * p2 * k12)
    alpha = rr_next / curve
    return c0 + alpha * p0, c1 + alpha * p1, alpha * p2


def edges(colours, two, info, parts, v0, v1, v2, planted, likelihoods, first, second, *refs):
    faces, edges_a, edges_b = refs[: 1 + two], refs[1 + two : 2 + 2 * two], refs[2 + 2 * two : 3 + 3 * two]
    out, lam, field = refs[3 + 3 * two :]
    labels, rows_x, rows_z, _ = likelihoods.shape
    rows = rows_z + TILE
    even = info[EVEN_X] == 1
    total = jnp.sum(parts[...], axis=0)
    total = jnp.broadcast_to(jnp.sum(total, axis=1, keepdims=True), total.shape)
    grams = []
    for t in range(3):
        tile = total[tile_rows(t)]
        grams += [tile, pltpu.roll(tile, 4, 0)]
    c0, c1, c2 = steps(*grams)
    for l in range(labels):
        s0, s1, s2 = (jnp.broadcast_to(c[l : l + 1], (rows, LANES)) for c in (c0, c1, c2))
        for at in range(rows_x + 3):
            source = at + HALO - 1
            lam[l, at] = s0 * v0[l, source] + s1 * v1[l, source] + s2 * v2[l, source]
            x = at - 1
            source = x % rows_x
            if 0 <= x < rows_x:
                member = jnp.where(planted[x] == info[COLOUR] + l, 1.0, 0.0)
                plane = jnp.where(planted[x] >= colours, likelihoods[l, x], member)
                plane = jnp.concatenate([plane, full_tile(*ends_z(info, faces, x, l))], axis=0)
            else:
                index = 2 * labels + labels * rows_x + 2 * l + (1 if x < 0 else source)
                received = [
                    jnp.concatenate([ref[index].astype(F32), full_tile(*ends_z(info, tiles, source, l))], axis=0)
                    for ref, tiles in ((first, edges_a), (second, edges_b))
                ]
                above, below = sides(even, *received)
                plane = below if x < 0 else above
            field[l, at] = plane
    for at in range(rows_x + 2):
        sums = [jnp.zeros((rows, LANES), F32)] * 3
        for l in range(labels):
            a, b = lam[l, at], field[l, at]
            sums[0] = sums[0] - (a - lam[l, at + 1]) * (b - field[l, at + 1])
            sums[1] = sums[1] - (a - up(a, 0)) * (b - up(b, 0))
            sums[2] = sums[2] - (a - up(a, 1)) * (b - up(b, 1))
        for d in range(3):
            out[d, at] = sums[d]


def filter_sums(info, edge, other, slope, stack, one, grads, out, products, rows_out):
    rows_x = edge.shape[1] - 2
    lane = lanes_iota(edge.shape[2])
    for xp in range(rows_x + 2):
        shifted = [[], [], []]
        for d in range(3):
            plane = ((edge[d, xp] + other[d, xp]) * slope[d, xp]).astype(BF16).astype(F32)
            shifted[0].append(jnp.where(lane < LANES - 1, up(plane, 1), 0.0))
            shifted[1].append(plane)
            shifted[2].append(jnp.where(lane > 0, down(plane, 1), 0.0))
        planes = shifted[0] + shifted[1] + shifted[2]
        planes += [jnp.zeros_like(planes[0])] * 7
        for pair in range(8):
            at = (xp * 16 + 2 * pair) * TILE
            for t in range(-1, 5):
                both = jnp.concatenate([plane[tile_rows(t)] for plane in planes[2 * pair : 2 * pair + 2]], axis=0)
                grads[at : at + 16, (t + 1) * LANES : (t + 2) * LANES] = both.astype(BF16)
    own = grads[LANES : LANES * (rows_x + 1), LANES : 5 * LANES]
    for o in range(3):
        products[o] = lax.dot_general(
            own, stack[:, o * LANES : (o + 4) * LANES], (((1,), (1,)), ((), ())), preferred_element_type=F32
        )
    rows_out[...] = jnp.zeros_like(rows_out)
    masks = {(h, j, o): band(h, j, o) for o in (-1, 0, 1) for h in range(2) for j in bands(o)}
    for kd in range(9):
        k, d = kd // 3, kd % 3
        for i in range(3):
            for j in range(3):
                total = jnp.zeros((TILE, LANES), F32)
                for o in (-1, 0, 1):
                    if j in bands(o):
                        for x in range(rows_x):
                            at = (x * 16 + kd) * TILE
                            col = (x + i) // 2 * LANES
                            piece = products[o + 1, at : at + TILE, col : col + LANES]
                            total = total + jnp.where(masks[(x + i) % 2, j, o], piece, 0.0)
                row = i * 9 + j * 3 + k
                rows_out[d, row : row + 1] = jnp.sum(total, axis=0, keepdims=True)
    for d in range(3):
        sums = lax.dot_general(
            one[...],
            rows_out[d],
            (((1,), (1,)), ((), ())),
            precision=lax.Precision.HIGHEST,
            preferred_element_type=F32,
        )
        for n in range(out.shape[0]):
            out[n, d * TILE : (d + 1) * TILE] = sums


def image_sums(info, grads, matrix, out, sums):
    total = jnp.dot(matrix[0], grads[:, 0:512], preferred_element_type=F32)
    total = total + jnp.dot(matrix[1], grads[:, 128:640], preferred_element_type=F32)
    sums[...] = total + jnp.dot(matrix[2], grads[:, 256:768], preferred_element_type=F32)
    channels, rows_x, rows_z, _ = out.shape
    for c in range(channels):
        for x in range(rows_x):
            at = (c * rows_x + x) * TILE
            for t in range(0, rows_z // TILE, 2):
                both = [sums[at : at + TILE, s * LANES : (s + 1) * LANES] for s in (t, t + 1)]
                out[c, x, t * TILE : (t + 2) * TILE] = jnp.concatenate(both, axis=0).astype(BF16)


def local(image, filt, planted, likelihoods, slope):
    channels = image.shape[0]
    labels, rows_x, rows_z, rows_y = likelihoods.shape
    if (channels, labels, rows_x, rows_z, rows_y) != (8, 4, HALO, 4 * TILE, LANES):
        raise ValueError("brick size")
    lab, xy, gz = lax.axis_index("lab"), lax.axis_index("xy"), lax.axis_index("gz")
    colours = labels * lax.axis_size("lab")
    size_x, size_z = rows_x * lax.axis_size("xy"), rows_z * lax.axis_size("gz")
    rows = rows_z + TILE
    two = lax.axis_size("gz") > 2
    phases = range(1 + two)
    members = lax.axis_size("xy") * lax.axis_size("gz")
    info = jnp.stack(
        [1 - xy % 2, 1 - gz % 2, xy * rows_x, gz * rows_z, lab * labels, 1 - (xy + lab) % 2]
    ).astype(jnp.int32)

    planes = channels + labels * rows_x + 2 * labels
    brick = shaped((planes, rows_z, LANES), BF16)
    inputs = (image, planted, likelihoods, slope)
    image, planted, likelihoods, slope, *packed = call(
        functools.partial(pack, colours, two),
        [shaped(a.shape, a.dtype) for a in inputs]
        + [shaped((rows_x, labels, TILE, LANES), BF16)] * (1 + two)
        + [brick, brick],
        info,
        *inputs,
        scratch=[pltpu.SemaphoreType.DMA((4,))],
        name="pack",
        space=pl.ANY,
    )
    send_a, send_b = packed[1 + two :]
    second = swap(send_b, "xy", 1)
    first = swap(send_a, "xy", 0)
    edges_b = [diagonal_swap(packed[phase], 1, phase) for phase in phases]
    edges_a = [diagonal_swap(packed[phase], 0, phase) for phase in phases]
    faces = [swap(packed[phase], "gz", phase) for phase in phases]
    received = (first, second, *faces, *edges_a, *edges_b)

    own_filt = lax.dynamic_slice_in_dim(filt, lab * channels, channels, 1)
    lines = jnp.transpose(own_filt, (4, 0, 2, 3, 1)).reshape(81, channels)
    lines = jnp.pad(lines, ((0, 7), (0, LANES - channels)))
    backs = jnp.transpose(own_filt, (1, 2, 3, 4, 0)).reshape(72, 9)
    backs = jnp.pad(backs, ((0, 0), (0, LANES - 9)))
    lane = jnp.arange(LANES, dtype=jnp.int32)
    by_channel = ((lane[None] >> 3) & 7) == lane[:, None]
    by_edge = (lane[None] >> 3) == lane[:, None]
    matrix, back_matrix = call(
        spread_filter,
        [shaped((3, 288, 384), BF16), shaped((3, 256, 768), BF16)],
        info,
        lines,
        backs,
        by_channel.astype(BF16),
        by_edge.astype(BF16),
        flops=10_000_000,
        name="spread_filter",
    )
    part, stack = call(
        functools.partial(convolve, two),
        [shaped((3, rows_x, rows_z, LANES), F32), shaped((384, 768), BF16)],
        info,
        image,
        *received,
        matrix,
        scratch=[pltpu.VMEM((288, 512), F32)],
        name="convolve",
    )
    logits, own, *sends = call(
        functools.partial(add_parts, two),
        [shaped(part.shape, F32), shaped(part.shape, BF16)]
        + [shaped((3, rows_x, TILE, LANES), BF16)] * (1 + two),
        info,
        part,
        lab_swap(part),
        name="add_parts",
    )
    mine = split_swap(own)
    mine_edges = [split_diagonal_swap(sends[phase], phase) for phase in phases]
    logit_faces = [swap(sends[phase], "gz", phase) for phase in phases]
    other = lab_swap(mine)
    other_edges = [lab_swap(block) for block in mine_edges]
    extended = (labels, rows_x + 2 * HALO, rows, LANES)
    ring = shaped((3, rows_x + 2, rows, LANES), F32)
    v0, v1, v2, squash_slope, dots = call(
        functools.partial(krylov, colours, size_x, size_z, two),
        [shaped(extended, F32)] * 3 + [ring, shaped((members, 6 * labels, LANES), F32)],
        info,
        planted,
        slope,
        logits,
        mine,
        other,
        first,
        second,
        *logit_faces,
        *mine_edges,
        *other_edges,
        *faces,
        *edges_a,
        *edges_b,
        scratch=[
            pltpu.VMEM((3,) + extended[1:], F32),
            pltpu.VMEM(extended[1:], F32),
            pltpu.VMEM((6 * labels, LANES), F32),
        ],
        name="krylov",
    )
    edge = call(
        functools.partial(edges, colours, two),
        ring,
        info,
        everyones(dots, ("xy", "gz")),
        v0,
        v1,
        v2,
        planted,
        likelihoods,
        *received,
        scratch=[pltpu.VMEM((labels, rows_x + 3, rows, LANES), F32)] * 2,
        name="edges",
    )
    grads, sums = call(
        filter_sums,
        [shaped((768, 768), BF16), shaped((members, 3 * TILE, LANES), F32)],
        info,
        edge,
        lab_swap(edge),
        squash_slope,
        stack,
        by_channel[:TILE].astype(F32),
        scratch=[pltpu.VMEM((3, 512, 384), F32), pltpu.VMEM((3, LANES, LANES), F32)],
        name="filter_sums",
    )
    grad_image = call(
        image_sums,
        shaped(image.shape, BF16),
        info,
        grads,
        back_matrix,
        scratch=[pltpu.VMEM((256, 512), F32)],
        flops=10_000_000,
        name="image_sums",
    )
    grad_filter = jnp.sum(everyones(sums, ("xy", "gz")), axis=0)
    return grad_image, grad_filter[:, :27].reshape(3, channels, 3, 3, 3)


def solution(mesh):
    return jax.shard_map(
        local,
        mesh=mesh,
        in_specs=(
            P("lab", ("crops", "xy"), "gz", None),
            P(),
            P(("crops", "xy"), "gz", None),
            P("lab", ("crops", "xy"), "gz", None),
            P("lab", ("crops", "xy"), "gz", None),
        ),
        out_specs=(P("lab", ("crops", "xy"), "gz", None), P("crops", "lab", None, None, None)),
        check_vma=False,
    )
```

```python
import functools

import jax
import jax.numpy as jnp
from jax import lax
from jax.experimental import pallas as pl
from jax.experimental.pallas import tpu as pltpu
from jax.sharding import PartitionSpec as P

HALO = 4
SEED = 64.0
SPREAD = 6.3
TILE = 8
LANES = 128
BF16, F32 = jnp.bfloat16, jnp.float32
EVEN_X, EVEN_Z, FIRST_X, FIRST_Z, COLOUR, UP, PREV_X, NEXT_X, PREV_Z, NEXT_Z = range(10)


def pair_routes(count, phase, closed=False):
    route = []
    for low in range(phase, count - 1, 2):
        route += [(low, low + 1), (low + 1, low)]
    if closed and phase == 1 and count % 2 == 0:
        route += [(count - 1, 0), (0, count - 1)]
    return route


def swap(block, axis, phase, closed=False):
    return lax.ppermute(block, axis, pair_routes(lax.axis_size(axis), phase, closed))


def lab_swap(block):
    return lax.ppermute(block, "lab", [(0, 1), (1, 0)])


def diagonal_swap(block, x_phase, z_phase):
    along_x = pair_routes(lax.axis_size("xy"), x_phase, True)
    along_z = pair_routes(lax.axis_size("gz"), z_phase, True)
    count = lax.axis_size("gz")
    route = [(sx * count + sz, dx * count + dz) for sx, dx in along_x for sz, dz in along_z]
    return lax.ppermute(block, ("xy", "gz"), route)


def split_swap(block):
    labs = lax.axis_size("lab")
    route = [
        (src * labs + lab, dst * labs + lab)
        for lab in range(labs)
        for src, dst in pair_routes(lax.axis_size("xy"), lab % 2, True)
    ]
    return lax.ppermute(block, ("xy", "lab"), route)


def split_diagonal_swap(block, z_phase):
    labs, count = lax.axis_size("lab"), lax.axis_size("gz")
    route = [
        ((sx * count + sz) * labs + lab, (dx * count + dz) * labs + lab)
        for lab in range(labs)
        for sx, dx in pair_routes(lax.axis_size("xy"), lab % 2, True)
        for sz, dz in pair_routes(count, z_phase, True)
    ]
    return lax.ppermute(block, ("xy", "gz", "lab"), route)


def everyones(copies, axes):
    return lax.all_to_all(copies, axes, 0, 0)


def call(kernel, outs, *ins, scratch=(), flops=1_000_000, name=None, space=pltpu.VMEM):
    specs = [pl.BlockSpec(memory_space=pltpu.SMEM)]
    specs += [pl.BlockSpec(memory_space=space)] * (len(ins) - 1)
    bytes_moved = sum(a.size * a.dtype.itemsize for a in ins)
    return pl.pallas_call(
        kernel,
        out_shape=outs,
        in_specs=specs,
        out_specs=jax.tree.map(lambda _: pl.BlockSpec(memory_space=pltpu.VMEM), outs),
        scratch_shapes=list(scratch),
        compiler_params=pltpu.CompilerParams(vmem_limit_bytes=40 * 2**20),
        cost_estimate=pl.CostEstimate(flops=flops, bytes_accessed=bytes_moved, transcendentals=0),
        name=name,
    )(*ins)


def shaped(shape, dtype):
    return jax.ShapeDtypeStruct(shape, dtype)


def rows_iota(rows=TILE):
    return lax.broadcasted_iota(jnp.int32, (rows, LANES), 0)


def lanes_iota(rows=TILE):
    return lax.broadcasted_iota(jnp.int32, (rows, LANES), 1)


def fields(planted, likelihood, slope, colours, colour):
    free = planted >= colours
    member = jnp.where(planted == colour, 1.0, 0.0)
    return jnp.where(free, slope, SEED), jnp.where(free, likelihood, member)


def pack(colours, two, info, image_in, planted_in, likelihoods_in, slope_in, image, planted, likelihoods, slope, *refs):
    faces, (send_a, send_b, sems) = refs[: 1 + two], refs[1 + two :]
    pairs = ((planted_in, planted), (slope_in, slope), (likelihoods_in, likelihoods), (image_in, image))
    copies = [pltpu.make_async_copy(src, dst, sems.at[n]) for n, (src, dst) in enumerate(pairs)]
    for copy in copies:
        copy.start()
    labels, rows_x, rows_z, _ = likelihoods.shape
    channels = image.shape[0]
    last, first = slice(rows_z - TILE, rows_z), slice(0, TILE)
    even = info[EVEN_X] == 1
    high, low = jnp.where(even, rows_x - 1, 0), jnp.where(even, 0, rows_x - 1)
    copies[0].wait()
    copies[1].wait()
    for x in range(rows_x):
        for l in range(labels):
            rhs = jnp.where(planted[x] >= colours, slope[l, x], SEED).astype(BF16)
            send_a[channels + l * rows_x + x] = rhs
            send_b[channels + l * rows_x + x] = rhs
    copies[2].wait()
    for l in range(labels):
        for send, at in ((send_a, high), (send_b, low)):
            for r in range(2):
                x = jnp.where(at == 0, 0, rows_x - 2) + r
                _, full = fields(planted[x], likelihoods[l, x], slope[l, x], colours, info[COLOUR] + l)
                send[channels + labels * rows_x + 2 * l + r] = full.astype(BF16)
    copies[3].wait()
    for c in range(channels):
        send_a[c] = image[c, high]
        send_b[c] = image[c, low]
    for phase, out in enumerate(faces):
        even = info[EVEN_Z] != phase
        place = (rows_iota() + jnp.where(even, 0, 4)) & 7

        def channel(c, x):
            return jnp.where(even, image[c, x, last].astype(F32), image[c, x, first].astype(F32))

        def turned(tile, for_even, for_odd):
            return jnp.where(even, pltpu.roll(tile, for_even, 0), pltpu.roll(tile, for_odd, 0))

        for x in range(rows_x):
            seeds = jnp.where(even, planted[x, last], planted[x, first])
            for l in range(labels):
                ends = [jnp.where(even, ref[l, x, last], ref[l, x, first]) for ref in (likelihoods, slope)]
                rhs, full = fields(seeds, *ends, colours, info[COLOUR] + l)
                first_channel = turned(channel(2 * l, x), 3, 6)
                second_channel = turned(channel(2 * l + 1, x), 4, 7)
                rest = jnp.where(place == 2, first_channel, second_channel)
                rest = jnp.where(place < 2, turned(full, 2, 4), rest)
                out[x, l] = jnp.where(place >= 4, rhs, rest).astype(BF16)


def sides(even, first, second):
    if second is None:
        return jnp.where(even, first, 0.0), jnp.where(even, 0.0, first)
    return jnp.where(even, first, second), jnp.where(even, second, first)


def ends_z(info, tiles, x, l):
    both = [ref[x, l].astype(F32) for ref in tiles]
    return sides(info[EVEN_Z] == 1, both[0], both[1] if len(both) > 1 else None)


def rhs_tile(above, below):
    return jnp.where(rows_iota() < 4, above, below)


def full_tile(above, below):
    return jnp.where(rows_iota() < 4, pltpu.roll(above, 4, 0), pltpu.roll(below, 6, 0))


def image_tile(info, above, below, c):
    up, down = (2, 5) if c % 2 == 0 else (1, 4)
    above = jnp.where(info[NEXT_Z] == 1, above, 0.0)
    below = jnp.where(info[PREV_Z] == 1, below, 0.0)
    return jnp.where(rows_iota() < 4, pltpu.roll(above, up, 0), pltpu.roll(below, down, 0))


def band(half, j, o, transposed=False):
    z, lane = rows_iota(), lanes_iota()
    other = lane & 7
    at = (z + 1 - other - 8 * o) if transposed else (other + 8 * o - z + 1)
    mask = at == j
    if half is not None:
        mask = mask & ((lane >> 6) == half)
    return mask


def bands(o, transposed=False):
    if o == 0:
        return (0, 1, 2)
    return (0,) if (o < 0) != transposed else (2,)


def spread_filter(info, first, second, one, two, wide_out, back_out):
    wide = jnp.dot(first[...], one[...], preferred_element_type=F32)
    back = jnp.dot(second[...], two[...], preferred_element_type=F32)
    zero = jnp.zeros((TILE, LANES), F32)
    for o in (-1, 0, 1):
        masks = {(h, j): band(h, j, o) for h in range(2) for j in bands(o)}
        for kd in range(9):
            for pair in range(2):
                for block in range(3):
                    tiles = []
                    for x in (2 * pair, 2 * pair + 1):
                        tile = zero
                        for i in range(3):
                            if (x + i) // 2 == block:
                                for j in bands(o):
                                    row = kd * 9 + i * 3 + j
                                    value = jnp.broadcast_to(wide[row : row + 1], (TILE, LANES))
                                    tile = jnp.where(masks[(x + i) % 2, j], value, tile)
                        tiles.append(tile)
                    at = (kd * 4 + 2 * pair) * TILE
                    wide_out[o + 1, at : at + 16, block * LANES : (block + 1) * LANES] = jnp.concatenate(
                        tiles, axis=0
                    ).astype(BF16)
        masks = {j: band(None, j, o, True) for j in bands(o, True)}
        for c in range(8):
            for pair in range(2):
                for block in range(6):
                    tiles = []
                    for x in (2 * pair, 2 * pair + 1):
                        tile = zero
                        i = x + 2 - block
                        if 0 <= i < 3:
                            for j in bands(o, True):
                                row = c * 9 + i * 3 + j
                                value = jnp.broadcast_to(back[row : row + 1], (TILE, LANES))
                                tile = jnp.where(masks[j], value, tile)
                        tiles.append(tile)
                    at = (c * 4 + 2 * pair) * TILE
                    back_out[o + 1, at : at + 16, block * LANES : (block + 1) * LANES] = jnp.concatenate(
                        tiles, axis=0
                    ).astype(BF16)


def tile_rows(t):
    at = (4 if t < 0 else t) * TILE
    return slice(at, at + TILE)


def convolve(two, info, image, first, second, *refs):
    faces, edges_a, edges_b = refs[: 1 + two], refs[1 + two : 2 + 2 * two], refs[2 + 2 * two : 3 + 3 * two]
    matrix, part, stack, sums = refs[3 + 3 * two :]
    channels, rows_x = image.shape[0], image.shape[1]
    even = info[EVEN_X] == 1
    for xp in range(rows_x + 2):
        for c in range(0, channels, 2):
            planes = []
            if 0 < xp <= rows_x:
                ends = [ends_z(info, faces, xp - 1, c // 2)]
            else:
                ends = [ends_z(info, tiles, rows_x - 1 if xp == 0 else 0, c // 2) for tiles in (edges_a, edges_b)]
            for ch in (c, c + 1):
                tiles = [image_tile(info, *pair, ch) for pair in ends]
                if 0 < xp <= rows_x:
                    planes.append(jnp.concatenate([image[ch, xp - 1].astype(F32), tiles[0]], axis=0))
                else:
                    received = [
                        jnp.concatenate([ref[ch].astype(F32), tile], axis=0)
                        for ref, tile in zip((first, second), tiles)
                    ]
                    above, below = sides(even, *received)
                    plane, exists = (below, PREV_X) if xp == 0 else (above, NEXT_X)
                    planes.append(jnp.where(info[exists] == 1, plane, 0.0))
            at = (xp * channels + c) * TILE
            for t in range(-1, 5):
                both = jnp.concatenate([plane[tile_rows(t)] for plane in planes], axis=0)
                stack[at : at + 16, (t + 1) * LANES : (t + 2) * LANES] = both.astype(BF16)
    total = jnp.dot(matrix[0], stack[:, 0:512], preferred_element_type=F32)
    total = total + jnp.dot(matrix[1], stack[:, 128:640], preferred_element_type=F32)
    sums[...] = total + jnp.dot(matrix[2], stack[:, 256:768], preferred_element_type=F32)
    lane = lanes_iota()
    for d in range(3):
        for x in range(rows_x):
            for t in range(4):
                cols = slice(t * LANES, (t + 1) * LANES)

                def piece(k):
                    at = ((k * 3 + d) * rows_x + x) * TILE
                    return sums[at : at + TILE, cols]

                before = jnp.where(lane > 0, pltpu.roll(piece(0), 1, 1), 0.0)
                after = jnp.where(lane < LANES - 1, pltpu.roll(piece(2), LANES - 1, 1), 0.0)
                part[d, x, tile_rows(t)] = piece(1) + before + after


def add_parts(two, info, part, other, logits, brick, *faces):
    rows_x, rows_z = part.shape[1], part.shape[2]
    for d in range(3):
        for x in range(rows_x):
            total = part[d, x] + other[d, x]
            logits[d, x] = total
            brick[d, x] = total.astype(BF16)
            for phase, face in enumerate(faces):
                even = info[EVEN_Z] != phase
                face[d, x] = jnp.where(even, total[rows_z - TILE :], total[:TILE]).astype(BF16)


def up(plane, dim):
    return pltpu.roll(plane, plane.shape[dim] - 1, dim)


def down(plane, dim):
    return pltpu.roll(plane, 1, dim)


def krylov(colours, size_x, size_z, two, info, planted, slope, logits, mine, other, first, second, *refs):
    groups = [refs[n * (1 + two) : (n + 1) * (1 + two)] for n in range(6)]
    faces, mine_edges, other_edges, rhs_faces, edges_a, edges_b = groups
    v0, v1, v2, slope_out, dots_out, weight, free, dots = refs[6 * (1 + two) :]
    labels, rows_x, rows_z, _ = slope.shape
    rows = rows_z + TILE
    channels = 2 * labels
    is_up, even = info[UP] == 1, info[EVEN_X] == 1
    z = rows_iota(rows)
    z = info[FIRST_Z] + jnp.where(z < rows_z + HALO, z, z - rows)
    inside_z = (z >= 0) & (z < size_z)
    in_z = jnp.where(inside_z, 1.0, 0.0)
    next_z = jnp.where(inside_z & (z < size_z - 1), 1.0, 0.0)
    in_zy = jnp.where(lanes_iota(rows) < LANES - 1, in_z, 0.0)
    for at in range(rows_x + 2 * HALO):
        x = at - HALO
        place = info[FIRST_X] + x
        inside = (place >= 0) & (place < size_x)
        in_x = jnp.where(inside, 1.0, 0.0)
        next_x = jnp.where(inside & (place < size_x - 1), 1.0, 0.0)
        for d in range(3):
            def grown(plane, tiles, source):
                return jnp.concatenate([plane, rhs_tile(*ends_z(info, tiles, d, source))], axis=0)

            if 0 <= x < rows_x:
                plane = grown(logits[d, x], faces, x)
            else:
                source = x % rows_x
                here = grown(mine[d, source].astype(F32), mine_edges, source)
                there = grown(other[d, source].astype(F32), other_edges, source)
                plane = jnp.where(is_up, there, here) if x < 0 else jnp.where(is_up, here, there)
            squashed = 1.0 / (1.0 + jnp.exp(-plane))
            valid = (in_z * next_x, next_z * in_x, in_zy * in_x)[d]
            weight[d, at] = (0.05 + squashed) * valid
            if -1 <= x <= rows_x:
                slope_out[d, x + 1] = squashed * (1.0 - squashed) * valid
        for l in range(labels):
            source = x % rows_x
            if 0 <= x < rows_x:
                plane = jnp.where(planted[x] >= colours, slope[l, x], SEED)
                plane = jnp.concatenate([plane, rhs_tile(*ends_z(info, rhs_faces, x, l))], axis=0)
            else:
                index = channels + l * rows_x + source
                received = [
                    jnp.concatenate([ref[index].astype(F32), rhs_tile(*ends_z(info, tiles, source, l))], axis=0)
                    for ref, tiles in ((first, edges_a), (second, edges_b))
                ]
                above, below = sides(even, *received)
                plane = below if x < 0 else above
            open_cell = plane < SEED / 2
            v0[l, at] = jnp.where(open_cell, plane, 0.0)
            if l == 0:
                free[at] = jnp.where(open_cell, 1.0, 0.0)

    def label(l, carry):
        def operate(v, start, stop):
            flow_before = weight[0, start - 1] * (v[l, start - 1] - v[l, start])
            for at in range(start, stop):
                here = v[l, at]
                flow = weight[0, at] * (here - v[l, at + 1])
                flow_z = weight[1, at] * (here - up(here, 0))
                flow_y = weight[2, at] * (here - up(here, 1))
                result = flow - flow_before + (flow_z - down(flow_z, 0)) + (flow_y - down(flow_y, 1))
                yield at, here, free[at] * result
                flow_before = flow

        for at, here, result in operate(v0, 1, rows_x + 2 * HALO - 1):
            v1[l, at] = result * (1.0 / SPREAD) - here
        for at, here, result in operate(v1, 2, rows_x + 2 * HALO - 2):
            v2[l, at] = result * (2.0 / SPREAD) - 2.0 * here - v0[l, at]
        sums = [jnp.zeros((TILE, LANES), F32)] * 6
        for at, here, result in operate(v2, HALO, HALO + rows_x):
            a, b = v0[l, at], v1[l, at]
            for n, product in enumerate((a * a, a * b, b * b, b * here, here * here, here * result)):
                for t in range(rows_z // TILE):
                    sums[n] = sums[n] + product[tile_rows(t)]
        for n in range(6):
            dots[pl.ds(n * labels + l, 1), :] = jnp.sum(sums[n], axis=0, keepdims=True)
        return carry

    lax.fori_loop(0, labels, label, 0)
    total = jnp.sum(dots[...], axis=1, keepdims=True)
    tile = jnp.zeros((TILE, LANES), F32)
    for n in range(6):
        column = total[tile_rows(n // 2)]
        column = jnp.broadcast_to(column, (TILE, LANES))
        tile = jnp.where(lanes_iota() == n, pltpu.roll(column, 4, 0) if n % 2 else column, tile)
    for n in range(dots_out.shape[0]):
        dots_out[n] = tile


def steps(g00, g01, g11, g12, g22, k22):
    g02 = 2.0 * g11 - g00
    k00 = SPREAD * (g00 + g01)
    k01 = SPREAD * (g01 + g11)
    k02 = SPREAD * (g02 + g12)
    k11 = SPREAD * (g11 + 0.5 * (g12 + g01))
    k12 = SPREAD * (g12 + 0.5 * (g22 + g02))
    alpha = g00 / k00
    c0 = alpha
    r0 = 1.0 - alpha * SPREAD
    r1 = -alpha * SPREAD
    rr = r0 * r0 * g00 + 2.0 * r0 * r1 * g01 + r1 * r1 * g11
    beta = rr / g00
    p0, p1 = r0 + beta, r1
    alpha = rr / (p0 * p0 * k00 + 2.0 * p0 * p1 * k01 + p1 * p1 * k11)
    c0, c1 = c0 + alpha * p0, alpha * p1
    r0 = r0 - alpha * SPREAD * (p0 + 0.5 * p1)
    r1 = r1 - alpha * SPREAD * (p0 + p1)
    r2 = -alpha * SPREAD * 0.5 * p1
    rr_next = r0 * r0 * g00 + r1 * r1 * g11 + r2 * r2 * g22
    rr_next = rr_next + 2.0 * (r0 * r1 * g01 + r0 * r2 * g02 + r1 * r2 * g12)
    beta = rr_next / rr
    p0, p1, p2 = r0 + beta * p0, r1 + beta * p1, r2
    curve = p0 * p0 * k00 + p1 * p1 * k11 + p2 * p2 * k22
    curve = curve + 2.0 * (p0 * p1 * k01 + p0 * p2 * k02 + p1 * p2 * k12)
    alpha = rr_next / curve
    return c0 + alpha * p0, c1 + alpha * p1, alpha * p2


def edges(colours, two, info, parts, v0, v1, v2, planted, likelihoods, first, second, *refs):
    faces, edges_a, edges_b = refs[: 1 + two], refs[1 + two : 2 + 2 * two], refs[2 + 2 * two : 3 + 3 * two]
    out, lam, field = refs[3 + 3 * two :]
    labels, rows_x, rows_z, _ = likelihoods.shape
    rows = rows_z + TILE
    even = info[EVEN_X] == 1
    total = jnp.sum(parts[...], axis=0)
    grams = [jnp.broadcast_to(total[:, n : n + 1], (TILE, LANES)) for n in range(6)]
    c0, c1, c2 = steps(*grams)
    for l in range(labels):
        s0, s1, s2 = (jnp.broadcast_to(c[l : l + 1], (rows, LANES)) for c in (c0, c1, c2))
        for at in range(rows_x + 3):
            source = at + HALO - 1
            lam[l, at] = s0 * v0[l, source] + s1 * v1[l, source] + s2 * v2[l, source]
            x = at - 1
            source = x % rows_x
            if 0 <= x < rows_x:
                member = jnp.where(planted[x] == info[COLOUR] + l, 1.0, 0.0)
                plane = jnp.where(planted[x] >= colours, likelihoods[l, x], member)
                plane = jnp.concatenate([plane, full_tile(*ends_z(info, faces, x, l))], axis=0)
            else:
                index = 2 * labels + labels * rows_x + 2 * l + (1 if x < 0 else source)
                received = [
                    jnp.concatenate([ref[index].astype(F32), full_tile(*ends_z(info, tiles, source, l))], axis=0)
                    for ref, tiles in ((first, edges_a), (second, edges_b))
                ]
                above, below = sides(even, *received)
                plane = below if x < 0 else above
            field[l, at] = plane
    for at in range(rows_x + 2):
        sums = [jnp.zeros((rows, LANES), F32)] * 3
        for l in range(labels):
            a, b = lam[l, at], field[l, at]
            sums[0] = sums[0] - (a - lam[l, at + 1]) * (b - field[l, at + 1])
            sums[1] = sums[1] - (a - up(a, 0)) * (b - up(b, 0))
            sums[2] = sums[2] - (a - up(a, 1)) * (b - up(b, 1))
        for d in range(3):
            out[d, at] = sums[d]


def filter_sums(info, edge, other, slope, stack, one, grads, out, products, rows_out):
    rows_x = edge.shape[1] - 2
    lane = lanes_iota(edge.shape[2])
    for xp in range(rows_x + 2):
        shifted = [[], [], []]
        for d in range(3):
            plane = ((edge[d, xp] + other[d, xp]) * slope[d, xp]).astype(BF16).astype(F32)
            shifted[0].append(jnp.where(lane < LANES - 1, up(plane, 1), 0.0))
            shifted[1].append(plane)
            shifted[2].append(jnp.where(lane > 0, down(plane, 1), 0.0))
        planes = shifted[0] + shifted[1] + shifted[2]
        planes += [jnp.zeros_like(planes[0])] * 7
        for pair in range(8):
            at = (xp * 16 + 2 * pair) * TILE
            for t in range(-1, 5):
                both = jnp.concatenate([plane[tile_rows(t)] for plane in planes[2 * pair : 2 * pair + 2]], axis=0)
                grads[at : at + 16, (t + 1) * LANES : (t + 2) * LANES] = both.astype(BF16)
    own = grads[LANES : LANES * (rows_x + 1), LANES : 5 * LANES]
    for o in range(3):
        products[o] = lax.dot_general(
            own, stack[:, o * LANES : (o + 4) * LANES], (((1,), (1,)), ((), ())), preferred_element_type=F32
        )
    rows_out[...] = jnp.zeros_like(rows_out)
    masks = {(h, j, o): band(h, j, o) for o in (-1, 0, 1) for h in range(2) for j in bands(o)}
    for kd in range(9):
        k, d = kd // 3, kd % 3
        for i in range(3):
            for j in range(3):
                total = jnp.zeros((TILE, LANES), F32)
                for o in (-1, 0, 1):
                    if j in bands(o):
                        for x in range(rows_x):
                            at = (x * 16 + kd) * TILE
                            col = (x + i) // 2 * LANES
                            piece = products[o + 1, at : at + TILE, col : col + LANES]
                            total = total + jnp.where(masks[(x + i) % 2, j, o], piece, 0.0)
                row = d * 27 + i * 9 + j * 3 + k
                rows_out[row : row + 1] = jnp.sum(total, axis=0, keepdims=True)
    sums = lax.dot_general(
        one[...],
        rows_out[...],
        (((1,), (1,)), ((), ())),
        precision=lax.Precision.HIGHEST,
        preferred_element_type=F32,
    )
    for n in range(out.shape[0]):
        out[n] = sums


def image_sums(info, grads, matrix, out, sums):
    total = jnp.dot(matrix[0], grads[:, 0:512], preferred_element_type=F32)
    total = total + jnp.dot(matrix[1], grads[:, 128:640], preferred_element_type=F32)
    sums[...] = total + jnp.dot(matrix[2], grads[:, 256:768], preferred_element_type=F32)
    channels, rows_x, rows_z, _ = out.shape
    for c in range(channels):
        for x in range(rows_x):
            at = (c * rows_x + x) * TILE
            for t in range(0, rows_z // TILE, 2):
                both = [sums[at : at + TILE, s * LANES : (s + 1) * LANES] for s in (t, t + 1)]
                out[c, x, t * TILE : (t + 2) * TILE] = jnp.concatenate(both, axis=0).astype(BF16)


def local(image, filt, planted, likelihoods, slope):
    channels = image.shape[0]
    labels, rows_x, rows_z, rows_y = likelihoods.shape
    if (channels, labels, rows_x, rows_z, rows_y) != (8, 4, HALO, 4 * TILE, LANES):
        raise ValueError("brick size")
    lab, xy, gz = lax.axis_index("lab"), lax.axis_index("xy"), lax.axis_index("gz")
    colours = labels * lax.axis_size("lab")
    size_x, size_z = rows_x * lax.axis_size("xy"), rows_z * lax.axis_size("gz")
    rows = rows_z + TILE
    two = lax.axis_size("gz") > 2
    phases = range(1 + two)
    members = lax.axis_size("xy") * lax.axis_size("gz")
    info = jnp.stack(
        [
            1 - xy % 2,
            1 - gz % 2,
            xy * rows_x,
            gz * rows_z,
            lab * labels,
            1 - (xy + lab) % 2,
            jnp.minimum(xy, 1),
            jnp.minimum(lax.axis_size("xy") - 1 - xy, 1),
            jnp.minimum(gz, 1),
            jnp.minimum(lax.axis_size("gz") - 1 - gz, 1),
        ]
    ).astype(jnp.int32)

    inputs = (image, planted, likelihoods, slope)
    planes = channels + labels * rows_x + 2 * labels
    brick = shaped((planes, rows_z, LANES), BF16)
    image, planted, likelihoods, slope, *packed = call(
        functools.partial(pack, colours, two),
        [shaped(a.shape, a.dtype) for a in inputs]
        + [shaped((rows_x, labels, TILE, LANES), BF16)] * (1 + two)
        + [brick, brick],
        info,
        *inputs,
        scratch=[pltpu.SemaphoreType.DMA((4,))],
        name="pack",
        space=pltpu.HBM,
    )
    send_a, send_b = packed[1 + two :]
    faces = [swap(packed[phase], "gz", phase, True) for phase in phases]
    edges_a = [diagonal_swap(packed[phase], 0, phase) for phase in phases]
    edges_b = [diagonal_swap(packed[phase], 1, phase) for phase in phases]
    second = swap(send_b, "xy", 1)
    first = swap(send_a, "xy", 0)
    received = (first, second, *faces, *edges_a, *edges_b)

    own_filt = lax.dynamic_slice_in_dim(filt, lab * channels, channels, 1)
    lines = jnp.transpose(own_filt, (4, 0, 2, 3, 1)).reshape(81, channels)
    lines = jnp.pad(lines, ((0, 7), (0, LANES - channels)))
    backs = jnp.transpose(own_filt, (1, 2, 3, 4, 0)).reshape(72, 9)
    backs = jnp.pad(backs, ((0, 0), (0, LANES - 9)))
    lane = jnp.arange(LANES, dtype=jnp.int32)
    by_channel = ((lane[None] >> 3) & 7) == lane[:, None]
    by_edge = (lane[None] >> 3) == lane[:, None]
    matrix, back_matrix = call(
        spread_filter,
        [shaped((3, 288, 384), BF16), shaped((3, 256, 768), BF16)],
        info,
        lines,
        backs,
        by_channel.astype(BF16),
        by_edge.astype(BF16),
        flops=10_000_000,
        name="spread_filter",
    )
    part, stack = call(
        functools.partial(convolve, two),
        [shaped((3, rows_x, rows_z, LANES), F32), shaped((384, 768), BF16)],
        info,
        image,
        *received,
        matrix,
        scratch=[pltpu.VMEM((288, 512), F32)],
        name="convolve",
    )
    logits, own, *sends = call(
        functools.partial(add_parts, two),
        [shaped(part.shape, F32), shaped(part.shape, BF16)]
        + [shaped((3, rows_x, TILE, LANES), BF16)] * (1 + two),
        info,
        part,
        lab_swap(part),
        name="add_parts",
    )
    mine = split_swap(own)
    mine_edges = [split_diagonal_swap(sends[phase], phase) for phase in phases]
    logit_faces = [swap(sends[phase], "gz", phase, True) for phase in phases]
    mine, mine_edges, logit_faces = lax.optimization_barrier((mine, mine_edges, logit_faces))
    other = lab_swap(mine)
    other_edges = [lab_swap(block) for block in mine_edges]
    extended = (labels, rows_x + 2 * HALO, rows, LANES)
    ring = shaped((3, rows_x + 2, rows, LANES), F32)
    v0, v1, v2, squash_slope, dots = call(
        functools.partial(krylov, colours, size_x, size_z, two),
        [shaped(extended, F32)] * 3 + [ring, shaped((members, TILE, LANES), F32)],
        info,
        planted,
        slope,
        logits,
        mine,
        other,
        first,
        second,
        *logit_faces,
        *mine_edges,
        *other_edges,
        *faces,
        *edges_a,
        *edges_b,
        scratch=[
            pltpu.VMEM((3,) + extended[1:], F32),
            pltpu.VMEM(extended[1:], F32),
            pltpu.VMEM((6 * labels, LANES), F32),
        ],
        name="krylov",
    )
    edge = call(
        functools.partial(edges, colours, two),
        ring,
        info,
        everyones(dots, ("xy", "gz")),
        v0,
        v1,
        v2,
        planted,
        likelihoods,
        *received,
        scratch=[pltpu.VMEM((labels, rows_x + 3, rows, LANES), F32)] * 2,
        name="edges",
    )
    grads, sums = call(
        filter_sums,
        [shaped((768, 768), BF16), shaped((members, TILE, LANES), F32)],
        info,
        edge,
        lab_swap(edge),
        squash_slope,
        stack,
        by_channel[:TILE].astype(F32),
        scratch=[pltpu.VMEM((3, 512, 384), F32), pltpu.VMEM((LANES, LANES), F32)],
        name="filter_sums",
    )
    grad_image = call(
        image_sums,
        shaped(image.shape, BF16),
        info,
        grads,
        back_matrix,
        scratch=[pltpu.VMEM((256, 512), F32)],
        flops=10_000_000,
        name="image_sums",
    )
    grad_filter = jnp.sum(everyones(sums, ("xy", "gz")), axis=0)
    grad_filter = grad_filter[:, :81].reshape(channels, 3, 27)
    return grad_image, jnp.transpose(grad_filter, (1, 0, 2)).reshape(3, channels, 3, 3, 3)


def solution(mesh):
    return jax.shard_map(
        local,
        mesh=mesh,
        in_specs=(
            P("lab", ("crops", "xy"), "gz", None),
            P(),
            P(("crops", "xy"), "gz", None),
            P("lab", ("crops", "xy"), "gz", None),
            P("lab", ("crops", "xy"), "gz", None),
        ),
        out_specs=(P("lab", ("crops", "xy"), "gz", None), P("crops", "lab", None, None, None)),
        check_vma=False,
    )
```

```python
import functools

import jax
import jax.numpy as jnp
from jax import lax
from jax.experimental import pallas as pl
from jax.experimental.pallas import tpu as pltpu
from jax.sharding import PartitionSpec as P

HALO = 4
SEED = 64.0
SPREAD = 6.3
TILE = 8
LANES = 128
BF16, F32 = jnp.bfloat16, jnp.float32
EVEN_X, EVEN_Z, FIRST_X, FIRST_Z, COLOUR, UP, PREV_X, NEXT_X, PREV_Z, NEXT_Z = range(10)


def pair_routes(count, phase, closed=False):
    route = []
    for low in range(phase, count - 1, 2):
        route += [(low, low + 1), (low + 1, low)]
    if closed and phase == 1 and count % 2 == 0:
        route += [(count - 1, 0), (0, count - 1)]
    return route


def swap(block, axis, phase, closed=False):
    return lax.ppermute(block, axis, pair_routes(lax.axis_size(axis), phase, closed))


def lab_swap(block):
    return lax.ppermute(block, "lab", [(0, 1), (1, 0)])


def diagonal_swap(block, x_phase, z_phase):
    along_x = pair_routes(lax.axis_size("xy"), x_phase, True)
    along_z = pair_routes(lax.axis_size("gz"), z_phase, True)
    count = lax.axis_size("gz")
    route = [(sx * count + sz, dx * count + dz) for sx, dx in along_x for sz, dz in along_z]
    return lax.ppermute(block, ("xy", "gz"), route)


def split_swap(block):
    labs = lax.axis_size("lab")
    route = [
        (src * labs + lab, dst * labs + lab)
        for lab in range(labs)
        for src, dst in pair_routes(lax.axis_size("xy"), lab % 2, True)
    ]
    return lax.ppermute(block, ("xy", "lab"), route)


def split_diagonal_swap(block, z_phase):
    labs, count = lax.axis_size("lab"), lax.axis_size("gz")
    route = [
        ((sx * count + sz) * labs + lab, (dx * count + dz) * labs + lab)
        for lab in range(labs)
        for sx, dx in pair_routes(lax.axis_size("xy"), lab % 2, True)
        for sz, dz in pair_routes(count, z_phase, True)
    ]
    return lax.ppermute(block, ("xy", "gz", "lab"), route)


def everyones(copies, axes):
    return lax.all_to_all(copies, axes, 0, 0)


def call(kernel, outs, *ins, scratch=(), flops=1_000_000, name=None, space=pltpu.VMEM):
    specs = [pl.BlockSpec(memory_space=pltpu.SMEM)]
    specs += [pl.BlockSpec(memory_space=space)] * (len(ins) - 1)
    bytes_moved = sum(a.size * a.dtype.itemsize for a in ins)
    return pl.pallas_call(
        kernel,
        out_shape=outs,
        in_specs=specs,
        out_specs=jax.tree.map(lambda _: pl.BlockSpec(memory_space=pltpu.VMEM), outs),
        scratch_shapes=list(scratch),
        compiler_params=pltpu.CompilerParams(vmem_limit_bytes=40 * 2**20),
        cost_estimate=pl.CostEstimate(flops=flops, bytes_accessed=bytes_moved, transcendentals=0),
        name=name,
    )(*ins)


def shaped(shape, dtype):
    return jax.ShapeDtypeStruct(shape, dtype)


def rows_iota(rows=TILE):
    return lax.broadcasted_iota(jnp.int32, (rows, LANES), 0)


def lanes_iota(rows=TILE):
    return lax.broadcasted_iota(jnp.int32, (rows, LANES), 1)


def fields(planted, likelihood, slope, colours, colour):
    free = planted >= colours
    member = jnp.where(planted == colour, 1.0, 0.0)
    return jnp.where(free, slope, SEED), jnp.where(free, likelihood, member)


def pack(
    colours,
    two,
    info,
    filt_in,
    image_in,
    planted_in,
    likelihoods_in,
    slope_in,
    wide_out,
    back_out,
    image,
    planted,
    likelihoods,
    slope,
    *refs,
):
    faces, (send_a, send_b, filt, taps, sems) = refs[: 1 + two], refs[1 + two :]
    pairs = (
        (planted_in, planted),
        (slope_in, slope),
        (likelihoods_in, likelihoods),
        (image_in, image),
        (filt_in, filt),
    )
    copies = [pltpu.make_async_copy(src, dst, sems.at[n]) for n, (src, dst) in enumerate(pairs)]
    for copy in reversed(copies):
        copy.start()
    copies[4].wait()
    spread_filter(info, filt, taps, wide_out, back_out)
    labels, rows_x, rows_z, _ = likelihoods.shape
    channels = image.shape[0]
    last, first = slice(rows_z - TILE, rows_z), slice(0, TILE)
    even = info[EVEN_X] == 1
    high, low = jnp.where(even, rows_x - 1, 0), jnp.where(even, 0, rows_x - 1)
    copies[0].wait()
    copies[1].wait()
    for x in range(rows_x):
        for l in range(labels):
            rhs = jnp.where(planted[x] >= colours, slope[l, x], SEED).astype(BF16)
            send_a[channels + l * rows_x + x] = rhs
            send_b[channels + l * rows_x + x] = rhs
    copies[2].wait()
    for l in range(labels):
        for send, at in ((send_a, high), (send_b, low)):
            for r in range(2):
                x = jnp.where(at == 0, 0, rows_x - 2) + r
                _, full = fields(planted[x], likelihoods[l, x], slope[l, x], colours, info[COLOUR] + l)
                send[channels + labels * rows_x + 2 * l + r] = full.astype(BF16)
    copies[3].wait()
    for c in range(channels):
        send_a[c] = image[c, high]
        send_b[c] = image[c, low]
    for phase, out in enumerate(faces):
        even = info[EVEN_Z] != phase
        place = (rows_iota() + jnp.where(even, 0, 4)) & 7

        def channel(c, x):
            return jnp.where(even, image[c, x, last].astype(F32), image[c, x, first].astype(F32))

        def turned(tile, for_even, for_odd):
            return jnp.where(even, pltpu.roll(tile, for_even, 0), pltpu.roll(tile, for_odd, 0))

        for x in range(rows_x):
            seeds = jnp.where(even, planted[x, last], planted[x, first])
            for l in range(labels):
                ends = [jnp.where(even, ref[l, x, last], ref[l, x, first]) for ref in (likelihoods, slope)]
                rhs, full = fields(seeds, *ends, colours, info[COLOUR] + l)
                first_channel = turned(channel(2 * l, x), 3, 6)
                second_channel = turned(channel(2 * l + 1, x), 4, 7)
                rest = jnp.where(place == 2, first_channel, second_channel)
                rest = jnp.where(place < 2, turned(full, 2, 4), rest)
                out[x, l] = jnp.where(place >= 4, rhs, rest).astype(BF16)


def sides(even, first, second):
    if second is None:
        return jnp.where(even, first, 0.0), jnp.where(even, 0.0, first)
    return jnp.where(even, first, second), jnp.where(even, second, first)


def ends_z(info, tiles, x, l):
    both = [ref[x, l].astype(F32) for ref in tiles]
    return sides(info[EVEN_Z] == 1, both[0], both[1] if len(both) > 1 else None)


def rhs_tile(above, below):
    return jnp.where(rows_iota() < 4, above, below)


def full_tile(above, below):
    return jnp.where(rows_iota() < 4, pltpu.roll(above, 4, 0), pltpu.roll(below, 6, 0))


def image_tile(info, above, below, c):
    up, down = (2, 5) if c % 2 == 0 else (1, 4)
    above = jnp.where(info[NEXT_Z] == 1, above, 0.0)
    below = jnp.where(info[PREV_Z] == 1, below, 0.0)
    return jnp.where(rows_iota() < 4, pltpu.roll(above, up, 0), pltpu.roll(below, down, 0))


def band(half, j, o, transposed=False):
    z, lane = rows_iota(), lanes_iota()
    other = lane & 7
    at = (z + 1 - other - 8 * o) if transposed else (other + 8 * o - z + 1)
    mask = at == j
    if half is not None:
        mask = mask & ((lane >> 6) == half)
    return mask


def bands(o, transposed=False):
    if o == 0:
        return (0, 1, 2)
    return (0,) if (o < 0) != transposed else (2,)


def spread_filter(info, filt, taps, wide_out, back_out):
    taps[...] = jnp.zeros_like(taps)
    for d in range(3):
        for i in range(3):
            for j in range(3):
                at = (d * 9 + i * 3 + j) * 4
                taps[at : at + 3, : filt.shape[-1]] = filt[d, i, j].astype(F32)
    lane = lanes_iota(LANES)
    channel = rows_iota(LANES) - 2 * info[COLOUR]
    all_taps = taps[...].astype(BF16)
    by_channel = jnp.where(channel == ((lane >> 3) & 7), 1.0, 0.0).astype(BF16)
    own = jnp.dot(
        all_taps, jnp.where(channel == lane, 1.0, 0.0).astype(BF16), preferred_element_type=F32
    ).astype(BF16)
    wide = jnp.dot(all_taps, by_channel, preferred_element_type=F32)
    tap, edge = rows_iota(taps.shape[0]), lanes_iota(taps.shape[0]) >> 3
    shift = jnp.where(edge >= 3, 1, 0) + jnp.where(edge >= 6, 1, 0)
    first_tap = jnp.where(edge < 9, (edge - 3 * shift) * 36 + shift, -LANES)
    places = [jnp.where(tap == first_tap + 4 * ij, 1.0, 0.0).astype(BF16) for ij in range(9)]
    back = [
        lax.dot_general(own, place, (((0,), (0,)), ((), ())), preferred_element_type=F32) for place in places
    ]
    zero = jnp.zeros((TILE, LANES), F32)
    for o in (-1, 0, 1):
        masks = {(h, j): band(h, j, o) for h in range(2) for j in bands(o)}
        for kd in range(9):
            for pair in range(2):
                for block in range(3):
                    tiles = []
                    for x in (2 * pair, 2 * pair + 1):
                        tile = zero
                        for i in range(3):
                            if (x + i) // 2 == block:
                                for j in bands(o):
                                    row = (kd % 3 * 9 + i * 3 + j) * 4 + kd // 3
                                    value = jnp.broadcast_to(wide[row : row + 1], (TILE, LANES))
                                    tile = jnp.where(masks[(x + i) % 2, j], value, tile)
                        tiles.append(tile)
                    at = (kd * 4 + 2 * pair) * TILE
                    wide_out[o + 1, at : at + 16, block * LANES : (block + 1) * LANES] = jnp.concatenate(
                        tiles, axis=0
                    ).astype(BF16)
        masks = {j: band(None, j, o, True) for j in bands(o, True)}
        for c in range(8):
            for pair in range(2):
                for block in range(6):
                    tiles = []
                    for x in (2 * pair, 2 * pair + 1):
                        tile = zero
                        i = x + 2 - block
                        if 0 <= i < 3:
                            for j in bands(o, True):
                                value = jnp.broadcast_to(back[i * 3 + j][c : c + 1], (TILE, LANES))
                                tile = jnp.where(masks[j], value, tile)
                        tiles.append(tile)
                    at = (c * 4 + 2 * pair) * TILE
                    back_out[o + 1, at : at + 16, block * LANES : (block + 1) * LANES] = jnp.concatenate(
                        tiles, axis=0
                    ).astype(BF16)


def tile_rows(t):
    at = (4 if t < 0 else t) * TILE
    return slice(at, at + TILE)


def convolve(two, info, image, first, second, *refs):
    faces, edges_a, edges_b = refs[: 1 + two], refs[1 + two : 2 + 2 * two], refs[2 + 2 * two : 3 + 3 * two]
    matrix, part, stack, sums = refs[3 + 3 * two :]
    channels, rows_x = image.shape[0], image.shape[1]
    even = info[EVEN_X] == 1
    for xp in range(rows_x + 2):
        for c in range(0, channels, 2):
            planes = []
            if 0 < xp <= rows_x:
                ends = [ends_z(info, faces, xp - 1, c // 2)]
            else:
                ends = [ends_z(info, tiles, rows_x - 1 if xp == 0 else 0, c // 2) for tiles in (edges_a, edges_b)]
            for ch in (c, c + 1):
                tiles = [image_tile(info, *pair, ch) for pair in ends]
                if 0 < xp <= rows_x:
                    planes.append(jnp.concatenate([image[ch, xp - 1].astype(F32), tiles[0]], axis=0))
                else:
                    received = [
                        jnp.concatenate([ref[ch].astype(F32), tile], axis=0)
                        for ref, tile in zip((first, second), tiles)
                    ]
                    above, below = sides(even, *received)
                    plane, exists = (below, PREV_X) if xp == 0 else (above, NEXT_X)
                    planes.append(jnp.where(info[exists] == 1, plane, 0.0))
            at = (xp * channels + c) * TILE
            for t in range(-1, 5):
                both = jnp.concatenate([plane[tile_rows(t)] for plane in planes], axis=0)
                stack[at : at + 16, (t + 1) * LANES : (t + 2) * LANES] = both.astype(BF16)
    total = jnp.dot(matrix[0], stack[:, 0:512], preferred_element_type=F32)
    total = total + jnp.dot(matrix[1], stack[:, 128:640], preferred_element_type=F32)
    sums[...] = total + jnp.dot(matrix[2], stack[:, 256:768], preferred_element_type=F32)
    lane = lanes_iota()
    for d in range(3):
        for x in range(rows_x):
            for t in range(4):
                cols = slice(t * LANES, (t + 1) * LANES)

                def piece(k):
                    at = ((k * 3 + d) * rows_x + x) * TILE
                    return sums[at : at + TILE, cols]

                before = jnp.where(lane > 0, pltpu.roll(piece(0), 1, 1), 0.0)
                after = jnp.where(lane < LANES - 1, pltpu.roll(piece(2), LANES - 1, 1), 0.0)
                part[d, x, tile_rows(t)] = piece(1) + before + after


def add_parts(two, info, part, other, logits, brick, *faces):
    rows_x, rows_z = part.shape[1], part.shape[2]
    for d in range(3):
        for x in range(rows_x):
            total = part[d, x] + other[d, x]
            logits[d, x] = total
            brick[d, x] = total.astype(BF16)
            for phase, face in enumerate(faces):
                even = info[EVEN_Z] != phase
                face[d, x] = jnp.where(even, total[rows_z - TILE :], total[:TILE]).astype(BF16)


def up(plane, dim):
    return pltpu.roll(plane, plane.shape[dim] - 1, dim)


def down(plane, dim):
    return pltpu.roll(plane, 1, dim)


def krylov(colours, size_x, size_z, two, info, planted, slope, logits, mine, other, first, second, *refs):
    groups = [refs[n * (1 + two) : (n + 1) * (1 + two)] for n in range(6)]
    faces, mine_edges, other_edges, rhs_faces, edges_a, edges_b = groups
    v0, v1, v2, slope_out, dots_out, weight, free, dots = refs[6 * (1 + two) :]
    labels, rows_x, rows_z, _ = slope.shape
    rows = rows_z + TILE
    channels = 2 * labels
    is_up, even = info[UP] == 1, info[EVEN_X] == 1
    z = rows_iota(rows)
    z = info[FIRST_Z] + jnp.where(z < rows_z + HALO, z, z - rows)
    inside_z = (z >= 0) & (z < size_z)
    in_z = jnp.where(inside_z, 1.0, 0.0)
    next_z = jnp.where(inside_z & (z < size_z - 1), 1.0, 0.0)
    in_zy = jnp.where(lanes_iota(rows) < LANES - 1, in_z, 0.0)
    for at in range(rows_x + 2 * HALO):
        x = at - HALO
        place = info[FIRST_X] + x
        inside = (place >= 0) & (place < size_x)
        in_x = jnp.where(inside, 1.0, 0.0)
        next_x = jnp.where(inside & (place < size_x - 1), 1.0, 0.0)
        for d in range(3):
            def grown(plane, tiles, source):
                return jnp.concatenate([plane, rhs_tile(*ends_z(info, tiles, d, source))], axis=0)

            if 0 <= x < rows_x:
                plane = grown(logits[d, x], faces, x)
            else:
                source = x % rows_x
                here = grown(mine[d, source].astype(F32), mine_edges, source)
                there = grown(other[d, source].astype(F32), other_edges, source)
                plane = jnp.where(is_up, there, here) if x < 0 else jnp.where(is_up, here, there)
            squashed = 1.0 / (1.0 + jnp.exp(-plane))
            valid = (in_z * next_x, next_z * in_x, in_zy * in_x)[d]
            weight[d, at] = (0.05 + squashed) * valid
            if -1 <= x <= rows_x:
                slope_out[d, x + 1] = squashed * (1.0 - squashed) * valid
        for l in range(labels):
            source = x % rows_x
            if 0 <= x < rows_x:
                plane = jnp.where(planted[x] >= colours, slope[l, x], SEED)
                plane = jnp.concatenate([plane, rhs_tile(*ends_z(info, rhs_faces, x, l))], axis=0)
            else:
                index = channels + l * rows_x + source
                received = [
                    jnp.concatenate([ref[index].astype(F32), rhs_tile(*ends_z(info, tiles, source, l))], axis=0)
                    for ref, tiles in ((first, edges_a), (second, edges_b))
                ]
                above, below = sides(even, *received)
                plane = below if x < 0 else above
            open_cell = plane < SEED / 2
            v0[l, at] = jnp.where(open_cell, plane, 0.0)
            if l == 0:
                free[at] = jnp.where(open_cell, 1.0, 0.0)

    def label(l, carry):
        def operate(v, start, stop):
            flow_before = weight[0, start - 1] * (v[l, start - 1] - v[l, start])
            for at in range(start, stop):
                here = v[l, at]
                flow = weight[0, at] * (here - v[l, at + 1])
                flow_z = weight[1, at] * (here - up(here, 0))
                flow_y = weight[2, at] * (here - up(here, 1))
                result = flow - flow_before + (flow_z - down(flow_z, 0)) + (flow_y - down(flow_y, 1))
                yield at, here, free[at] * result
                flow_before = flow

        for at, here, result in operate(v0, 1, rows_x + 2 * HALO - 1):
            v1[l, at] = result * (1.0 / SPREAD) - here
        for at, here, result in operate(v1, 2, rows_x + 2 * HALO - 2):
            v2[l, at] = result * (2.0 / SPREAD) - 2.0 * here - v0[l, at]
        sums = [jnp.zeros((TILE, LANES), F32)] * 6
        for at, here, result in operate(v2, HALO, HALO + rows_x):
            a, b = v0[l, at], v1[l, at]
            for n, product in enumerate((a * a, a * b, b * b, b * here, here * here, here * result)):
                for t in range(rows_z // TILE):
                    sums[n] = sums[n] + product[tile_rows(t)]
        for n in range(6):
            dots[pl.ds(n * labels + l, 1), :] = jnp.sum(sums[n], axis=0, keepdims=True)
        return carry

    lax.fori_loop(0, labels, label, 0)
    total = jnp.sum(dots[...], axis=1, keepdims=True)
    tile = jnp.zeros((TILE, LANES), F32)
    for n in range(6):
        column = total[tile_rows(n // 2)]
        column = jnp.broadcast_to(column, (TILE, LANES))
        tile = jnp.where(lanes_iota() == n, pltpu.roll(column, 4, 0) if n % 2 else column, tile)
    for n in range(dots_out.shape[0]):
        dots_out[n] = tile


def steps(g00, g01, g11, g12, g22, k22):
    g02 = 2.0 * g11 - g00
    k00 = SPREAD * (g00 + g01)
    k01 = SPREAD * (g01 + g11)
    k02 = SPREAD * (g02 + g12)
    k11 = SPREAD * (g11 + 0.5 * (g12 + g01))
    k12 = SPREAD * (g12 + 0.5 * (g22 + g02))
    alpha = g00 / k00
    c0 = alpha
    r0 = 1.0 - alpha * SPREAD
    r1 = -alpha * SPREAD
    rr = r0 * r0 * g00 + 2.0 * r0 * r1 * g01 + r1 * r1 * g11
    beta = rr / g00
    p0, p1 = r0 + beta, r1
    alpha = rr / (p0 * p0 * k00 + 2.0 * p0 * p1 * k01 + p1 * p1 * k11)
    c0, c1 = c0 + alpha * p0, alpha * p1
    r0 = r0 - alpha * SPREAD * (p0 + 0.5 * p1)
    r1 = r1 - alpha * SPREAD * (p0 + p1)
    r2 = -alpha * SPREAD * 0.5 * p1
    rr_next = r0 * r0 * g00 + r1 * r1 * g11 + r2 * r2 * g22
    rr_next = rr_next + 2.0 * (r0 * r1 * g01 + r0 * r2 * g02 + r1 * r2 * g12)
    beta = rr_next / rr
    p0, p1, p2 = r0 + beta * p0, r1 + beta * p1, r2
    curve = p0 * p0 * k00 + p1 * p1 * k11 + p2 * p2 * k22
    curve = curve + 2.0 * (p0 * p1 * k01 + p0 * p2 * k02 + p1 * p2 * k12)
    alpha = rr_next / curve
    return c0 + alpha * p0, c1 + alpha * p1, alpha * p2


def edges(colours, two, info, parts, v0, v1, v2, planted, likelihoods, first, second, *refs):
    faces, edges_a, edges_b = refs[: 1 + two], refs[1 + two : 2 + 2 * two], refs[2 + 2 * two : 3 + 3 * two]
    out, lam, field = refs[3 + 3 * two :]
    labels, rows_x, rows_z, _ = likelihoods.shape
    rows = rows_z + TILE
    even = info[EVEN_X] == 1
    total = jnp.sum(parts[...], axis=0)
    grams = [jnp.broadcast_to(total[:, n : n + 1], (TILE, LANES)) for n in range(6)]
    c0, c1, c2 = steps(*grams)
    for l in range(labels):
        s0, s1, s2 = (jnp.broadcast_to(c[l : l + 1], (rows, LANES)) for c in (c0, c1, c2))
        for at in range(rows_x + 3):
            source = at + HALO - 1
            lam[l, at] = s0 * v0[l, source] + s1 * v1[l, source] + s2 * v2[l, source]
            x = at - 1
            source = x % rows_x
            if 0 <= x < rows_x:
                member = jnp.where(planted[x] == info[COLOUR] + l, 1.0, 0.0)
                plane = jnp.where(planted[x] >= colours, likelihoods[l, x], member)
                plane = jnp.concatenate([plane, full_tile(*ends_z(info, faces, x, l))], axis=0)
            else:
                index = 2 * labels + labels * rows_x + 2 * l + (1 if x < 0 else source)
                received = [
                    jnp.concatenate([ref[index].astype(F32), full_tile(*ends_z(info, tiles, source, l))], axis=0)
                    for ref, tiles in ((first, edges_a), (second, edges_b))
                ]
                above, below = sides(even, *received)
                plane = below if x < 0 else above
            field[l, at] = plane
    for at in range(rows_x + 2):
        sums = [jnp.zeros((rows, LANES), F32)] * 3
        for l in range(labels):
            a, b = lam[l, at], field[l, at]
            sums[0] = sums[0] - (a - lam[l, at + 1]) * (b - field[l, at + 1])
            sums[1] = sums[1] - (a - up(a, 0)) * (b - up(b, 0))
            sums[2] = sums[2] - (a - up(a, 1)) * (b - up(b, 1))
        for d in range(3):
            out[d, at] = sums[d]


def filter_sums(info, edge, other, slope, stack, grads, out, products, rows_out):
    rows_x = edge.shape[1] - 2
    lane = lanes_iota(edge.shape[2])
    for xp in range(rows_x + 2):
        shifted = [[], [], []]
        for d in range(3):
            plane = ((edge[d, xp] + other[d, xp]) * slope[d, xp]).astype(BF16).astype(F32)
            shifted[0].append(jnp.where(lane < LANES - 1, up(plane, 1), 0.0))
            shifted[1].append(plane)
            shifted[2].append(jnp.where(lane > 0, down(plane, 1), 0.0))
        planes = shifted[0] + shifted[1] + shifted[2]
        planes += [jnp.zeros_like(planes[0])] * 7
        for pair in range(8):
            at = (xp * 16 + 2 * pair) * TILE
            for t in range(-1, 5):
                both = jnp.concatenate([plane[tile_rows(t)] for plane in planes[2 * pair : 2 * pair + 2]], axis=0)
                grads[at : at + 16, (t + 1) * LANES : (t + 2) * LANES] = both.astype(BF16)
    own = grads[LANES : LANES * (rows_x + 1), LANES : 5 * LANES]
    for o in range(3):
        products[o] = lax.dot_general(
            own, stack[:, o * LANES : (o + 4) * LANES], (((1,), (1,)), ((), ())), preferred_element_type=F32
        )
    rows_out[...] = jnp.zeros_like(rows_out)
    masks = {(h, j, o): band(h, j, o) for o in (-1, 0, 1) for h in range(2) for j in bands(o)}
    for kd in range(9):
        k, d = kd // 3, kd % 3
        for i in range(3):
            for j in range(3):
                total = jnp.zeros((TILE, LANES), F32)
                for o in (-1, 0, 1):
                    if j in bands(o):
                        for x in range(rows_x):
                            at = (x * 16 + kd) * TILE
                            col = (x + i) // 2 * LANES
                            piece = products[o + 1, at : at + TILE, col : col + LANES]
                            total = total + jnp.where(masks[(x + i) % 2, j, o], piece, 0.0)
                row = d * 27 + i * 9 + j * 3 + k
                rows_out[row : row + 1] = jnp.sum(total, axis=0, keepdims=True)
    sums = lax.dot_general(
        jnp.where(((lanes_iota() >> 3) & 7) == rows_iota(), 1.0, 0.0),
        rows_out[...],
        (((1,), (1,)), ((), ())),
        precision=lax.Precision.HIGHEST,
        preferred_element_type=F32,
    )
    for n in range(out.shape[0]):
        out[n] = sums


def image_sums(info, grads, matrix, out, sums):
    total = jnp.dot(matrix[0], grads[:, 0:512], preferred_element_type=F32)
    total = total + jnp.dot(matrix[1], grads[:, 128:640], preferred_element_type=F32)
    sums[...] = total + jnp.dot(matrix[2], grads[:, 256:768], preferred_element_type=F32)
    channels, rows_x, rows_z, _ = out.shape
    for c in range(channels):
        for x in range(rows_x):
            at = (c * rows_x + x) * TILE
            for t in range(0, rows_z // TILE, 2):
                both = [sums[at : at + TILE, s * LANES : (s + 1) * LANES] for s in (t, t + 1)]
                out[c, x, t * TILE : (t + 2) * TILE] = jnp.concatenate(both, axis=0).astype(BF16)


def local(image, filt, planted, likelihoods, slope):
    channels = image.shape[0]
    labels, rows_x, rows_z, rows_y = likelihoods.shape
    if (channels, labels, rows_x, rows_z, rows_y) != (8, 4, HALO, 4 * TILE, LANES):
        raise ValueError("brick size")
    lab, xy, gz = lax.axis_index("lab"), lax.axis_index("xy"), lax.axis_index("gz")
    colours = labels * lax.axis_size("lab")
    size_x, size_z = rows_x * lax.axis_size("xy"), rows_z * lax.axis_size("gz")
    rows = rows_z + TILE
    two = lax.axis_size("gz") > 2
    phases = range(1 + two)
    members = lax.axis_size("xy") * lax.axis_size("gz")
    info = jnp.stack(
        [
            1 - xy % 2,
            1 - gz % 2,
            xy * rows_x,
            gz * rows_z,
            lab * labels,
            1 - (xy + lab) % 2,
            jnp.minimum(xy, 1),
            jnp.minimum(lax.axis_size("xy") - 1 - xy, 1),
            jnp.minimum(gz, 1),
            jnp.minimum(lax.axis_size("gz") - 1 - gz, 1),
        ]
    ).astype(jnp.int32)

    inputs = (image, planted, likelihoods, slope)
    planes = channels + labels * rows_x + 2 * labels
    brick = shaped((planes, rows_z, LANES), BF16)
    taps = jnp.transpose(filt, (0, 2, 3, 4, 1))
    matrix, back_matrix, image, planted, likelihoods, slope, *packed = call(
        functools.partial(pack, colours, two),
        [shaped((3, 288, 384), BF16), shaped((3, 256, 768), BF16)]
        + [shaped(a.shape, a.dtype) for a in inputs]
        + [shaped((rows_x, labels, TILE, LANES), BF16)] * (1 + two)
        + [brick, brick],
        info,
        *(pltpu.with_memory_space_constraint(a, pltpu.HBM) for a in (taps, *inputs)),
        scratch=[
            pltpu.VMEM(taps.shape, BF16),
            pltpu.VMEM((112, LANES), F32),
            pltpu.SemaphoreType.DMA((5,)),
        ],
        name="pack",
        space=pltpu.HBM,
    )
    send_a, send_b = packed[1 + two :]
    faces = [swap(packed[phase], "gz", phase, True) for phase in phases]
    edges_a = [diagonal_swap(packed[phase], 0, phase) for phase in phases]
    edges_b = [diagonal_swap(packed[phase], 1, phase) for phase in phases]
    second = swap(send_b, "xy", 1)
    first = swap(send_a, "xy", 0)
    received = (first, second, *faces, *edges_a, *edges_b)

    part, stack = call(
        functools.partial(convolve, two),
        [shaped((3, rows_x, rows_z, LANES), F32), shaped((384, 768), BF16)],
        info,
        image,
        *received,
        matrix,
        scratch=[pltpu.VMEM((288, 512), F32)],
        name="convolve",
    )
    logits, own, *sends = call(
        functools.partial(add_parts, two),
        [shaped(part.shape, F32), shaped(part.shape, BF16)]
        + [shaped((3, rows_x, TILE, LANES), BF16)] * (1 + two),
        info,
        part,
        lab_swap(part),
        name="add_parts",
    )
    mine = split_swap(own)
    mine_edges = [split_diagonal_swap(sends[phase], phase) for phase in phases]
    logit_faces = [swap(sends[phase], "gz", phase, True) for phase in phases]
    mine, mine_edges, logit_faces = lax.optimization_barrier((mine, mine_edges, logit_faces))
    other = lab_swap(mine)
    other_edges = [lab_swap(block) for block in mine_edges]
    extended = (labels, rows_x + 2 * HALO, rows, LANES)
    ring = shaped((3, rows_x + 2, rows, LANES), F32)
    v0, v1, v2, squash_slope, dots = call(
        functools.partial(krylov, colours, size_x, size_z, two),
        [shaped(extended, F32)] * 3 + [ring, shaped((members, TILE, LANES), F32)],
        info,
        planted,
        slope,
        logits,
        mine,
        other,
        first,
        second,
        *logit_faces,
        *mine_edges,
        *other_edges,
        *faces,
        *edges_a,
        *edges_b,
        scratch=[
            pltpu.VMEM((3,) + extended[1:], F32),
            pltpu.VMEM(extended[1:], F32),
            pltpu.VMEM((6 * labels, LANES), F32),
        ],
        name="krylov",
    )
    edge = call(
        functools.partial(edges, colours, two),
        ring,
        info,
        everyones(dots, ("xy", "gz")),
        v0,
        v1,
        v2,
        planted,
        likelihoods,
        *received,
        scratch=[pltpu.VMEM((labels, rows_x + 3, rows, LANES), F32)] * 2,
        name="edges",
    )
    grads, sums = call(
        filter_sums,
        [shaped((768, 768), BF16), shaped((members, TILE, LANES), F32)],
        info,
        edge,
        lab_swap(edge),
        squash_slope,
        stack,
        scratch=[pltpu.VMEM((3, 512, 384), F32), pltpu.VMEM((LANES, LANES), F32)],
        name="filter_sums",
    )
    grad_image = call(
        image_sums,
        shaped(image.shape, BF16),
        info,
        grads,
        back_matrix,
        scratch=[pltpu.VMEM((256, 512), F32)],
        flops=10_000_000,
        name="image_sums",
    )
    grad_filter = jnp.sum(everyones(sums, ("xy", "gz")), axis=0)
    grad_filter = grad_filter[:, :81].reshape(channels, 3, 27)
    return grad_image, jnp.transpose(grad_filter, (1, 0, 2)).reshape(3, channels, 3, 3, 3)


def solution(mesh):
    return jax.shard_map(
        local,
        mesh=mesh,
        in_specs=(
            P("lab", ("crops", "xy"), "gz", None),
            P(),
            P(("crops", "xy"), "gz", None),
            P("lab", ("crops", "xy"), "gz", None),
            P("lab", ("crops", "xy"), "gz", None),
        ),
        out_specs=(P("lab", ("crops", "xy"), "gz", None), P("crops", "lab", None, None, None)),
        check_vma=False,
    )
```

```python
import functools

import jax
import jax.numpy as jnp
from jax import lax
from jax.experimental import pallas as pl
from jax.experimental.pallas import tpu as pltpu
from jax.sharding import PartitionSpec as P

HALO = 4
SEED = 64.0
SPREAD = 6.3
TILE = 8
LANES = 128
BF16, F32 = jnp.bfloat16, jnp.float32
EVEN_X, EVEN_Z, FIRST_X, FIRST_Z, COLOUR, UP, PREV_X, NEXT_X, PREV_Z, NEXT_Z = range(10)


def pair_routes(count, phase, closed=False):
    route = []
    for low in range(phase, count - 1, 2):
        route += [(low, low + 1), (low + 1, low)]
    if closed and phase == 1 and count % 2 == 0:
        route += [(count - 1, 0), (0, count - 1)]
    return route


def swap(block, axis, phase, closed=False):
    return lax.ppermute(block, axis, pair_routes(lax.axis_size(axis), phase, closed))


def lab_swap(block):
    return lax.ppermute(block, "lab", [(0, 1), (1, 0)])


def diagonal_swap(block, x_phase, z_phase):
    along_x = pair_routes(lax.axis_size("xy"), x_phase, True)
    along_z = pair_routes(lax.axis_size("gz"), z_phase, True)
    count = lax.axis_size("gz")
    route = [(sx * count + sz, dx * count + dz) for sx, dx in along_x for sz, dz in along_z]
    return lax.ppermute(block, ("xy", "gz"), route)


def split_swap(block):
    labs = lax.axis_size("lab")
    route = [
        (src * labs + lab, dst * labs + lab)
        for lab in range(labs)
        for src, dst in pair_routes(lax.axis_size("xy"), lab % 2, True)
    ]
    return lax.ppermute(block, ("xy", "lab"), route)


def split_diagonal_swap(block, z_phase):
    labs, count = lax.axis_size("lab"), lax.axis_size("gz")
    route = [
        ((sx * count + sz) * labs + lab, (dx * count + dz) * labs + lab)
        for lab in range(labs)
        for sx, dx in pair_routes(lax.axis_size("xy"), lab % 2, True)
        for sz, dz in pair_routes(count, z_phase, True)
    ]
    return lax.ppermute(block, ("xy", "gz", "lab"), route)


def everyones(copies, axes):
    return lax.all_to_all(copies, axes, 0, 0)


def call(kernel, outs, *ins, scratch=(), flops=1_000_000, name=None, space=pltpu.VMEM):
    specs = [pl.BlockSpec(memory_space=pltpu.SMEM)]
    specs += [pl.BlockSpec(memory_space=space)] * (len(ins) - 1)
    bytes_moved = sum(a.size * a.dtype.itemsize for a in ins)
    return pl.pallas_call(
        kernel,
        out_shape=outs,
        in_specs=specs,
        out_specs=jax.tree.map(lambda _: pl.BlockSpec(memory_space=pltpu.VMEM), outs),
        scratch_shapes=list(scratch),
        compiler_params=pltpu.CompilerParams(vmem_limit_bytes=40 * 2**20),
        cost_estimate=pl.CostEstimate(flops=flops, bytes_accessed=bytes_moved, transcendentals=0),
        name=name,
    )(*ins)


def shaped(shape, dtype):
    return jax.ShapeDtypeStruct(shape, dtype)


def rows_iota(rows=TILE):
    return lax.broadcasted_iota(jnp.int32, (rows, LANES), 0)


def lanes_iota(rows=TILE):
    return lax.broadcasted_iota(jnp.int32, (rows, LANES), 1)


def fields(planted, likelihood, slope, colours, colour):
    free = planted >= colours
    member = jnp.where(planted == colour, 1.0, 0.0)
    return jnp.where(free, slope, SEED), jnp.where(free, likelihood, member)


def pack(
    colours,
    two,
    info,
    filt_in,
    image_in,
    planted_in,
    likelihoods_in,
    slope_in,
    wide_out,
    back_out,
    image,
    planted,
    likelihoods,
    slope,
    *refs,
):
    faces, (send_a, send_b, filt, taps, sems) = refs[: 1 + two], refs[1 + two :]
    pairs = (
        (planted_in, planted),
        (slope_in, slope),
        (likelihoods_in, likelihoods),
        (image_in, image),
        (filt_in, filt),
    )
    copies = [pltpu.make_async_copy(src, dst, sems.at[n]) for n, (src, dst) in enumerate(pairs)]
    for copy in reversed(copies):
        copy.start()
    copies[4].wait()
    spread_filter(info, filt, taps, wide_out, back_out)
    labels, rows_x, rows_z, _ = likelihoods.shape
    channels = image.shape[0]
    last, first = slice(rows_z - TILE, rows_z), slice(0, TILE)
    even = info[EVEN_X] == 1
    high, low = jnp.where(even, rows_x - 1, 0), jnp.where(even, 0, rows_x - 1)
    copies[0].wait()
    copies[1].wait()
    for x in range(rows_x):
        for l in range(labels):
            rhs = jnp.where(planted[x] >= colours, slope[l, x], SEED).astype(BF16)
            send_a[channels + l * rows_x + x] = rhs
            send_b[channels + l * rows_x + x] = rhs
    copies[2].wait()
    for l in range(labels):
        for send, at in ((send_a, high), (send_b, low)):
            for r in range(2):
                x = jnp.where(at == 0, 0, rows_x - 2) + r
                _, full = fields(planted[x], likelihoods[l, x], slope[l, x], colours, info[COLOUR] + l)
                send[channels + labels * rows_x + 2 * l + r] = full.astype(BF16)
    copies[3].wait()
    for c in range(channels):
        send_a[c] = image[c, high]
        send_b[c] = image[c, low]
    for phase, out in enumerate(faces):
        even = info[EVEN_Z] != phase
        place = (rows_iota() + jnp.where(even, 0, 4)) & 7

        def channel(c, x):
            return jnp.where(even, image[c, x, last].astype(F32), image[c, x, first].astype(F32))

        def turned(tile, for_even, for_odd):
            return jnp.where(even, pltpu.roll(tile, for_even, 0), pltpu.roll(tile, for_odd, 0))

        for x in range(rows_x):
            seeds = jnp.where(even, planted[x, last], planted[x, first])
            for l in range(labels):
                ends = [jnp.where(even, ref[l, x, last], ref[l, x, first]) for ref in (likelihoods, slope)]
                rhs, full = fields(seeds, *ends, colours, info[COLOUR] + l)
                first_channel = turned(channel(2 * l, x), 3, 6)
                second_channel = turned(channel(2 * l + 1, x), 4, 7)
                rest = jnp.where(place == 2, first_channel, second_channel)
                rest = jnp.where(place < 2, turned(full, 2, 4), rest)
                out[x, l] = jnp.where(place >= 4, rhs, rest).astype(BF16)


def sides(even, first, second):
    if second is None:
        return jnp.where(even, first, 0.0), jnp.where(even, 0.0, first)
    return jnp.where(even, first, second), jnp.where(even, second, first)


def ends_z(info, tiles, x, l):
    both = [ref[x, l].astype(F32) for ref in tiles]
    return sides(info[EVEN_Z] == 1, both[0], both[1] if len(both) > 1 else None)


def rhs_tile(above, below):
    return jnp.where(rows_iota() < 4, above, below)


def full_tile(above, below):
    return jnp.where(rows_iota() < 4, pltpu.roll(above, 4, 0), pltpu.roll(below, 6, 0))


def image_tile(info, above, below, c):
    up, down = (2, 5) if c % 2 == 0 else (1, 4)
    above = jnp.where(info[NEXT_Z] == 1, above, 0.0)
    below = jnp.where(info[PREV_Z] == 1, below, 0.0)
    return jnp.where(rows_iota() < 4, pltpu.roll(above, up, 0), pltpu.roll(below, down, 0))


def band(half, j, o, transposed=False):
    z, lane = rows_iota(), lanes_iota()
    other = lane & 7
    at = (z + 1 - other - 8 * o) if transposed else (other + 8 * o - z + 1)
    mask = at == j
    if half is not None:
        mask = mask & ((lane >> 6) == half)
    return mask


def bands(o, transposed=False):
    if o == 0:
        return (0, 1, 2)
    return (0,) if (o < 0) != transposed else (2,)


def spread_filter(info, filt, taps, wide_out, back_out):
    taps[...] = jnp.zeros_like(taps)
    for d in range(3):
        for i in range(3):
            for j in range(3):
                at = (d * 9 + i * 3 + j) * 4
                taps[at : at + 3, : filt.shape[-1]] = filt[d, i, j].astype(F32)
    lane = lanes_iota(LANES)
    channel = rows_iota(LANES) - 2 * info[COLOUR]
    all_taps = taps[...].astype(BF16)
    by_channel = jnp.where(channel == ((lane >> 3) & 7), 1.0, 0.0).astype(BF16)
    own = jnp.dot(
        all_taps, jnp.where(channel == lane, 1.0, 0.0).astype(BF16), preferred_element_type=F32
    ).astype(BF16)
    wide = jnp.dot(all_taps, by_channel, preferred_element_type=F32)
    tap, edge = rows_iota(taps.shape[0]), lanes_iota(taps.shape[0]) >> 3
    shift = jnp.where(edge >= 3, 1, 0) + jnp.where(edge >= 6, 1, 0)
    first_tap = jnp.where(edge < 9, (edge - 3 * shift) * 36 + shift, -LANES)
    places = [jnp.where(tap == first_tap + 4 * ij, 1.0, 0.0).astype(BF16) for ij in range(9)]
    back = [
        lax.dot_general(own, place, (((0,), (0,)), ((), ())), preferred_element_type=F32) for place in places
    ]
    zero = jnp.zeros((TILE, LANES), F32)
    for at_out, distances in enumerate(((0,), (-1, 1))):
        cases = [(o, j) for o in distances for j in bands(o)]
        masks = {(h, j): band(h, j, o) for h in range(2) for o, j in cases}
        for kd in range(9):
            for pair in range(2):
                for block in range(3):
                    tiles = []
                    for x in (2 * pair, 2 * pair + 1):
                        tile = zero
                        for i in range(3):
                            if (x + i) // 2 == block:
                                for _, j in cases:
                                    row = (kd % 3 * 9 + i * 3 + j) * 4 + kd // 3
                                    value = jnp.broadcast_to(wide[row : row + 1], (TILE, LANES))
                                    tile = jnp.where(masks[(x + i) % 2, j], value, tile)
                        tiles.append(tile)
                    at = (kd * 4 + 2 * pair) * TILE
                    wide_out[at_out, at : at + 16, block * LANES : (block + 1) * LANES] = jnp.concatenate(
                        tiles, axis=0
                    ).astype(BF16)
        cases = [(o, j) for o in distances for j in bands(o, True)]
        masks = {j: band(None, j, o, True) for o, j in cases}
        for c in range(8):
            for pair in range(2):
                for block in range(6):
                    tiles = []
                    for x in (2 * pair, 2 * pair + 1):
                        tile = zero
                        i = x + 2 - block
                        if 0 <= i < 3:
                            for _, j in cases:
                                value = jnp.broadcast_to(back[i * 3 + j][c : c + 1], (TILE, LANES))
                                tile = jnp.where(masks[j], value, tile)
                        tiles.append(tile)
                    at = (c * 4 + 2 * pair) * TILE
                    back_out[at_out, at : at + 16, block * LANES : (block + 1) * LANES] = jnp.concatenate(
                        tiles, axis=0
                    ).astype(BF16)


def store_tiles(out, at, planes):
    for t in range(4):
        both = jnp.concatenate([plane[tile_rows(t)] for plane in planes], axis=0)
        out[at : at + 16, t * LANES : (t + 1) * LANES] = both.astype(BF16)
        both = [jnp.where(rows_iota() < 4, plane[tile_rows(t + 1)], plane[tile_rows(t - 1)]) for plane in planes]
        both = jnp.concatenate(both, axis=0)
        out[at : at + 16, (t + 4) * LANES : (t + 5) * LANES] = both.astype(BF16)


def tile_rows(t):
    at = (4 if t < 0 else t) * TILE
    return slice(at, at + TILE)


def convolve(two, info, image, first, second, *refs):
    faces, edges_a, edges_b = refs[: 1 + two], refs[1 + two : 2 + 2 * two], refs[2 + 2 * two : 3 + 3 * two]
    matrix, part, stack, sums = refs[3 + 3 * two :]
    channels, rows_x = image.shape[0], image.shape[1]
    even = info[EVEN_X] == 1
    for xp in range(rows_x + 2):
        for c in range(0, channels, 2):
            planes = []
            if 0 < xp <= rows_x:
                ends = [ends_z(info, faces, xp - 1, c // 2)]
            else:
                ends = [ends_z(info, tiles, rows_x - 1 if xp == 0 else 0, c // 2) for tiles in (edges_a, edges_b)]
            for ch in (c, c + 1):
                tiles = [image_tile(info, *pair, ch) for pair in ends]
                if 0 < xp <= rows_x:
                    planes.append(jnp.concatenate([image[ch, xp - 1].astype(F32), tiles[0]], axis=0))
                else:
                    received = [
                        jnp.concatenate([ref[ch].astype(F32), tile], axis=0)
                        for ref, tile in zip((first, second), tiles)
                    ]
                    above, below = sides(even, *received)
                    plane, exists = (below, PREV_X) if xp == 0 else (above, NEXT_X)
                    planes.append(jnp.where(info[exists] == 1, plane, 0.0))
            at = (xp * channels + c) * TILE
            store_tiles(stack, at, planes)
    total = jnp.dot(matrix[0], stack[:, :512], preferred_element_type=F32)
    sums[...] = total + jnp.dot(matrix[1], stack[:, 512:], preferred_element_type=F32)
    lane = lanes_iota()
    for d in range(3):
        for x in range(rows_x):
            for t in range(4):
                cols = slice(t * LANES, (t + 1) * LANES)

                def piece(k):
                    at = ((k * 3 + d) * rows_x + x) * TILE
                    return sums[at : at + TILE, cols]

                before = jnp.where(lane > 0, pltpu.roll(piece(0), 1, 1), 0.0)
                after = jnp.where(lane < LANES - 1, pltpu.roll(piece(2), LANES - 1, 1), 0.0)
                part[d, x, tile_rows(t)] = piece(1) + before + after


def add_parts(two, info, part, other, logits, brick, *faces):
    rows_x, rows_z = part.shape[1], part.shape[2]
    for d in range(3):
        for x in range(rows_x):
            total = part[d, x] + other[d, x]
            logits[d, x] = total
            brick[d, x] = total.astype(BF16)
            for phase, face in enumerate(faces):
                even = info[EVEN_Z] != phase
                face[d, x] = jnp.where(even, total[rows_z - TILE :], total[:TILE]).astype(BF16)


def up(plane, dim):
    return pltpu.roll(plane, plane.shape[dim] - 1, dim)


def down(plane, dim):
    return pltpu.roll(plane, 1, dim)


def prepare(colours, two, info, planted, slope, likelihoods, first, second, *refs):
    faces, edges_a, edges_b = refs[: 1 + two], refs[1 + two : 2 + 2 * two], refs[2 + 2 * two : 3 + 3 * two]
    v0, free, field = refs[3 + 3 * two :]
    labels, rows_x, _, _ = slope.shape
    channels = 2 * labels
    even = info[EVEN_X] == 1

    def grown(index, source, l, tile):
        received = [
            jnp.concatenate([ref[index].astype(F32), tile(*ends_z(info, tiles, source, l))], axis=0)
            for ref, tiles in ((first, edges_a), (second, edges_b))
        ]
        return sides(even, *received)

    for x in range(rows_x):
        for l in range(labels):
            ends = ends_z(info, faces, x, l)
            rhs, full = fields(planted[x], likelihoods[l, x], slope[l, x], colours, info[COLOUR] + l)
            rhs = jnp.concatenate([rhs, rhs_tile(*ends)], axis=0)
            field[l, x + 1] = jnp.concatenate([full, full_tile(*ends)], axis=0)
            above, below = grown(channels + l * rows_x + x, x, l, rhs_tile)
            for at, plane in ((x + HALO, rhs), (x, below), (x + HALO + rows_x, above)):
                open_cell = plane < SEED / 2
                v0[l, at] = jnp.where(open_cell, plane, 0.0)
                if l == 0:
                    free[at] = jnp.where(open_cell, 1.0, 0.0)
    for l in range(labels):
        base = 2 * labels + labels * rows_x + 2 * l
        field[l, 0] = grown(base + 1, rows_x - 1, l, full_tile)[1]
        for r in range(2):
            field[l, rows_x + 1 + r] = grown(base + r, r, l, full_tile)[0]


def krylov(size_x, size_z, two, info, v0, free, logits, mine, other, *refs):
    faces, mine_edges, other_edges = (refs[n * (1 + two) : (n + 1) * (1 + two)] for n in range(3))
    v1, v2, slope_out, dots_out, weight, dots = refs[3 * (1 + two) :]
    labels, _, rows, _ = v0.shape
    rows_x, rows_z = logits.shape[1:3]
    is_up = info[UP] == 1
    z = rows_iota(rows)
    z = info[FIRST_Z] + jnp.where(z < rows_z + HALO, z, z - rows)
    inside_z = (z >= 0) & (z < size_z)
    in_z = jnp.where(inside_z, 1.0, 0.0)
    next_z = jnp.where(inside_z & (z < size_z - 1), 1.0, 0.0)
    in_zy = jnp.where(lanes_iota(rows) < LANES - 1, in_z, 0.0)
    for at in range(rows_x + 2 * HALO):
        x = at - HALO
        place = info[FIRST_X] + x
        inside = (place >= 0) & (place < size_x)
        in_x = jnp.where(inside, 1.0, 0.0)
        next_x = jnp.where(inside & (place < size_x - 1), 1.0, 0.0)
        for d in range(3):
            def grown(plane, tiles, source):
                return jnp.concatenate([plane, rhs_tile(*ends_z(info, tiles, d, source))], axis=0)

            if 0 <= x < rows_x:
                plane = grown(logits[d, x], faces, x)
            else:
                source = x % rows_x
                here = grown(mine[d, source].astype(F32), mine_edges, source)
                there = grown(other[d, source].astype(F32), other_edges, source)
                plane = jnp.where(is_up, there, here) if x < 0 else jnp.where(is_up, here, there)
            squashed = 1.0 / (1.0 + jnp.exp(-plane))
            valid = (in_z * next_x, next_z * in_x, in_zy * in_x)[d]
            weight[d, at] = (0.05 + squashed) * valid
            if -1 <= x <= rows_x:
                slope_out[d, x + 1] = squashed * (1.0 - squashed) * valid

    def label(l, carry):
        def operate(v, start, stop):
            flow_before = weight[0, start - 1] * (v[l, start - 1] - v[l, start])
            for at in range(start, stop):
                here = v[l, at]
                flow = weight[0, at] * (here - v[l, at + 1])
                flow_z = weight[1, at] * (here - up(here, 0))
                flow_y = weight[2, at] * (here - up(here, 1))
                result = flow - flow_before + (flow_z - down(flow_z, 0)) + (flow_y - down(flow_y, 1))
                yield at, here, free[at] * result
                flow_before = flow

        for at, here, result in operate(v0, 1, rows_x + 2 * HALO - 1):
            v1[l, at] = result * (1.0 / SPREAD) - here
        for at, here, result in operate(v1, 2, rows_x + 2 * HALO - 2):
            v2[l, at] = result * (2.0 / SPREAD) - 2.0 * here - v0[l, at]
        sums = [jnp.zeros((TILE, LANES), F32)] * 6
        for at, here, result in operate(v2, HALO, HALO + rows_x):
            a, b = v0[l, at], v1[l, at]
            for n, product in enumerate((a * a, a * b, b * b, b * here, here * here, here * result)):
                for t in range(rows_z // TILE):
                    sums[n] = sums[n] + product[tile_rows(t)]
        for n in range(6):
            dots[pl.ds(n * labels + l, 1), :] = jnp.sum(sums[n], axis=0, keepdims=True)
        return carry

    lax.fori_loop(0, labels, label, 0)
    total = jnp.sum(dots[...], axis=1, keepdims=True)
    tile = jnp.zeros((TILE, LANES), F32)
    for n in range(6):
        column = total[tile_rows(n // 2)]
        column = jnp.broadcast_to(column, (TILE, LANES))
        tile = jnp.where(lanes_iota() == n, pltpu.roll(column, 4, 0) if n % 2 else column, tile)
    for n in range(dots_out.shape[0]):
        dots_out[n] = tile


def steps(g00, g01, g11, g12, g22, k22):
    g02 = 2.0 * g11 - g00
    k00 = SPREAD * (g00 + g01)
    k01 = SPREAD * (g01 + g11)
    k02 = SPREAD * (g02 + g12)
    k11 = SPREAD * (g11 + 0.5 * (g12 + g01))
    k12 = SPREAD * (g12 + 0.5 * (g22 + g02))
    alpha = g00 / k00
    c0 = alpha
    r0 = 1.0 - alpha * SPREAD
    r1 = -alpha * SPREAD
    rr = r0 * r0 * g00 + 2.0 * r0 * r1 * g01 + r1 * r1 * g11
    beta = rr / g00
    p0, p1 = r0 + beta, r1
    alpha = rr / (p0 * p0 * k00 + 2.0 * p0 * p1 * k01 + p1 * p1 * k11)
    c0, c1 = c0 + alpha * p0, alpha * p1
    r0 = r0 - alpha * SPREAD * (p0 + 0.5 * p1)
    r1 = r1 - alpha * SPREAD * (p0 + p1)
    r2 = -alpha * SPREAD * 0.5 * p1
    rr_next = r0 * r0 * g00 + r1 * r1 * g11 + r2 * r2 * g22
    rr_next = rr_next + 2.0 * (r0 * r1 * g01 + r0 * r2 * g02 + r1 * r2 * g12)
    beta = rr_next / rr
    p0, p1, p2 = r0 + beta * p0, r1 + beta * p1, r2
    curve = p0 * p0 * k00 + p1 * p1 * k11 + p2 * p2 * k22
    curve = curve + 2.0 * (p0 * p1 * k01 + p0 * p2 * k02 + p1 * p2 * k12)
    alpha = rr_next / curve
    return c0 + alpha * p0, c1 + alpha * p1, alpha * p2


def edges(info, parts, v0, v1, v2, field, out, lam):
    labels, _, rows, _ = v0.shape
    rows_x = out.shape[1] - 2
    total = jnp.sum(parts[...], axis=0)
    grams = [jnp.broadcast_to(total[:, n : n + 1], (TILE, LANES)) for n in range(6)]
    c0, c1, c2 = steps(*grams)
    for l in range(labels):
        s0, s1, s2 = (jnp.broadcast_to(c[l : l + 1], (rows, LANES)) for c in (c0, c1, c2))
        for at in range(rows_x + 3):
            source = at + HALO - 1
            lam[l, at] = s0 * v0[l, source] + s1 * v1[l, source] + s2 * v2[l, source]
    for at in range(rows_x + 2):
        sums = [jnp.zeros((rows, LANES), F32)] * 3
        for l in range(labels):
            a, b = lam[l, at], field[l, at]
            sums[0] = sums[0] - (a - lam[l, at + 1]) * (b - field[l, at + 1])
            sums[1] = sums[1] - (a - up(a, 0)) * (b - up(b, 0))
            sums[2] = sums[2] - (a - up(a, 1)) * (b - up(b, 1))
        for d in range(3):
            out[d, at] = sums[d]


def filter_sums(info, edge, other, slope, stack, grads, out, products, rows_out):
    rows_x = edge.shape[1] - 2
    lane = lanes_iota(edge.shape[2])
    for xp in range(rows_x + 2):
        shifted = [[], [], []]
        for d in range(3):
            plane = ((edge[d, xp] + other[d, xp]) * slope[d, xp]).astype(BF16).astype(F32)
            shifted[0].append(jnp.where(lane < LANES - 1, up(plane, 1), 0.0))
            shifted[1].append(plane)
            shifted[2].append(jnp.where(lane > 0, down(plane, 1), 0.0))
        planes = shifted[0] + shifted[1] + shifted[2]
        planes += [jnp.zeros_like(planes[0])] * 7
        for pair in range(8):
            at = (xp * 16 + 2 * pair) * TILE
            store_tiles(grads, at, planes[2 * pair : 2 * pair + 2])
    own = grads[LANES : LANES * (rows_x + 1), : 4 * LANES]
    for n in range(2):
        products[n] = lax.dot_general(
            own, stack[:, 512 * n : 512 * (n + 1)], (((1,), (1,)), ((), ())), preferred_element_type=F32
        )
    rows_out[...] = jnp.zeros_like(rows_out)
    masks = {(h, j, o): band(h, j, o) for o in (-1, 0, 1) for h in range(2) for j in bands(o)}
    for kd in range(9):
        k, d = kd // 3, kd % 3
        for i in range(3):
            for j in range(3):
                total = jnp.zeros((TILE, LANES), F32)
                for o in (-1, 0, 1):
                    if j in bands(o):
                        for x in range(rows_x):
                            at = (x * 16 + kd) * TILE
                            col = (x + i) // 2 * LANES
                            piece = products[abs(o), at : at + TILE, col : col + LANES]
                            total = total + jnp.where(masks[(x + i) % 2, j, o], piece, 0.0)
                row = d * 27 + i * 9 + j * 3 + k
                rows_out[row : row + 1] = jnp.sum(total, axis=0, keepdims=True)
    sums = lax.dot_general(
        jnp.where(((lanes_iota() >> 3) & 7) == rows_iota(), 1.0, 0.0),
        rows_out[...],
        (((1,), (1,)), ((), ())),
        precision=lax.Precision.HIGHEST,
        preferred_element_type=F32,
    )
    for n in range(out.shape[0]):
        out[n] = sums


def image_sums(info, grads, matrix, out, sums):
    total = jnp.dot(matrix[0], grads[:, :512], preferred_element_type=F32)
    sums[...] = total + jnp.dot(matrix[1], grads[:, 512:], preferred_element_type=F32)
    channels, rows_x, rows_z, _ = out.shape
    for c in range(channels):
        for x in range(rows_x):
            at = (c * rows_x + x) * TILE
            for t in range(0, rows_z // TILE, 2):
                both = [sums[at : at + TILE, s * LANES : (s + 1) * LANES] for s in (t, t + 1)]
                out[c, x, t * TILE : (t + 2) * TILE] = jnp.concatenate(both, axis=0).astype(BF16)


def local(image, filt, planted, likelihoods, slope):
    channels = image.shape[0]
    labels, rows_x, rows_z, rows_y = likelihoods.shape
    if (channels, labels, rows_x, rows_z, rows_y) != (8, 4, HALO, 4 * TILE, LANES):
        raise ValueError("brick size")
    lab, xy, gz = lax.axis_index("lab"), lax.axis_index("xy"), lax.axis_index("gz")
    colours = labels * lax.axis_size("lab")
    size_x, size_z = rows_x * lax.axis_size("xy"), rows_z * lax.axis_size("gz")
    rows = rows_z + TILE
    two = lax.axis_size("gz") > 2
    phases = range(1 + two)
    members = lax.axis_size("xy") * lax.axis_size("gz")
    info = jnp.stack(
        [
            1 - xy % 2,
            1 - gz % 2,
            xy * rows_x,
            gz * rows_z,
            lab * labels,
            1 - (xy + lab) % 2,
            jnp.minimum(xy, 1),
            jnp.minimum(lax.axis_size("xy") - 1 - xy, 1),
            jnp.minimum(gz, 1),
            jnp.minimum(lax.axis_size("gz") - 1 - gz, 1),
        ]
    ).astype(jnp.int32)

    inputs = (image, planted, likelihoods, slope)
    planes = channels + labels * rows_x + 2 * labels
    brick = shaped((planes, rows_z, LANES), BF16)
    taps = jnp.transpose(filt, (0, 2, 3, 4, 1))
    matrix, back_matrix, image, planted, likelihoods, slope, *packed = call(
        functools.partial(pack, colours, two),
        [shaped((2, 288, 384), BF16), shaped((2, 256, 768), BF16)]
        + [shaped(a.shape, a.dtype) for a in inputs]
        + [shaped((rows_x, labels, TILE, LANES), BF16)] * (1 + two)
        + [brick, brick],
        info,
        *(pltpu.with_memory_space_constraint(a, pltpu.HBM) for a in (taps, *inputs)),
        scratch=[
            pltpu.VMEM(taps.shape, BF16),
            pltpu.VMEM((112, LANES), F32),
            pltpu.SemaphoreType.DMA((5,)),
        ],
        name="pack",
        space=pltpu.HBM,
    )
    send_a, send_b = packed[1 + two :]
    faces = [swap(packed[phase], "gz", phase, True) for phase in phases]
    edges_a = [diagonal_swap(packed[phase], 0, phase) for phase in phases]
    edges_b = [diagonal_swap(packed[phase], 1, phase) for phase in phases]
    second = swap(send_b, "xy", 1)
    first = swap(send_a, "xy", 0)
    received = (first, second, *faces, *edges_a, *edges_b)

    part, stack = call(
        functools.partial(convolve, two),
        [shaped((3, rows_x, rows_z, LANES), F32), shaped((384, 1024), BF16)],
        info,
        image,
        *received,
        matrix,
        scratch=[pltpu.VMEM((288, 512), F32)],
        name="convolve",
    )
    logits, own, *sends = call(
        functools.partial(add_parts, two),
        [shaped(part.shape, F32), shaped(part.shape, BF16)]
        + [shaped((3, rows_x, TILE, LANES), BF16)] * (1 + two),
        info,
        part,
        lab_swap(part),
        name="add_parts",
    )
    mine = split_swap(own)
    mine_edges = [split_diagonal_swap(sends[phase], phase) for phase in phases]
    logit_faces = [swap(sends[phase], "gz", phase, True) for phase in phases]
    mine, mine_edges, logit_faces = lax.optimization_barrier((mine, mine_edges, logit_faces))
    other = lab_swap(mine)
    other_edges = [lab_swap(block) for block in mine_edges]
    extended = (labels, rows_x + 2 * HALO, rows, LANES)
    ring = shaped((3, rows_x + 2, rows, LANES), F32)
    v0, free, field = call(
        functools.partial(prepare, colours, two),
        [shaped(extended, F32), shaped(extended[1:], F32), shaped((labels, rows_x + 3, rows, LANES), F32)],
        info,
        planted,
        slope,
        likelihoods,
        *received,
        name="prepare",
    )
    v1, v2, squash_slope, dots = call(
        functools.partial(krylov, size_x, size_z, two),
        [shaped(extended, F32)] * 2 + [ring, shaped((members, TILE, LANES), F32)],
        info,
        v0,
        free,
        logits,
        mine,
        other,
        *logit_faces,
        *mine_edges,
        *other_edges,
        scratch=[pltpu.VMEM((3,) + extended[1:], F32), pltpu.VMEM((6 * labels, LANES), F32)],
        name="krylov",
    )
    edge = call(
        edges,
        ring,
        info,
        everyones(dots, ("xy", "gz")),
        v0,
        v1,
        v2,
        field,
        scratch=[pltpu.VMEM((labels, rows_x + 3, rows, LANES), F32)],
        name="edges",
    )
    grads, sums = call(
        filter_sums,
        [shaped((768, 1024), BF16), shaped((members, TILE, LANES), F32)],
        info,
        edge,
        lab_swap(edge),
        squash_slope,
        stack,
        scratch=[pltpu.VMEM((2, 512, 384), F32), pltpu.VMEM((LANES, LANES), F32)],
        name="filter_sums",
    )
    grad_image = call(
        image_sums,
        shaped(image.shape, BF16),
        info,
        grads,
        back_matrix,
        scratch=[pltpu.VMEM((256, 512), F32)],
        flops=10_000_000,
        name="image_sums",
    )
    grad_filter = jnp.sum(everyones(sums, ("xy", "gz")), axis=0)
    grad_filter = grad_filter[:, :81].reshape(channels, 3, 27)
    return grad_image, jnp.transpose(grad_filter, (1, 0, 2)).reshape(3, channels, 3, 3, 3)


def solution(mesh):
    return jax.shard_map(
        local,
        mesh=mesh,
        in_specs=(
            P("lab", ("crops", "xy"), "gz", None),
            P(),
            P(("crops", "xy"), "gz", None),
            P("lab", ("crops", "xy"), "gz", None),
            P("lab", ("crops", "xy"), "gz", None),
        ),
        out_specs=(P("lab", ("crops", "xy"), "gz", None), P("crops", "lab", None, None, None)),
        check_vma=False,
    )
```

```python
import functools

import jax
import jax.numpy as jnp
from jax import lax
from jax.experimental import pallas as pl
from jax.experimental.pallas import tpu as pltpu
from jax.sharding import PartitionSpec as P

HALO = 4
SEED = 64.0
SPREAD = 6.3
TILE = 8
LANES = 128
BF16, F32 = jnp.bfloat16, jnp.float32
EVEN_X, EVEN_Z, FIRST_X, FIRST_Z, COLOUR, UP, PREV_X, NEXT_X, PREV_Z, NEXT_Z = range(10)


SWAP_AXES = ("xy", "gz", "lab")


def mate(place, phase, count):
    other = place + 1 if (place - phase) % 2 == 0 else place - 1
    return other if phase <= min(place, other) and max(place, other) < count else None


def swap(block, partner):
    sizes = [lax.axis_size(axis) for axis in SWAP_AXES]
    devices = [(x, z, lab) for x in range(sizes[0]) for z in range(sizes[1]) for lab in range(sizes[2])]
    pairs = {}
    for device in devices:
        if partner(*device) is not None:
            pairs[device] = partner(*device)
    for other_of in (lambda x, z, lab: (x, z, lab ^ 1), lambda x, z, lab: (x, z ^ 1, lab)):
        for device in devices:
            other = other_of(*device)
            if device not in pairs and other in devices and other not in pairs:
                pairs[device], pairs[other] = other, device

    def flat(x, z, lab):
        return (x * sizes[1] + z) * sizes[2] + lab

    return lax.ppermute(block, SWAP_AXES, [(flat(*src), flat(*dst)) for src, dst in sorted(pairs.items())])


def x_swap(block, phase):
    count = lax.axis_size("xy")

    def partner(x, z, lab):
        other = mate(x, phase, count)
        return None if other is None else (other, z, lab)

    return swap(block, partner)


def z_swap(block, phase):
    count = lax.axis_size("gz")

    def partner(x, z, lab):
        other = mate(z, phase, count)
        return None if other is None else (x, other, lab)

    return swap(block, partner)


def diagonal_swap(block, x_phase, z_phase):
    counts = lax.axis_size("xy"), lax.axis_size("gz")

    def partner(x, z, lab):
        others = mate(x, x_phase, counts[0]), mate(z, z_phase, counts[1])
        return None if None in others else (*others, lab)

    return swap(block, partner)


def lab_swap(block):
    return lax.ppermute(block, "lab", [(0, 1), (1, 0)])


def split_swap(block):
    count = lax.axis_size("xy")

    def partner(x, z, lab):
        other = mate(x, lab % 2, count)
        return None if other is None else (other, z, lab)

    return swap(block, partner)


def split_diagonal_swap(block, z_phase):
    counts = lax.axis_size("xy"), lax.axis_size("gz")

    def partner(x, z, lab):
        others = mate(x, lab % 2, counts[0]), mate(z, z_phase, counts[1])
        return None if None in others else (*others, lab)

    return swap(block, partner)


def everyones(copies, axes):
    return lax.all_to_all(copies, axes, 0, 0)


def call(kernel, outs, *ins, scratch=(), flops=1_000_000, name=None, space=pltpu.VMEM):
    specs = [pl.BlockSpec(memory_space=pltpu.SMEM)]
    specs += [pl.BlockSpec(memory_space=space)] * (len(ins) - 1)
    bytes_moved = sum(a.size * a.dtype.itemsize for a in ins)
    return pl.pallas_call(
        kernel,
        out_shape=outs,
        in_specs=specs,
        out_specs=jax.tree.map(lambda _: pl.BlockSpec(memory_space=pltpu.VMEM), outs),
        scratch_shapes=list(scratch),
        compiler_params=pltpu.CompilerParams(vmem_limit_bytes=40 * 2**20),
        cost_estimate=pl.CostEstimate(flops=flops, bytes_accessed=bytes_moved, transcendentals=0),
        name=name,
    )(*ins)


def shaped(shape, dtype):
    return jax.ShapeDtypeStruct(shape, dtype)


def rows_iota(rows=TILE):
    return lax.broadcasted_iota(jnp.int32, (rows, LANES), 0)


def lanes_iota(rows=TILE):
    return lax.broadcasted_iota(jnp.int32, (rows, LANES), 1)


def fields(planted, likelihood, slope, colours, colour):
    free = planted >= colours
    member = jnp.where(planted == colour, 1.0, 0.0)
    return jnp.where(free, slope, SEED), jnp.where(free, likelihood, member)


def pack(
    colours,
    two,
    info,
    filt_in,
    image_in,
    planted_in,
    likelihoods_in,
    slope_in,
    wide_out,
    back_out,
    image,
    planted,
    likelihoods,
    slope,
    *refs,
):
    faces, (send_a, send_b, filt, taps, sems) = refs[: 1 + two], refs[1 + two :]
    pairs = (
        (planted_in, planted),
        (slope_in, slope),
        (likelihoods_in, likelihoods),
        (image_in, image),
        (filt_in, filt),
    )
    copies = [pltpu.make_async_copy(src, dst, sems.at[n]) for n, (src, dst) in enumerate(pairs)]
    for copy in reversed(copies):
        copy.start()
    copies[4].wait()
    spread_filter(info, filt, taps, wide_out, back_out)
    labels, rows_x, rows_z, _ = likelihoods.shape
    channels = image.shape[0]
    last, first = slice(rows_z - TILE, rows_z), slice(0, TILE)
    even = info[EVEN_X] == 1
    high, low = jnp.where(even, rows_x - 1, 0), jnp.where(even, 0, rows_x - 1)
    copies[0].wait()
    copies[1].wait()
    for x in range(rows_x):
        for l in range(labels):
            rhs = jnp.where(planted[x] >= colours, slope[l, x], SEED).astype(BF16)
            send_a[channels + l * rows_x + x] = rhs
            send_b[channels + l * rows_x + x] = rhs
    copies[2].wait()
    for l in range(labels):
        for send, at in ((send_a, high), (send_b, low)):
            for r in range(2):
                x = jnp.where(at == 0, 0, rows_x - 2) + r
                _, full = fields(planted[x], likelihoods[l, x], slope[l, x], colours, info[COLOUR] + l)
                send[channels + labels * rows_x + 2 * l + r] = full.astype(BF16)
    copies[3].wait()
    for c in range(channels):
        send_a[c] = image[c, high]
        send_b[c] = image[c, low]
    for phase, out in enumerate(faces):
        even = info[EVEN_Z] != phase
        place = (rows_iota() + jnp.where(even, 0, 4)) & 7

        def channel(c, x):
            return jnp.where(even, image[c, x, last].astype(F32), image[c, x, first].astype(F32))

        def turned(tile, for_even, for_odd):
            return jnp.where(even, pltpu.roll(tile, for_even, 0), pltpu.roll(tile, for_odd, 0))

        for x in range(rows_x):
            seeds = jnp.where(even, planted[x, last], planted[x, first])
            for l in range(labels):
                ends = [jnp.where(even, ref[l, x, last], ref[l, x, first]) for ref in (likelihoods, slope)]
                rhs, full = fields(seeds, *ends, colours, info[COLOUR] + l)
                first_channel = turned(channel(2 * l, x), 3, 6)
                second_channel = turned(channel(2 * l + 1, x), 4, 7)
                rest = jnp.where(place == 2, first_channel, second_channel)
                rest = jnp.where(place < 2, turned(full, 2, 4), rest)
                out[x, l] = jnp.where(place >= 4, rhs, rest).astype(BF16)


def sides(even, first, second):
    if second is None:
        return jnp.where(even, first, 0.0), jnp.where(even, 0.0, first)
    return jnp.where(even, first, second), jnp.where(even, second, first)


def ends_z(info, tiles, x, l):
    both = [ref[x, l].astype(F32) for ref in tiles]
    return sides(info[EVEN_Z] == 1, both[0], both[1] if len(both) > 1 else None)


def rhs_tile(above, below):
    return jnp.where(rows_iota() < 4, above, below)


def full_tile(above, below):
    return jnp.where(rows_iota() < 4, pltpu.roll(above, 4, 0), pltpu.roll(below, 6, 0))


def image_tile(info, above, below, c):
    up, down = (2, 5) if c % 2 == 0 else (1, 4)
    above = jnp.where(info[NEXT_Z] == 1, above, 0.0)
    below = jnp.where(info[PREV_Z] == 1, below, 0.0)
    return jnp.where(rows_iota() < 4, pltpu.roll(above, up, 0), pltpu.roll(below, down, 0))


def band(half, j, o, transposed=False):
    z, lane = rows_iota(), lanes_iota()
    other = lane & 7
    at = (z + 1 - other - 8 * o) if transposed else (other + 8 * o - z + 1)
    mask = at == j
    if half is not None:
        mask = mask & ((lane >> 6) == half)
    return mask


def bands(o, transposed=False):
    if o == 0:
        return (0, 1, 2)
    return (0,) if (o < 0) != transposed else (2,)


def spread_filter(info, filt, taps, wide_out, back_out):
    taps[...] = jnp.zeros_like(taps)
    for d in range(3):
        for i in range(3):
            for j in range(3):
                at = (d * 9 + i * 3 + j) * 4
                taps[at : at + 3, : filt.shape[-1]] = filt[d, i, j].astype(F32)
    lane = lanes_iota(LANES)
    channel = rows_iota(LANES) - 2 * info[COLOUR]
    all_taps = taps[...].astype(BF16)
    by_channel = jnp.where(channel == ((lane >> 3) & 7), 1.0, 0.0).astype(BF16)
    own = jnp.dot(
        all_taps, jnp.where(channel == lane, 1.0, 0.0).astype(BF16), preferred_element_type=F32
    ).astype(BF16)
    wide = jnp.dot(all_taps, by_channel, preferred_element_type=F32)
    tap, edge = rows_iota(taps.shape[0]), lanes_iota(taps.shape[0]) >> 3
    shift = jnp.where(edge >= 3, 1, 0) + jnp.where(edge >= 6, 1, 0)
    first_tap = jnp.where(edge < 9, (edge - 3 * shift) * 36 + shift, -LANES)
    places = [jnp.where(tap == first_tap + 4 * ij, 1.0, 0.0).astype(BF16) for ij in range(9)]
    back = [
        lax.dot_general(own, place, (((0,), (0,)), ((), ())), preferred_element_type=F32) for place in places
    ]
    zero = jnp.zeros((TILE, LANES), F32)
    for at_out, distances in enumerate(((0,), (-1, 1))):
        cases = [(o, j) for o in distances for j in bands(o)]
        masks = {(h, j): band(h, j, o) for h in range(2) for o, j in cases}
        for kd in range(9):
            for pair in range(2):
                for block in range(3):
                    tiles = []
                    for x in (2 * pair, 2 * pair + 1):
                        tile = zero
                        for i in range(3):
                            if (x + i) // 2 == block:
                                for _, j in cases:
                                    row = (kd % 3 * 9 + i * 3 + j) * 4 + kd // 3
                                    value = jnp.broadcast_to(wide[row : row + 1], (TILE, LANES))
                                    tile = jnp.where(masks[(x + i) % 2, j], value, tile)
                        tiles.append(tile)
                    at = (kd * 4 + 2 * pair) * TILE
                    wide_out[at_out, at : at + 16, block * LANES : (block + 1) * LANES] = jnp.concatenate(
                        tiles, axis=0
                    ).astype(BF16)
        cases = [(o, j) for o in distances for j in bands(o, True)]
        masks = {j: band(None, j, o, True) for o, j in cases}
        for c in range(8):
            for pair in range(2):
                for block in range(6):
                    tiles = []
                    for x in (2 * pair, 2 * pair + 1):
                        tile = zero
                        i = x + 2 - block
                        if 0 <= i < 3:
                            for _, j in cases:
                                value = jnp.broadcast_to(back[i * 3 + j][c : c + 1], (TILE, LANES))
                                tile = jnp.where(masks[j], value, tile)
                        tiles.append(tile)
                    at = (c * 4 + 2 * pair) * TILE
                    back_out[at_out, at : at + 16, block * LANES : (block + 1) * LANES] = jnp.concatenate(
                        tiles, axis=0
                    ).astype(BF16)


def store_tiles(out, at, planes):
    for t in range(4):
        both = jnp.concatenate([plane[tile_rows(t)] for plane in planes], axis=0)
        out[at : at + 16, t * LANES : (t + 1) * LANES] = both.astype(BF16)
        both = [jnp.where(rows_iota() < 4, plane[tile_rows(t + 1)], plane[tile_rows(t - 1)]) for plane in planes]
        both = jnp.concatenate(both, axis=0)
        out[at : at + 16, (t + 4) * LANES : (t + 5) * LANES] = both.astype(BF16)


def tile_rows(t):
    at = (4 if t < 0 else t) * TILE
    return slice(at, at + TILE)


def convolve(two, info, image, first, second, *refs):
    faces, edges_a, edges_b = refs[: 1 + two], refs[1 + two : 2 + 2 * two], refs[2 + 2 * two : 3 + 3 * two]
    matrix, part, stack, sums = refs[3 + 3 * two :]
    channels, rows_x = image.shape[0], image.shape[1]
    even = info[EVEN_X] == 1
    for xp in range(rows_x + 2):
        for c in range(0, channels, 2):
            planes = []
            if 0 < xp <= rows_x:
                ends = [ends_z(info, faces, xp - 1, c // 2)]
            else:
                ends = [ends_z(info, tiles, rows_x - 1 if xp == 0 else 0, c // 2) for tiles in (edges_a, edges_b)]
            for ch in (c, c + 1):
                tiles = [image_tile(info, *pair, ch) for pair in ends]
                if 0 < xp <= rows_x:
                    planes.append(jnp.concatenate([image[ch, xp - 1].astype(F32), tiles[0]], axis=0))
                else:
                    received = [
                        jnp.concatenate([ref[ch].astype(F32), tile], axis=0)
                        for ref, tile in zip((first, second), tiles)
                    ]
                    above, below = sides(even, *received)
                    plane, exists = (below, PREV_X) if xp == 0 else (above, NEXT_X)
                    planes.append(jnp.where(info[exists] == 1, plane, 0.0))
            at = (xp * channels + c) * TILE
            store_tiles(stack, at, planes)
    total = jnp.dot(matrix[0], stack[:, :512], preferred_element_type=F32)
    sums[...] = total + jnp.dot(matrix[1], stack[:, 512:], preferred_element_type=F32)
    lane = lanes_iota()
    for d in range(3):
        for x in range(rows_x):
            for t in range(4):
                cols = slice(t * LANES, (t + 1) * LANES)

                def piece(k):
                    at = ((k * 3 + d) * rows_x + x) * TILE
                    return sums[at : at + TILE, cols]

                before = jnp.where(lane > 0, pltpu.roll(piece(0), 1, 1), 0.0)
                after = jnp.where(lane < LANES - 1, pltpu.roll(piece(2), LANES - 1, 1), 0.0)
                part[d, x, tile_rows(t)] = piece(1) + before + after


def add_parts(two, info, part, other, logits, brick, *faces):
    rows_x, rows_z = part.shape[1], part.shape[2]
    for d in range(3):
        for x in range(rows_x):
            total = part[d, x] + other[d, x]
            logits[d, x] = total
            brick[d, x] = total.astype(BF16)
            for phase, face in enumerate(faces):
                even = info[EVEN_Z] != phase
                face[d, x] = jnp.where(even, total[rows_z - TILE :], total[:TILE]).astype(BF16)


def up(plane, dim):
    return pltpu.roll(plane, plane.shape[dim] - 1, dim)


def down(plane, dim):
    return pltpu.roll(plane, 1, dim)


def prepare(colours, two, info, planted, slope, likelihoods, first, second, *refs):
    faces, edges_a, edges_b = refs[: 1 + two], refs[1 + two : 2 + 2 * two], refs[2 + 2 * two : 3 + 3 * two]
    v0, free, field = refs[3 + 3 * two :]
    labels, rows_x, _, _ = slope.shape
    channels = 2 * labels
    even = info[EVEN_X] == 1

    def grown(index, source, l, tile):
        received = [
            jnp.concatenate([ref[index].astype(F32), tile(*ends_z(info, tiles, source, l))], axis=0)
            for ref, tiles in ((first, edges_a), (second, edges_b))
        ]
        return sides(even, *received)

    for x in range(rows_x):
        for l in range(labels):
            ends = ends_z(info, faces, x, l)
            rhs, full = fields(planted[x], likelihoods[l, x], slope[l, x], colours, info[COLOUR] + l)
            rhs = jnp.concatenate([rhs, rhs_tile(*ends)], axis=0)
            field[l, x + 1] = jnp.concatenate([full, full_tile(*ends)], axis=0)
            above, below = grown(channels + l * rows_x + x, x, l, rhs_tile)
            for at, plane in ((x + HALO, rhs), (x, below), (x + HALO + rows_x, above)):
                open_cell = plane < SEED / 2
                v0[l, at] = jnp.where(open_cell, plane, 0.0)
                if l == 0:
                    free[at] = jnp.where(open_cell, 1.0, 0.0)
    for l in range(labels):
        base = 2 * labels + labels * rows_x + 2 * l
        field[l, 0] = grown(base + 1, rows_x - 1, l, full_tile)[1]
        for r in range(2):
            field[l, rows_x + 1 + r] = grown(base + r, r, l, full_tile)[0]


def krylov(size_x, size_z, two, info, v0, free, logits, mine, other, *refs):
    faces, mine_edges, other_edges = (refs[n * (1 + two) : (n + 1) * (1 + two)] for n in range(3))
    v1, v2, slope_out, dots_out, weight, dots = refs[3 * (1 + two) :]
    labels, _, rows, _ = v0.shape
    rows_x, rows_z = logits.shape[1:3]
    is_up = info[UP] == 1
    z = rows_iota(rows)
    z = info[FIRST_Z] + jnp.where(z < rows_z + HALO, z, z - rows)
    inside_z = (z >= 0) & (z < size_z)
    in_z = jnp.where(inside_z, 1.0, 0.0)
    next_z = jnp.where(inside_z & (z < size_z - 1), 1.0, 0.0)
    in_zy = jnp.where(lanes_iota(rows) < LANES - 1, in_z, 0.0)
    for at in range(rows_x + 2 * HALO):
        x = at - HALO
        place = info[FIRST_X] + x
        inside = (place >= 0) & (place < size_x)
        in_x = jnp.where(inside, 1.0, 0.0)
        next_x = jnp.where(inside & (place < size_x - 1), 1.0, 0.0)
        for d in range(3):
            def grown(plane, tiles, source):
                return jnp.concatenate([plane, rhs_tile(*ends_z(info, tiles, d, source))], axis=0)

            if 0 <= x < rows_x:
                plane = grown(logits[d, x], faces, x)
            else:
                source = x % rows_x
                here = grown(mine[d, source].astype(F32), mine_edges, source)
                there = grown(other[d, source].astype(F32), other_edges, source)
                plane = jnp.where(is_up, there, here) if x < 0 else jnp.where(is_up, here, there)
            squashed = 1.0 / (1.0 + jnp.exp(-plane))
            valid = (in_z * next_x, next_z * in_x, in_zy * in_x)[d]
            weight[d, at] = (0.05 + squashed) * valid
            if -1 <= x <= rows_x:
                slope_out[d, x + 1] = squashed * (1.0 - squashed) * valid

    def label(l, carry):
        def operate(v, start, stop):
            flow_before = weight[0, start - 1] * (v[l, start - 1] - v[l, start])
            for at in range(start, stop):
                here = v[l, at]
                flow = weight[0, at] * (here - v[l, at + 1])
                flow_z = weight[1, at] * (here - up(here, 0))
                flow_y = weight[2, at] * (here - up(here, 1))
                result = flow - flow_before + (flow_z - down(flow_z, 0)) + (flow_y - down(flow_y, 1))
                yield at, here, free[at] * result
                flow_before = flow

        for at, here, result in operate(v0, 1, rows_x + 2 * HALO - 1):
            v1[l, at] = result * (1.0 / SPREAD) - here
        for at, here, result in operate(v1, 2, rows_x + 2 * HALO - 2):
            v2[l, at] = result * (2.0 / SPREAD) - 2.0 * here - v0[l, at]
        sums = [jnp.zeros((TILE, LANES), F32)] * 6
        for at, here, result in operate(v2, HALO, HALO + rows_x):
            a, b = v0[l, at], v1[l, at]
            for n, product in enumerate((a * a, a * b, b * b, b * here, here * here, here * result)):
                for t in range(rows_z // TILE):
                    sums[n] = sums[n] + product[tile_rows(t)]
        for n in range(6):
            dots[pl.ds(n * labels + l, 1), :] = jnp.sum(sums[n], axis=0, keepdims=True)
        return carry

    lax.fori_loop(0, labels, label, 0)
    total = jnp.sum(dots[...], axis=1, keepdims=True)
    tile = jnp.zeros((TILE, LANES), F32)
    for n in range(6):
        column = total[tile_rows(n // 2)]
        column = jnp.broadcast_to(column, (TILE, LANES))
        tile = jnp.where(lanes_iota() == n, pltpu.roll(column, 4, 0) if n % 2 else column, tile)
    for n in range(dots_out.shape[0]):
        dots_out[n] = tile


def steps(g00, g01, g11, g12, g22, k22):
    g02 = 2.0 * g11 - g00
    k00 = SPREAD * (g00 + g01)
    k01 = SPREAD * (g01 + g11)
    k02 = SPREAD * (g02 + g12)
    k11 = SPREAD * (g11 + 0.5 * (g12 + g01))
    k12 = SPREAD * (g12 + 0.5 * (g22 + g02))
    alpha = g00 / k00
    c0 = alpha
    r0 = 1.0 - alpha * SPREAD
    r1 = -alpha * SPREAD
    rr = r0 * r0 * g00 + 2.0 * r0 * r1 * g01 + r1 * r1 * g11
    beta = rr / g00
    p0, p1 = r0 + beta, r1
    alpha = rr / (p0 * p0 * k00 + 2.0 * p0 * p1 * k01 + p1 * p1 * k11)
    c0, c1 = c0 + alpha * p0, alpha * p1
    r0 = r0 - alpha * SPREAD * (p0 + 0.5 * p1)
    r1 = r1 - alpha * SPREAD * (p0 + p1)
    r2 = -alpha * SPREAD * 0.5 * p1
    rr_next = r0 * r0 * g00 + r1 * r1 * g11 + r2 * r2 * g22
    rr_next = rr_next + 2.0 * (r0 * r1 * g01 + r0 * r2 * g02 + r1 * r2 * g12)
    beta = rr_next / rr
    p0, p1, p2 = r0 + beta * p0, r1 + beta * p1, r2
    curve = p0 * p0 * k00 + p1 * p1 * k11 + p2 * p2 * k22
    curve = curve + 2.0 * (p0 * p1 * k01 + p0 * p2 * k02 + p1 * p2 * k12)
    alpha = rr_next / curve
    return c0 + alpha * p0, c1 + alpha * p1, alpha * p2


def edges(info, parts, v0, v1, v2, field, out, lam):
    labels, _, rows, _ = v0.shape
    rows_x = out.shape[1] - 2
    total = jnp.sum(parts[...], axis=0)
    grams = [jnp.broadcast_to(total[:, n : n + 1], (TILE, LANES)) for n in range(6)]
    c0, c1, c2 = steps(*grams)
    for l in range(labels):
        s0, s1, s2 = (jnp.broadcast_to(c[l : l + 1], (rows, LANES)) for c in (c0, c1, c2))
        for at in range(rows_x + 3):
            source = at + HALO - 1
            lam[l, at] = s0 * v0[l, source] + s1 * v1[l, source] + s2 * v2[l, source]
    for at in range(rows_x + 2):
        sums = [jnp.zeros((rows, LANES), F32)] * 3
        for l in range(labels):
            a, b = lam[l, at], field[l, at]
            sums[0] = sums[0] - (a - lam[l, at + 1]) * (b - field[l, at + 1])
            sums[1] = sums[1] - (a - up(a, 0)) * (b - up(b, 0))
            sums[2] = sums[2] - (a - up(a, 1)) * (b - up(b, 1))
        for d in range(3):
            out[d, at] = sums[d]


def filter_sums(info, edge, other, slope, stack, grads, out, products, rows_out):
    rows_x = edge.shape[1] - 2
    lane = lanes_iota(edge.shape[2])
    for xp in range(rows_x + 2):
        shifted = [[], [], []]
        for d in range(3):
            plane = ((edge[d, xp] + other[d, xp]) * slope[d, xp]).astype(BF16).astype(F32)
            shifted[0].append(jnp.where(lane < LANES - 1, up(plane, 1), 0.0))
            shifted[1].append(plane)
            shifted[2].append(jnp.where(lane > 0, down(plane, 1), 0.0))
        planes = shifted[0] + shifted[1] + shifted[2]
        planes += [jnp.zeros_like(planes[0])] * 7
        for pair in range(8):
            at = (xp * 16 + 2 * pair) * TILE
            store_tiles(grads, at, planes[2 * pair : 2 * pair + 2])
    own = grads[LANES : LANES * (rows_x + 1), : 4 * LANES]
    for n in range(2):
        products[n] = lax.dot_general(
            own, stack[:, 512 * n : 512 * (n + 1)], (((1,), (1,)), ((), ())), preferred_element_type=F32
        )
    rows_out[...] = jnp.zeros_like(rows_out)
    masks = {(h, j, o): band(h, j, o) for o in (-1, 0, 1) for h in range(2) for j in bands(o)}
    for kd in range(9):
        k, d = kd // 3, kd % 3
        for i in range(3):
            for j in range(3):
                total = jnp.zeros((TILE, LANES), F32)
                for o in (-1, 0, 1):
                    if j in bands(o):
                        for x in range(rows_x):
                            at = (x * 16 + kd) * TILE
                            col = (x + i) // 2 * LANES
                            piece = products[abs(o), at : at + TILE, col : col + LANES]
                            total = total + jnp.where(masks[(x + i) % 2, j, o], piece, 0.0)
                row = d * 27 + i * 9 + j * 3 + k
                rows_out[row : row + 1] = jnp.sum(total, axis=0, keepdims=True)
    sums = lax.dot_general(
        jnp.where(((lanes_iota() >> 3) & 7) == rows_iota(), 1.0, 0.0),
        rows_out[...],
        (((1,), (1,)), ((), ())),
        precision=lax.Precision.HIGHEST,
        preferred_element_type=F32,
    )
    for n in range(out.shape[0]):
        out[n] = sums


def image_sums(info, grads, matrix, out, sums):
    total = jnp.dot(matrix[0], grads[:, :512], preferred_element_type=F32)
    sums[...] = total + jnp.dot(matrix[1], grads[:, 512:], preferred_element_type=F32)
    channels, rows_x, rows_z, _ = out.shape
    for c in range(channels):
        for x in range(rows_x):
            at = (c * rows_x + x) * TILE
            for t in range(0, rows_z // TILE, 2):
                both = [sums[at : at + TILE, s * LANES : (s + 1) * LANES] for s in (t, t + 1)]
                out[c, x, t * TILE : (t + 2) * TILE] = jnp.concatenate(both, axis=0).astype(BF16)


def local(image, filt, planted, likelihoods, slope):
    channels = image.shape[0]
    labels, rows_x, rows_z, rows_y = likelihoods.shape
    if (channels, labels, rows_x, rows_z, rows_y) != (8, 4, HALO, 4 * TILE, LANES):
        raise ValueError("brick size")
    lab, xy, gz = lax.axis_index("lab"), lax.axis_index("xy"), lax.axis_index("gz")
    colours = labels * lax.axis_size("lab")
    size_x, size_z = rows_x * lax.axis_size("xy"), rows_z * lax.axis_size("gz")
    rows = rows_z + TILE
    two = lax.axis_size("gz") > 2
    phases = range(1 + two)
    members = lax.axis_size("xy") * lax.axis_size("gz")
    info = jnp.stack(
        [
            1 - xy % 2,
            1 - gz % 2,
            xy * rows_x,
            gz * rows_z,
            lab * labels,
            1 - (xy + lab) % 2,
            jnp.minimum(xy, 1),
            jnp.minimum(lax.axis_size("xy") - 1 - xy, 1),
            jnp.minimum(gz, 1),
            jnp.minimum(lax.axis_size("gz") - 1 - gz, 1),
        ]
    ).astype(jnp.int32)

    inputs = (image, planted, likelihoods, slope)
    planes = channels + labels * rows_x + 2 * labels
    brick = shaped((planes, rows_z, LANES), BF16)
    taps = jnp.transpose(filt, (0, 2, 3, 4, 1))
    matrix, back_matrix, image, planted, likelihoods, slope, *packed = call(
        functools.partial(pack, colours, two),
        [shaped((2, 288, 384), BF16), shaped((2, 256, 768), BF16)]
        + [shaped(a.shape, a.dtype) for a in inputs]
        + [shaped((rows_x, labels, TILE, LANES), BF16)] * (1 + two)
        + [brick, brick],
        info,
        *(pltpu.with_memory_space_constraint(a, pltpu.HBM) for a in (taps, *inputs)),
        scratch=[
            pltpu.VMEM(taps.shape, BF16),
            pltpu.VMEM((112, LANES), F32),
            pltpu.SemaphoreType.DMA((5,)),
        ],
        name="pack",
        space=pltpu.HBM,
    )
    send_a, send_b = packed[1 + two :]
    faces = [z_swap(packed[phase], phase) for phase in phases]
    edges_a = [diagonal_swap(packed[phase], 0, phase) for phase in phases]
    edges_b = [diagonal_swap(packed[phase], 1, phase) for phase in phases]
    second = x_swap(send_b, 1)
    first = x_swap(send_a, 0)
    received = (first, second, *faces, *edges_a, *edges_b)

    part, stack = call(
        functools.partial(convolve, two),
        [shaped((3, rows_x, rows_z, LANES), F32), shaped((384, 1024), BF16)],
        info,
        image,
        *received,
        matrix,
        scratch=[pltpu.VMEM((288, 512), F32)],
        name="convolve",
    )
    logits, own, *sends = call(
        functools.partial(add_parts, two),
        [shaped(part.shape, F32), shaped(part.shape, BF16)]
        + [shaped((3, rows_x, TILE, LANES), BF16)] * (1 + two),
        info,
        part,
        lab_swap(part),
        name="add_parts",
    )
    mine = split_swap(own)
    mine_edges = [split_diagonal_swap(sends[phase], phase) for phase in phases]
    logit_faces = [z_swap(sends[phase], phase) for phase in phases]
    mine, mine_edges, logit_faces = lax.optimization_barrier((mine, mine_edges, logit_faces))
    other = lab_swap(mine)
    other_edges = [lab_swap(block) for block in mine_edges]
    extended = (labels, rows_x + 2 * HALO, rows, LANES)
    ring = shaped((3, rows_x + 2, rows, LANES), F32)
    v0, free, field = call(
        functools.partial(prepare, colours, two),
        [shaped(extended, F32), shaped(extended[1:], F32), shaped((labels, rows_x + 3, rows, LANES), F32)],
        info,
        planted,
        slope,
        likelihoods,
        *received,
        name="prepare",
    )
    v1, v2, squash_slope, dots = call(
        functools.partial(krylov, size_x, size_z, two),
        [shaped(extended, F32)] * 2 + [ring, shaped((members, TILE, LANES), F32)],
        info,
        v0,
        free,
        logits,
        mine,
        other,
        *logit_faces,
        *mine_edges,
        *other_edges,
        scratch=[pltpu.VMEM((3,) + extended[1:], F32), pltpu.VMEM((6 * labels, LANES), F32)],
        name="krylov",
    )
    edge = call(
        edges,
        ring,
        info,
        everyones(dots, ("xy", "gz")),
        v0,
        v1,
        v2,
        field,
        scratch=[pltpu.VMEM((labels, rows_x + 3, rows, LANES), F32)],
        name="edges",
    )
    grads, sums = call(
        filter_sums,
        [shaped((768, 1024), BF16), shaped((members, TILE, LANES), F32)],
        info,
        edge,
        lab_swap(edge),
        squash_slope,
        stack,
        scratch=[pltpu.VMEM((2, 512, 384), F32), pltpu.VMEM((LANES, LANES), F32)],
        name="filter_sums",
    )
    grad_image = call(
        image_sums,
        shaped(image.shape, BF16),
        info,
        grads,
        back_matrix,
        scratch=[pltpu.VMEM((256, 512), F32)],
        flops=10_000_000,
        name="image_sums",
    )
    grad_filter = jnp.sum(everyones(sums, ("xy", "gz")), axis=0)
    grad_filter = grad_filter[:, :81].reshape(channels, 3, 27)
    return grad_image, jnp.transpose(grad_filter, (1, 0, 2)).reshape(3, channels, 3, 3, 3)


def solution(mesh):
    return jax.shard_map(
        local,
        mesh=mesh,
        in_specs=(
            P("lab", ("crops", "xy"), "gz", None),
            P(),
            P(("crops", "xy"), "gz", None),
            P("lab", ("crops", "xy"), "gz", None),
            P("lab", ("crops", "xy"), "gz", None),
        ),
        out_specs=(P("lab", ("crops", "xy"), "gz", None), P("crops", "lab", None, None, None)),
        check_vma=False,
    )
```

```python
import functools

import jax
import jax.numpy as jnp
from jax import lax
from jax.experimental import pallas as pl
from jax.experimental.pallas import tpu as pltpu
from jax.sharding import PartitionSpec as P

HALO = 4
SEED = 64.0
SPREAD = 6.3
TILE = 8
LANES = 128
BF16, F32 = jnp.bfloat16, jnp.float32
EVEN_X, EVEN_Z, FIRST_X, FIRST_Z, COLOUR, UP, PREV_X, NEXT_X, PREV_Z, NEXT_Z = range(10)


SWAP_AXES = ("xy", "gz", "lab")


def mate(place, phase, count):
    other = place + 1 if (place - phase) % 2 == 0 else place - 1
    return other if phase <= min(place, other) and max(place, other) < count else None


def swap(block, partner):
    sizes = [lax.axis_size(axis) for axis in SWAP_AXES]
    devices = [(x, z, lab) for x in range(sizes[0]) for z in range(sizes[1]) for lab in range(sizes[2])]
    pairs = {}
    for device in devices:
        if partner(*device) is not None:
            pairs[device] = partner(*device)
    for other_of in (lambda x, z, lab: (x, z, lab ^ 1), lambda x, z, lab: (x, z ^ 1, lab)):
        for device in devices:
            other = other_of(*device)
            if device not in pairs and other in devices and other not in pairs:
                pairs[device], pairs[other] = other, device

    def flat(x, z, lab):
        return (x * sizes[1] + z) * sizes[2] + lab

    return lax.ppermute(block, SWAP_AXES, [(flat(*src), flat(*dst)) for src, dst in sorted(pairs.items())])


def x_swap(block, phase):
    count = lax.axis_size("xy")

    def partner(x, z, lab):
        other = mate(x, phase, count)
        return None if other is None else (other, z, lab)

    return swap(block, partner)


def z_swap(block, phase):
    count = lax.axis_size("gz")

    def partner(x, z, lab):
        other = mate(z, phase, count)
        return None if other is None else (x, other, lab)

    return swap(block, partner)


def diagonal_swap(block, x_phase, z_phase):
    counts = lax.axis_size("xy"), lax.axis_size("gz")

    def partner(x, z, lab):
        others = mate(x, x_phase, counts[0]), mate(z, z_phase, counts[1])
        return None if None in others else (*others, lab)

    return swap(block, partner)


def lab_swap(block):
    return lax.ppermute(block, "lab", [(0, 1), (1, 0)])


def split_swap(block):
    count = lax.axis_size("xy")

    def partner(x, z, lab):
        other = mate(x, lab % 2, count)
        return None if other is None else (other, z, lab)

    return swap(block, partner)


def split_diagonal_swap(block, z_phase):
    counts = lax.axis_size("xy"), lax.axis_size("gz")

    def partner(x, z, lab):
        others = mate(x, lab % 2, counts[0]), mate(z, z_phase, counts[1])
        return None if None in others else (*others, lab)

    return swap(block, partner)


def everyones(copies, axes):
    return lax.all_to_all(copies, axes, 0, 0)


def call(kernel, outs, *ins, scratch=(), flops=1_000_000, name=None, space=pltpu.VMEM):
    specs = [pl.BlockSpec(memory_space=pltpu.SMEM)]
    specs += [pl.BlockSpec(memory_space=space)] * (len(ins) - 1)
    bytes_moved = sum(a.size * a.dtype.itemsize for a in ins)
    return pl.pallas_call(
        kernel,
        out_shape=outs,
        in_specs=specs,
        out_specs=jax.tree.map(lambda _: pl.BlockSpec(memory_space=pltpu.VMEM), outs),
        scratch_shapes=list(scratch),
        compiler_params=pltpu.CompilerParams(vmem_limit_bytes=40 * 2**20),
        cost_estimate=pl.CostEstimate(flops=flops, bytes_accessed=bytes_moved, transcendentals=0),
        name=name,
    )(*ins)


def shaped(shape, dtype):
    return jax.ShapeDtypeStruct(shape, dtype)


def rows_iota(rows=TILE):
    return lax.broadcasted_iota(jnp.int32, (rows, LANES), 0)


def lanes_iota(rows=TILE):
    return lax.broadcasted_iota(jnp.int32, (rows, LANES), 1)


def fields(planted, likelihood, slope, colours, colour):
    free = planted >= colours
    member = jnp.where(planted == colour, 1.0, 0.0)
    return jnp.where(free, slope, SEED), jnp.where(free, likelihood, member)


def pack(
    colours,
    two,
    info,
    filt_in,
    image_in,
    planted_in,
    likelihoods_in,
    slope_in,
    wide_out,
    back_out,
    image,
    planted,
    likelihoods,
    slope,
    *refs,
):
    faces, (send_a, send_b, filt, taps, sems) = refs[: 1 + two], refs[1 + two :]
    pairs = (
        (planted_in, planted),
        (slope_in, slope),
        (likelihoods_in, likelihoods),
        (image_in, image),
        (filt_in, filt),
    )
    copies = [pltpu.make_async_copy(src, dst, sems.at[n]) for n, (src, dst) in enumerate(pairs)]
    for copy in reversed(copies):
        copy.start()
    copies[4].wait()
    spread_filter(info, filt, taps, wide_out, back_out)
    labels, rows_x, rows_z, _ = likelihoods.shape
    channels = image.shape[0]
    last, first = slice(rows_z - TILE, rows_z), slice(0, TILE)
    even = info[EVEN_X] == 1
    high, low = jnp.where(even, rows_x - 1, 0), jnp.where(even, 0, rows_x - 1)
    copies[0].wait()
    copies[1].wait()
    for x in range(rows_x):
        for l in range(labels):
            rhs = jnp.where(planted[x] >= colours, slope[l, x], SEED).astype(BF16)
            send_a[channels + l * rows_x + x] = rhs
            send_b[channels + l * rows_x + x] = rhs
    copies[2].wait()
    for l in range(labels):
        for send, at in ((send_a, high), (send_b, low)):
            for r in range(2):
                x = jnp.where(at == 0, 0, rows_x - 2) + r
                _, full = fields(planted[x], likelihoods[l, x], slope[l, x], colours, info[COLOUR] + l)
                send[channels + labels * rows_x + 2 * l + r] = full.astype(BF16)
    copies[3].wait()
    for c in range(channels):
        send_a[c] = image[c, high]
        send_b[c] = image[c, low]
    for phase, out in enumerate(faces):
        even = info[EVEN_Z] != phase
        place = (rows_iota() + jnp.where(even, 0, 4)) & 7

        def channel(c, x):
            return jnp.where(even, image[c, x, last].astype(F32), image[c, x, first].astype(F32))

        def turned(tile, for_even, for_odd):
            return jnp.where(even, pltpu.roll(tile, for_even, 0), pltpu.roll(tile, for_odd, 0))

        for x in range(rows_x):
            seeds = jnp.where(even, planted[x, last], planted[x, first])
            for l in range(labels):
                ends = [jnp.where(even, ref[l, x, last], ref[l, x, first]) for ref in (likelihoods, slope)]
                rhs, full = fields(seeds, *ends, colours, info[COLOUR] + l)
                first_channel = turned(channel(2 * l, x), 3, 6)
                second_channel = turned(channel(2 * l + 1, x), 4, 7)
                rest = jnp.where(place == 2, first_channel, second_channel)
                rest = jnp.where(place < 2, turned(full, 2, 4), rest)
                out[x, l] = jnp.where(place >= 4, rhs, rest).astype(BF16)


def sides(even, first, second):
    if second is None:
        return jnp.where(even, first, 0.0), jnp.where(even, 0.0, first)
    return jnp.where(even, first, second), jnp.where(even, second, first)


def ends_z(info, tiles, x, l):
    both = [ref[x, l].astype(F32) for ref in tiles]
    return sides(info[EVEN_Z] == 1, both[0], both[1] if len(both) > 1 else None)


def rhs_tile(above, below):
    return jnp.where(rows_iota() < 4, above, below)


def full_tile(above, below):
    return jnp.where(rows_iota() < 4, pltpu.roll(above, 4, 0), pltpu.roll(below, 6, 0))


def image_tile(info, above, below, c):
    up, down = (2, 5) if c % 2 == 0 else (1, 4)
    above = jnp.where(info[NEXT_Z] == 1, above, 0.0)
    below = jnp.where(info[PREV_Z] == 1, below, 0.0)
    return jnp.where(rows_iota() < 4, pltpu.roll(above, up, 0), pltpu.roll(below, down, 0))


def band(half, j, o, transposed=False):
    z, lane = rows_iota(), lanes_iota()
    other = lane & 7
    at = (z + 1 - other - 8 * o) if transposed else (other + 8 * o - z + 1)
    mask = at == j
    if half is not None:
        mask = mask & ((lane >> 6) == half)
    return mask


def bands(o, transposed=False):
    if o == 0:
        return (0, 1, 2)
    return (0,) if (o < 0) != transposed else (2,)


def spread_filter(info, filt, taps, wide_out, back_out):
    taps[...] = jnp.zeros_like(taps)
    for d in range(3):
        for i in range(3):
            for j in range(3):
                at = (d * 9 + i * 3 + j) * 4
                taps[at : at + 3, : filt.shape[-1]] = filt[d, i, j].astype(F32)
    lane = lanes_iota(LANES)
    channel = rows_iota(LANES) - 2 * info[COLOUR]
    all_taps = taps[...].astype(BF16)
    by_channel = jnp.where(channel == ((lane >> 3) & 7), 1.0, 0.0).astype(BF16)
    own = jnp.dot(
        all_taps, jnp.where(channel == lane, 1.0, 0.0).astype(BF16), preferred_element_type=F32
    ).astype(BF16)
    wide = jnp.dot(all_taps, by_channel, preferred_element_type=F32)
    tap, edge = rows_iota(taps.shape[0]), lanes_iota(taps.shape[0]) >> 3
    shift = jnp.where(edge >= 3, 1, 0) + jnp.where(edge >= 6, 1, 0)
    first_tap = jnp.where(edge < 9, (edge - 3 * shift) * 36 + shift, -LANES)
    places = [jnp.where(tap == first_tap + 4 * ij, 1.0, 0.0).astype(BF16) for ij in range(9)]
    back = [
        lax.dot_general(own, place, (((0,), (0,)), ((), ())), preferred_element_type=F32) for place in places
    ]
    zero = jnp.zeros((TILE, LANES), F32)
    for at_out, distances in enumerate(((0,), (-1, 1))):
        cases = [(o, j) for o in distances for j in bands(o)]
        masks = {(h, j): band(h, j, o) for h in range(2) for o, j in cases}
        for kd in range(9):
            for pair in range(2):
                for block in range(3):
                    tiles = []
                    for x in (2 * pair, 2 * pair + 1):
                        tile = zero
                        for i in range(3):
                            if (x + i) // 2 == block:
                                for _, j in cases:
                                    row = (kd % 3 * 9 + i * 3 + j) * 4 + kd // 3
                                    value = jnp.broadcast_to(wide[row : row + 1], (TILE, LANES))
                                    tile = jnp.where(masks[(x + i) % 2, j], value, tile)
                        tiles.append(tile)
                    at = (kd * 4 + 2 * pair) * TILE
                    wide_out[at_out, at : at + 16, block * LANES : (block + 1) * LANES] = jnp.concatenate(
                        tiles, axis=0
                    ).astype(BF16)
        cases = [(o, j) for o in distances for j in bands(o, True)]
        masks = {j: band(None, j, o, True) for o, j in cases}
        for c in range(8):
            for pair in range(2):
                for block in range(6):
                    tiles = []
                    for x in (2 * pair, 2 * pair + 1):
                        tile = zero
                        i = x + 2 - block
                        if 0 <= i < 3:
                            for _, j in cases:
                                value = jnp.broadcast_to(back[i * 3 + j][c : c + 1], (TILE, LANES))
                                tile = jnp.where(masks[j], value, tile)
                        tiles.append(tile)
                    at = (c * 4 + 2 * pair) * TILE
                    back_out[at_out, at : at + 16, block * LANES : (block + 1) * LANES] = jnp.concatenate(
                        tiles, axis=0
                    ).astype(BF16)


def store_tiles(out, at, planes):
    for t in range(4):
        both = jnp.concatenate([plane[tile_rows(t)] for plane in planes], axis=0)
        out[at : at + 16, t * LANES : (t + 1) * LANES] = both.astype(BF16)
        both = [jnp.where(rows_iota() < 4, plane[tile_rows(t + 1)], plane[tile_rows(t - 1)]) for plane in planes]
        both = jnp.concatenate(both, axis=0)
        out[at : at + 16, (t + 4) * LANES : (t + 5) * LANES] = both.astype(BF16)


def tile_rows(t):
    at = (4 if t < 0 else t) * TILE
    return slice(at, at + TILE)


def convolve(two, info, image, first, second, *refs):
    faces, edges_a, edges_b = refs[: 1 + two], refs[1 + two : 2 + 2 * two], refs[2 + 2 * two : 3 + 3 * two]
    matrix, part, stack, sums = refs[3 + 3 * two :]
    channels, rows_x = image.shape[0], image.shape[1]
    even = info[EVEN_X] == 1
    for xp in range(rows_x + 2):
        for c in range(0, channels, 2):
            planes = []
            if 0 < xp <= rows_x:
                ends = [ends_z(info, faces, xp - 1, c // 2)]
            else:
                ends = [ends_z(info, tiles, rows_x - 1 if xp == 0 else 0, c // 2) for tiles in (edges_a, edges_b)]
            for ch in (c, c + 1):
                tiles = [image_tile(info, *pair, ch) for pair in ends]
                if 0 < xp <= rows_x:
                    planes.append(jnp.concatenate([image[ch, xp - 1].astype(F32), tiles[0]], axis=0))
                else:
                    received = [
                        jnp.concatenate([ref[ch].astype(F32), tile], axis=0)
                        for ref, tile in zip((first, second), tiles)
                    ]
                    above, below = sides(even, *received)
                    plane, exists = (below, PREV_X) if xp == 0 else (above, NEXT_X)
                    planes.append(jnp.where(info[exists] == 1, plane, 0.0))
            at = (xp * channels + c) * TILE
            store_tiles(stack, at, planes)
    total = jnp.dot(matrix[0], stack[:, :512], preferred_element_type=F32)
    sums[...] = total + jnp.dot(matrix[1], stack[:, 512:], preferred_element_type=F32)
    lane = lanes_iota()
    for d in range(3):
        for x in range(rows_x):
            for t in range(4):
                cols = slice(t * LANES, (t + 1) * LANES)

                def piece(k):
                    at = ((k * 3 + d) * rows_x + x) * TILE
                    return sums[at : at + TILE, cols]

                before = jnp.where(lane > 0, pltpu.roll(piece(0), 1, 1), 0.0)
                after = jnp.where(lane < LANES - 1, pltpu.roll(piece(2), LANES - 1, 1), 0.0)
                part[d, x, tile_rows(t)] = piece(1) + before + after


def add_parts(two, info, part, other, logits, brick, *faces):
    rows_x, rows_z = part.shape[1], part.shape[2]
    for d in range(3):
        for x in range(rows_x):
            total = part[d, x] + other[d, x]
            logits[d, x] = total
            brick[d, x] = total.astype(BF16)
            for phase, face in enumerate(faces):
                even = info[EVEN_Z] != phase
                face[d, x] = jnp.where(even, total[rows_z - TILE :], total[:TILE]).astype(BF16)


def up(plane, dim):
    return pltpu.roll(plane, plane.shape[dim] - 1, dim)


def down(plane, dim):
    return pltpu.roll(plane, 1, dim)


def prepare(colours, two, info, planted, slope, likelihoods, first, second, *refs):
    faces, edges_a, edges_b = refs[: 1 + two], refs[1 + two : 2 + 2 * two], refs[2 + 2 * two : 3 + 3 * two]
    v0, free, field = refs[3 + 3 * two :]
    labels, rows_x, _, _ = slope.shape
    channels = 2 * labels
    even = info[EVEN_X] == 1

    def grown(index, source, l, tile):
        received = [
            jnp.concatenate([ref[index].astype(F32), tile(*ends_z(info, tiles, source, l))], axis=0)
            for ref, tiles in ((first, edges_a), (second, edges_b))
        ]
        return sides(even, *received)

    for x in range(rows_x):
        for l in range(labels):
            ends = ends_z(info, faces, x, l)
            rhs, full = fields(planted[x], likelihoods[l, x], slope[l, x], colours, info[COLOUR] + l)
            rhs = jnp.concatenate([rhs, rhs_tile(*ends)], axis=0)
            field[l, x + 1] = jnp.concatenate([full, full_tile(*ends)], axis=0)
            above, below = grown(channels + l * rows_x + x, x, l, rhs_tile)
            for at, plane in ((x + HALO, rhs), (x, below), (x + HALO + rows_x, above)):
                open_cell = plane < SEED / 2
                v0[l, at] = jnp.where(open_cell, plane, 0.0)
                if l == 0:
                    free[at] = jnp.where(open_cell, 1.0, 0.0)
    for l in range(labels):
        base = 2 * labels + labels * rows_x + 2 * l
        field[l, 0] = grown(base + 1, rows_x - 1, l, full_tile)[1]
        for r in range(2):
            field[l, rows_x + 1 + r] = grown(base + r, r, l, full_tile)[0]


def krylov(size_x, size_z, two, info, v0, free, logits, mine, other, *refs):
    faces, mine_edges, other_edges = (refs[n * (1 + two) : (n + 1) * (1 + two)] for n in range(3))
    v1, v2, slope_out, dots_out, weight, dots = refs[3 * (1 + two) :]
    labels, _, rows, _ = v0.shape
    rows_x, rows_z = logits.shape[1:3]
    is_up = info[UP] == 1
    z = rows_iota(rows)
    z = info[FIRST_Z] + jnp.where(z < rows_z + HALO, z, z - rows)
    inside_z = (z >= 0) & (z < size_z)
    in_z = jnp.where(inside_z, 1.0, 0.0)
    next_z = jnp.where(inside_z & (z < size_z - 1), 1.0, 0.0)
    in_zy = jnp.where(lanes_iota(rows) < LANES - 1, in_z, 0.0)
    for at in range(1, rows_x + 2 * HALO - 1):
        x = at - HALO
        place = info[FIRST_X] + x
        inside = (place >= 0) & (place < size_x)
        in_x = jnp.where(inside, 1.0, 0.0)
        next_x = jnp.where(inside & (place < size_x - 1), 1.0, 0.0)
        for d in range(3):
            def grown(plane, tiles, source):
                return jnp.concatenate([plane, rhs_tile(*ends_z(info, tiles, d, source))], axis=0)

            if 0 <= x < rows_x:
                plane = grown(logits[d, x], faces, x)
            else:
                source = x % rows_x
                here = grown(mine[d, source].astype(F32), mine_edges, source)
                there = grown(other[d, source].astype(F32), other_edges, source)
                plane = jnp.where(is_up, there, here) if x < 0 else jnp.where(is_up, here, there)
            squashed = 1.0 / (1.0 + jnp.exp(-plane))
            valid = (in_z * next_x, next_z * in_x, in_zy * in_x)[d]
            weight[d, at] = (0.05 + squashed) * valid
            if -1 <= x <= rows_x:
                slope_out[d, x + 1] = squashed * (1.0 - squashed) * valid

    def label(l, carry):
        def operate(v, start, stop):
            flow_before = weight[0, start - 1] * (v[l, start - 1] - v[l, start])
            for at in range(start, stop):
                here = v[l, at]
                flow = weight[0, at] * (here - v[l, at + 1])
                flow_z = weight[1, at] * (here - up(here, 0))
                flow_y = weight[2, at] * (here - up(here, 1))
                result = flow - flow_before + (flow_z - down(flow_z, 0)) + (flow_y - down(flow_y, 1))
                yield at, here, free[at] * result
                flow_before = flow

        for at, here, result in operate(v0, 2, rows_x + 2 * HALO - 1):
            v1[l, at] = result * (1.0 / SPREAD) - here
        for at, here, result in operate(v1, 3, rows_x + 2 * HALO - 2):
            v2[l, at] = result * (2.0 / SPREAD) - 2.0 * here - v0[l, at]
        sums = [jnp.zeros((TILE, LANES), F32)] * 6
        for at, here, result in operate(v2, HALO, HALO + rows_x):
            a, b = v0[l, at], v1[l, at]
            for n, product in enumerate((a * a, a * b, b * b, b * here, here * here, here * result)):
                for t in range(rows_z // TILE):
                    sums[n] = sums[n] + product[tile_rows(t)]
        for n in range(6):
            dots[pl.ds(n * labels + l, 1), :] = jnp.sum(sums[n], axis=0, keepdims=True)
        return carry

    lax.fori_loop(0, labels, label, 0)
    total = jnp.sum(dots[...], axis=1, keepdims=True)
    tile = jnp.zeros((TILE, LANES), F32)
    for n in range(6):
        column = total[tile_rows(n // 2)]
        column = jnp.broadcast_to(column, (TILE, LANES))
        tile = jnp.where(lanes_iota() == n, pltpu.roll(column, 4, 0) if n % 2 else column, tile)
    for n in range(dots_out.shape[0]):
        dots_out[n] = tile


def steps(g00, g01, g11, g12, g22, k22):
    g02 = 2.0 * g11 - g00
    k00 = SPREAD * (g00 + g01)
    k01 = SPREAD * (g01 + g11)
    k02 = SPREAD * (g02 + g12)
    k11 = SPREAD * (g11 + 0.5 * (g12 + g01))
    k12 = SPREAD * (g12 + 0.5 * (g22 + g02))
    alpha = g00 / k00
    c0 = alpha
    r0 = 1.0 - alpha * SPREAD
    r1 = -alpha * SPREAD
    rr = r0 * r0 * g00 + 2.0 * r0 * r1 * g01 + r1 * r1 * g11
    beta = rr / g00
    p0, p1 = r0 + beta, r1
    alpha = rr / (p0 * p0 * k00 + 2.0 * p0 * p1 * k01 + p1 * p1 * k11)
    c0, c1 = c0 + alpha * p0, alpha * p1
    r0 = r0 - alpha * SPREAD * (p0 + 0.5 * p1)
    r1 = r1 - alpha * SPREAD * (p0 + p1)
    r2 = -alpha * SPREAD * 0.5 * p1
    rr_next = r0 * r0 * g00 + r1 * r1 * g11 + r2 * r2 * g22
    rr_next = rr_next + 2.0 * (r0 * r1 * g01 + r0 * r2 * g02 + r1 * r2 * g12)
    beta = rr_next / rr
    p0, p1, p2 = r0 + beta * p0, r1 + beta * p1, r2
    curve = p0 * p0 * k00 + p1 * p1 * k11 + p2 * p2 * k22
    curve = curve + 2.0 * (p0 * p1 * k01 + p0 * p2 * k02 + p1 * p2 * k12)
    alpha = rr_next / curve
    return c0 + alpha * p0, c1 + alpha * p1, alpha * p2


def edges(info, parts, v0, v1, v2, field, out, lam):
    labels, _, rows, _ = v0.shape
    rows_x = out.shape[1] - 2
    total = jnp.sum(parts[...], axis=0)
    grams = [jnp.broadcast_to(total[:, n : n + 1], (TILE, LANES)) for n in range(6)]
    c0, c1, c2 = steps(*grams)
    for l in range(labels):
        s0, s1, s2 = (jnp.broadcast_to(c[l : l + 1], (rows, LANES)) for c in (c0, c1, c2))
        for at in range(rows_x + 3):
            source = at + HALO - 1
            lam[l, at] = s0 * v0[l, source] + s1 * v1[l, source] + s2 * v2[l, source]
    for at in range(rows_x + 2):
        sums = [jnp.zeros((rows, LANES), F32)] * 3
        for l in range(labels):
            a, b = lam[l, at], field[l, at]
            sums[0] = sums[0] - (a - lam[l, at + 1]) * (b - field[l, at + 1])
            sums[1] = sums[1] - (a - up(a, 0)) * (b - up(b, 0))
            sums[2] = sums[2] - (a - up(a, 1)) * (b - up(b, 1))
        for d in range(3):
            out[d, at] = sums[d]


def logit_grads(edge, other, slope, xp):
    lane = lanes_iota(edge.shape[2])
    shifted = [[], [], []]
    for d in range(3):
        plane = ((edge[d, xp] + other[d, xp]) * slope[d, xp]).astype(BF16).astype(F32)
        shifted[0].append(jnp.where(lane < LANES - 1, up(plane, 1), 0.0))
        shifted[1].append(plane)
        shifted[2].append(jnp.where(lane > 0, down(plane, 1), 0.0))
    return shifted[0] + shifted[1] + shifted[2]


def filter_sums(info, edge, other, slope, stack, out, own, products, rows_out):
    rows_x = edge.shape[1] - 2
    for x in range(rows_x):
        planes = logit_grads(edge, other, slope, x + 1)
        planes.append(jnp.zeros_like(planes[0]))
        for pair in range(5):
            at = (x * 16 + 2 * pair) * TILE
            for t in range(4):
                both = jnp.concatenate([plane[tile_rows(t)] for plane in planes[2 * pair : 2 * pair + 2]], axis=0)
                own[at : at + 16, t * LANES : (t + 1) * LANES] = both.astype(BF16)
        own[(x * 16 + 10) * TILE : (x + 1) * 16 * TILE, :] = jnp.zeros((6 * TILE, 4 * LANES), BF16)
    for n in range(2):
        products[n] = lax.dot_general(
            own[...], stack[:, 512 * n : 512 * (n + 1)], (((1,), (1,)), ((), ())), preferred_element_type=F32
        )
    rows_out[...] = jnp.zeros_like(rows_out)
    masks = {(h, j, o): band(h, j, o) for o in (-1, 0, 1) for h in range(2) for j in bands(o)}
    for kd in range(9):
        k, d = kd // 3, kd % 3
        for i in range(3):
            for j in range(3):
                total = jnp.zeros((TILE, LANES), F32)
                for o in (-1, 0, 1):
                    if j in bands(o):
                        for x in range(rows_x):
                            at = (x * 16 + kd) * TILE
                            col = (x + i) // 2 * LANES
                            piece = products[abs(o), at : at + TILE, col : col + LANES]
                            total = total + jnp.where(masks[(x + i) % 2, j, o], piece, 0.0)
                row = d * 27 + i * 9 + j * 3 + k
                rows_out[row : row + 1] = jnp.sum(total, axis=0, keepdims=True)
    sums = lax.dot_general(
        jnp.where(((lanes_iota() >> 3) & 7) == rows_iota(), 1.0, 0.0),
        rows_out[...],
        (((1,), (1,)), ((), ())),
        precision=lax.Precision.HIGHEST,
        preferred_element_type=F32,
    )
    for n in range(out.shape[0]):
        out[n] = sums


def image_sums(info, edge, other, slope, matrix, out, grads, sums):
    for xp in range(edge.shape[1]):
        planes = logit_grads(edge, other, slope, xp)
        planes += [jnp.zeros_like(planes[0])] * 7
        for pair in range(8):
            store_tiles(grads, (xp * 16 + 2 * pair) * TILE, planes[2 * pair : 2 * pair + 2])
    total = jnp.dot(matrix[0], grads[:, :512], preferred_element_type=F32)
    sums[...] = total + jnp.dot(matrix[1], grads[:, 512:], preferred_element_type=F32)
    channels, rows_x, rows_z, _ = out.shape
    for c in range(channels):
        for x in range(rows_x):
            at = (c * rows_x + x) * TILE
            for t in range(0, rows_z // TILE, 2):
                both = [sums[at : at + TILE, s * LANES : (s + 1) * LANES] for s in (t, t + 1)]
                out[c, x, t * TILE : (t + 2) * TILE] = jnp.concatenate(both, axis=0).astype(BF16)


def local(image, filt, planted, likelihoods, slope):
    channels = image.shape[0]
    labels, rows_x, rows_z, rows_y = likelihoods.shape
    if (channels, labels, rows_x, rows_z, rows_y) != (8, 4, HALO, 4 * TILE, LANES):
        raise ValueError("brick size")
    lab, xy, gz = lax.axis_index("lab"), lax.axis_index("xy"), lax.axis_index("gz")
    colours = labels * lax.axis_size("lab")
    size_x, size_z = rows_x * lax.axis_size("xy"), rows_z * lax.axis_size("gz")
    rows = rows_z + TILE
    two = lax.axis_size("gz") > 2
    phases = range(1 + two)
    members = lax.axis_size("xy") * lax.axis_size("gz")
    info = jnp.stack(
        [
            1 - xy % 2,
            1 - gz % 2,
            xy * rows_x,
            gz * rows_z,
            lab * labels,
            1 - (xy + lab) % 2,
            jnp.minimum(xy, 1),
            jnp.minimum(lax.axis_size("xy") - 1 - xy, 1),
            jnp.minimum(gz, 1),
            jnp.minimum(lax.axis_size("gz") - 1 - gz, 1),
        ]
    ).astype(jnp.int32)

    inputs = (image, planted, likelihoods, slope)
    planes = channels + labels * rows_x + 2 * labels
    brick = shaped((planes, rows_z, LANES), BF16)
    taps = jnp.transpose(filt, (0, 2, 3, 4, 1))
    matrix, back_matrix, image, planted, likelihoods, slope, *packed = call(
        functools.partial(pack, colours, two),
        [shaped((2, 288, 384), BF16), shaped((2, 256, 768), BF16)]
        + [shaped(a.shape, a.dtype) for a in inputs]
        + [shaped((rows_x, labels, TILE, LANES), BF16)] * (1 + two)
        + [brick, brick],
        info,
        *(pltpu.with_memory_space_constraint(a, pltpu.HBM) for a in (taps, *inputs)),
        scratch=[
            pltpu.VMEM(taps.shape, BF16),
            pltpu.VMEM((112, LANES), F32),
            pltpu.SemaphoreType.DMA((5,)),
        ],
        name="pack",
        space=pltpu.HBM,
    )
    send_a, send_b = packed[1 + two :]
    faces = [z_swap(packed[phase], phase) for phase in phases]
    edges_a = [diagonal_swap(packed[phase], 0, phase) for phase in phases]
    edges_b = [diagonal_swap(packed[phase], 1, phase) for phase in phases]
    second = x_swap(send_b, 1)
    first = x_swap(send_a, 0)
    received = (first, second, *faces, *edges_a, *edges_b)

    part, stack = call(
        functools.partial(convolve, two),
        [shaped((3, rows_x, rows_z, LANES), F32), shaped((384, 1024), BF16)],
        info,
        image,
        *received,
        matrix,
        scratch=[pltpu.VMEM((288, 512), F32)],
        name="convolve",
    )
    logits, own, *sends = call(
        functools.partial(add_parts, two),
        [shaped(part.shape, F32), shaped(part.shape, BF16)]
        + [shaped((3, rows_x, TILE, LANES), BF16)] * (1 + two),
        info,
        part,
        lab_swap(part),
        name="add_parts",
    )
    mine = split_swap(own)
    mine_edges = [split_diagonal_swap(sends[phase], phase) for phase in phases]
    logit_faces = [z_swap(sends[phase], phase) for phase in phases]
    mine, mine_edges, logit_faces = lax.optimization_barrier((mine, mine_edges, logit_faces))
    other = lab_swap(mine)
    other_edges = [lab_swap(block) for block in mine_edges]
    extended = (labels, rows_x + 2 * HALO, rows, LANES)
    ring = shaped((3, rows_x + 2, rows, LANES), F32)
    v0, free, field = call(
        functools.partial(prepare, colours, two),
        [shaped(extended, F32), shaped(extended[1:], F32), shaped((labels, rows_x + 3, rows, LANES), F32)],
        info,
        planted,
        slope,
        likelihoods,
        *received,
        name="prepare",
    )
    v1, v2, squash_slope, dots = call(
        functools.partial(krylov, size_x, size_z, two),
        [shaped(extended, F32)] * 2 + [ring, shaped((members, TILE, LANES), F32)],
        info,
        v0,
        free,
        logits,
        mine,
        other,
        *logit_faces,
        *mine_edges,
        *other_edges,
        scratch=[pltpu.VMEM((3,) + extended[1:], F32), pltpu.VMEM((6 * labels, LANES), F32)],
        name="krylov",
    )
    edge = call(
        edges,
        ring,
        info,
        everyones(dots, ("xy", "gz")),
        v0,
        v1,
        v2,
        field,
        scratch=[pltpu.VMEM((labels, rows_x + 3, rows, LANES), F32)],
        name="edges",
    )
    other_edge = lab_swap(edge)
    sums = call(
        filter_sums,
        shaped((members, TILE, LANES), F32),
        info,
        edge,
        other_edge,
        squash_slope,
        stack,
        scratch=[
            pltpu.VMEM((512, 512), BF16),
            pltpu.VMEM((2, 512, 384), F32),
            pltpu.VMEM((LANES, LANES), F32),
        ],
        name="filter_sums",
    )
    grad_image = call(
        image_sums,
        shaped(image.shape, BF16),
        info,
        edge,
        other_edge,
        squash_slope,
        back_matrix,
        scratch=[pltpu.VMEM((768, 1024), BF16), pltpu.VMEM((256, 512), F32)],
        flops=10_000_000,
        name="image_sums",
    )
    grad_filter = jnp.sum(everyones(sums, ("xy", "gz")), axis=0)
    grad_filter = grad_filter[:, :81].reshape(channels, 3, 27)
    return grad_image, jnp.transpose(grad_filter, (1, 0, 2)).reshape(3, channels, 3, 3, 3)


def solution(mesh):
    return jax.shard_map(
        local,
        mesh=mesh,
        in_specs=(
            P("lab", ("crops", "xy"), "gz", None),
            P(),
            P(("crops", "xy"), "gz", None),
            P("lab", ("crops", "xy"), "gz", None),
            P("lab", ("crops", "xy"), "gz", None),
        ),
        out_specs=(P("lab", ("crops", "xy"), "gz", None), P("crops", "lab", None, None, None)),
        check_vma=False,
    )
```

```python
import functools

import jax
import jax.numpy as jnp
from jax import lax
from jax.experimental import pallas as pl
from jax.experimental.pallas import tpu as pltpu
from jax.sharding import PartitionSpec as P

HALO = 4
SEED = 64.0
SPREAD = 6.3
TILE = 8
LANES = 128
BF16, F32 = jnp.bfloat16, jnp.float32
EVEN_X, EVEN_Z, FIRST_X, FIRST_Z, COLOUR, UP, PREV_X, NEXT_X, PREV_Z, NEXT_Z = range(10)


SWAP_AXES = ("xy", "gz", "lab")


def mate(place, phase, count):
    other = place + 1 if (place - phase) % 2 == 0 else place - 1
    return other if phase <= min(place, other) and max(place, other) < count else None


def swap(block, partner):
    sizes = [lax.axis_size(axis) for axis in SWAP_AXES]
    devices = [(x, z, lab) for x in range(sizes[0]) for z in range(sizes[1]) for lab in range(sizes[2])]
    pairs = {}
    for device in devices:
        if partner(*device) is not None:
            pairs[device] = partner(*device)
    for other_of in (lambda x, z, lab: (x, z, lab ^ 1), lambda x, z, lab: (x, z ^ 1, lab)):
        for device in devices:
            other = other_of(*device)
            if device not in pairs and other in devices and other not in pairs:
                pairs[device], pairs[other] = other, device

    def flat(x, z, lab):
        return (x * sizes[1] + z) * sizes[2] + lab

    return lax.ppermute(block, SWAP_AXES, [(flat(*src), flat(*dst)) for src, dst in sorted(pairs.items())])


def x_swap(block, phase):
    count = lax.axis_size("xy")

    def partner(x, z, lab):
        other = mate(x, phase, count)
        return None if other is None else (other, z, lab)

    return swap(block, partner)


def z_swap(block, phase):
    count = lax.axis_size("gz")

    def partner(x, z, lab):
        other = mate(z, phase, count)
        return None if other is None else (x, other, lab)

    return swap(block, partner)


def diagonal_swap(block, x_phase, z_phase):
    counts = lax.axis_size("xy"), lax.axis_size("gz")

    def partner(x, z, lab):
        others = mate(x, x_phase, counts[0]), mate(z, z_phase, counts[1])
        return None if None in others else (*others, lab)

    return swap(block, partner)


def lab_swap(block):
    return lax.ppermute(block, "lab", [(0, 1), (1, 0)])


def split_swap(block):
    count = lax.axis_size("xy")

    def partner(x, z, lab):
        other = mate(x, lab % 2, count)
        return None if other is None else (other, z, lab)

    return swap(block, partner)


def split_diagonal_swap(block, z_phase):
    counts = lax.axis_size("xy"), lax.axis_size("gz")

    def partner(x, z, lab):
        others = mate(x, lab % 2, counts[0]), mate(z, z_phase, counts[1])
        return None if None in others else (*others, lab)

    return swap(block, partner)


def everyones(copies, axes):
    return lax.all_to_all(copies, axes, 0, 0)


def call(kernel, outs, *ins, scratch=(), flops=1_000_000, name=None, space=pltpu.VMEM):
    specs = [pl.BlockSpec(memory_space=pltpu.SMEM)]
    specs += [pl.BlockSpec(memory_space=space)] * (len(ins) - 1)
    bytes_moved = sum(a.size * a.dtype.itemsize for a in ins)
    return pl.pallas_call(
        kernel,
        out_shape=outs,
        in_specs=specs,
        out_specs=jax.tree.map(lambda _: pl.BlockSpec(memory_space=pltpu.VMEM), outs),
        scratch_shapes=list(scratch),
        compiler_params=pltpu.CompilerParams(vmem_limit_bytes=40 * 2**20),
        cost_estimate=pl.CostEstimate(flops=flops, bytes_accessed=bytes_moved, transcendentals=0),
        name=name,
    )(*ins)


def shaped(shape, dtype):
    return jax.ShapeDtypeStruct(shape, dtype)


def rows_iota(rows=TILE):
    return lax.broadcasted_iota(jnp.int32, (rows, LANES), 0)


def lanes_iota(rows=TILE):
    return lax.broadcasted_iota(jnp.int32, (rows, LANES), 1)


def fields(planted, likelihood, slope, colours, colour):
    free = planted >= colours
    member = jnp.where(planted == colour, 1.0, 0.0)
    return jnp.where(free, slope, SEED), jnp.where(free, likelihood, member)


def pack(
    colours,
    two,
    info,
    filt_in,
    image_in,
    planted_in,
    likelihoods_in,
    slope_in,
    wide_out,
    back_out,
    image,
    planted,
    likelihoods,
    slope,
    *refs,
):
    faces, (send_a, send_b, filt, taps, sems) = refs[: 1 + two], refs[1 + two :]
    pairs = (
        (planted_in, planted),
        (slope_in, slope),
        (likelihoods_in, likelihoods),
        (image_in, image),
        (filt_in, filt),
    )
    copies = [pltpu.make_async_copy(src, dst, sems.at[n]) for n, (src, dst) in enumerate(pairs)]
    for copy in reversed(copies):
        copy.start()
    copies[4].wait()
    spread_filter(info, filt, taps, wide_out, back_out)
    labels, rows_x, rows_z, _ = likelihoods.shape
    channels = image.shape[0]
    last, first = slice(rows_z - TILE, rows_z), slice(0, TILE)
    even = info[EVEN_X] == 1
    high, low = jnp.where(even, rows_x - 1, 0), jnp.where(even, 0, rows_x - 1)
    copies[0].wait()
    copies[1].wait()
    for x in range(rows_x):
        for l in range(labels):
            rhs = jnp.where(planted[x] >= colours, slope[l, x], SEED).astype(BF16)
            send_a[channels + l * rows_x + x] = rhs
            send_b[channels + l * rows_x + x] = rhs
    copies[2].wait()
    for l in range(labels):
        for send, at in ((send_a, high), (send_b, low)):
            for r in range(2):
                x = jnp.where(at == 0, 0, rows_x - 2) + r
                _, full = fields(planted[x], likelihoods[l, x], slope[l, x], colours, info[COLOUR] + l)
                send[channels + labels * rows_x + 2 * l + r] = full.astype(BF16)
    copies[3].wait()
    for c in range(channels):
        send_a[c] = image[c, high]
        send_b[c] = image[c, low]
    for phase, out in enumerate(faces):
        even = info[EVEN_Z] != phase
        place = (rows_iota() + jnp.where(even, 0, 4)) & 7

        def channel(c, x):
            return jnp.where(even, image[c, x, last].astype(F32), image[c, x, first].astype(F32))

        def turned(tile, for_even, for_odd):
            return jnp.where(even, pltpu.roll(tile, for_even, 0), pltpu.roll(tile, for_odd, 0))

        for x in range(rows_x):
            seeds = jnp.where(even, planted[x, last], planted[x, first])
            for l in range(labels):
                ends = [jnp.where(even, ref[l, x, last], ref[l, x, first]) for ref in (likelihoods, slope)]
                rhs, full = fields(seeds, *ends, colours, info[COLOUR] + l)
                first_channel = turned(channel(2 * l, x), 3, 6)
                second_channel = turned(channel(2 * l + 1, x), 4, 7)
                rest = jnp.where(place == 2, first_channel, second_channel)
                rest = jnp.where(place < 2, turned(full, 2, 4), rest)
                out[x, l] = jnp.where(place >= 4, rhs, rest).astype(BF16)


def sides(even, first, second):
    if second is None:
        return jnp.where(even, first, 0.0), jnp.where(even, 0.0, first)
    return jnp.where(even, first, second), jnp.where(even, second, first)


def ends_z(info, tiles, x, l):
    both = [ref[x, l].astype(F32) for ref in tiles]
    return sides(info[EVEN_Z] == 1, both[0], both[1] if len(both) > 1 else None)


def rhs_tile(above, below):
    return jnp.where(rows_iota() < 4, above, below)


def full_tile(above, below):
    return jnp.where(rows_iota() < 4, pltpu.roll(above, 4, 0), pltpu.roll(below, 6, 0))


def image_tile(info, above, below, c):
    up, down = (2, 5) if c % 2 == 0 else (1, 4)
    above = jnp.where(info[NEXT_Z] == 1, above, 0.0)
    below = jnp.where(info[PREV_Z] == 1, below, 0.0)
    return jnp.where(rows_iota() < 4, pltpu.roll(above, up, 0), pltpu.roll(below, down, 0))


def band(half, j, o, transposed=False):
    z, lane = rows_iota(), lanes_iota()
    other = lane & 7
    at = (z + 1 - other - 8 * o) if transposed else (other + 8 * o - z + 1)
    mask = at == j
    if half is not None:
        mask = mask & ((lane >> 6) == half)
    return mask


def bands(o, transposed=False):
    if o == 0:
        return (0, 1, 2)
    return (0,) if (o < 0) != transposed else (2,)


def spread_filter(info, filt, taps, wide_out, back_out):
    taps[...] = jnp.zeros_like(taps)
    for d in range(3):
        for i in range(3):
            for j in range(3):
                at = (d * 9 + i * 3 + j) * 4
                taps[at : at + 3, : filt.shape[-1]] = filt[d, i, j].astype(F32)
    lane = lanes_iota(LANES)
    channel = rows_iota(LANES) - 2 * info[COLOUR]
    all_taps = taps[...].astype(BF16)
    by_channel = jnp.where(channel == ((lane >> 3) & 7), 1.0, 0.0).astype(BF16)
    own = jnp.dot(
        all_taps, jnp.where(channel == lane, 1.0, 0.0).astype(BF16), preferred_element_type=F32
    ).astype(BF16)
    wide = jnp.dot(all_taps, by_channel, preferred_element_type=F32)
    tap, edge = rows_iota(taps.shape[0]), lanes_iota(taps.shape[0]) >> 3
    shift = jnp.where(edge >= 3, 1, 0) + jnp.where(edge >= 6, 1, 0)
    first_tap = jnp.where(edge < 9, (edge - 3 * shift) * 36 + shift, -LANES)
    places = [jnp.where(tap == first_tap + 4 * ij, 1.0, 0.0).astype(BF16) for ij in range(9)]
    back = [
        lax.dot_general(own, place, (((0,), (0,)), ((), ())), preferred_element_type=F32) for place in places
    ]
    zero = jnp.zeros((TILE, LANES), F32)
    for at_out, distances in enumerate(((0,), (-1, 1))):
        cases = [(o, j) for o in distances for j in bands(o)]
        masks = {(h, j): band(h, j, o) for h in range(2) for o, j in cases}
        for kd in range(9):
            for pair in range(2):
                for block in range(3):
                    tiles = []
                    for x in (2 * pair, 2 * pair + 1):
                        tile = zero
                        for i in range(3):
                            if (x + i) // 2 == block:
                                for _, j in cases:
                                    row = (kd % 3 * 9 + i * 3 + j) * 4 + kd // 3
                                    value = jnp.broadcast_to(wide[row : row + 1], (TILE, LANES))
                                    tile = jnp.where(masks[(x + i) % 2, j], value, tile)
                        tiles.append(tile)
                    at = (kd * 4 + 2 * pair) * TILE
                    wide_out[at_out, at : at + 16, block * LANES : (block + 1) * LANES] = jnp.concatenate(
                        tiles, axis=0
                    ).astype(BF16)
        cases = [(o, j) for o in distances for j in bands(o, True)]
        masks = {j: band(None, j, o, True) for o, j in cases}
        for c in range(8):
            for pair in range(2):
                for block in range(6):
                    tiles = []
                    for x in (2 * pair, 2 * pair + 1):
                        tile = zero
                        i = x + 2 - block
                        if 0 <= i < 3:
                            for _, j in cases:
                                value = jnp.broadcast_to(back[i * 3 + j][c : c + 1], (TILE, LANES))
                                tile = jnp.where(masks[j], value, tile)
                        tiles.append(tile)
                    at = (c * 4 + 2 * pair) * TILE
                    back_out[at_out, at : at + 16, block * LANES : (block + 1) * LANES] = jnp.concatenate(
                        tiles, axis=0
                    ).astype(BF16)


def store_tiles(out, at, planes):
    for t in range(4):
        both = jnp.concatenate([plane[tile_rows(t)] for plane in planes], axis=0)
        out[at : at + 16, t * LANES : (t + 1) * LANES] = both.astype(BF16)
        both = [jnp.where(rows_iota() < 4, plane[tile_rows(t + 1)], plane[tile_rows(t - 1)]) for plane in planes]
        both = jnp.concatenate(both, axis=0)
        out[at : at + 16, (t + 4) * LANES : (t + 5) * LANES] = both.astype(BF16)


def tile_rows(t):
    at = (4 if t < 0 else t) * TILE
    return slice(at, at + TILE)


def convolve(two, info, image, first, second, *refs):
    faces, edges_a, edges_b = refs[: 1 + two], refs[1 + two : 2 + 2 * two], refs[2 + 2 * two : 3 + 3 * two]
    matrix, part, stack, sums = refs[3 + 3 * two :]
    channels, rows_x = image.shape[0], image.shape[1]
    even = info[EVEN_X] == 1
    for xp in range(rows_x + 2):
        for c in range(0, channels, 2):
            planes = []
            if 0 < xp <= rows_x:
                ends = [ends_z(info, faces, xp - 1, c // 2)]
            else:
                ends = [ends_z(info, tiles, rows_x - 1 if xp == 0 else 0, c // 2) for tiles in (edges_a, edges_b)]
            for ch in (c, c + 1):
                tiles = [image_tile(info, *pair, ch) for pair in ends]
                if 0 < xp <= rows_x:
                    planes.append(jnp.concatenate([image[ch, xp - 1].astype(F32), tiles[0]], axis=0))
                else:
                    received = [
                        jnp.concatenate([ref[ch].astype(F32), tile], axis=0)
                        for ref, tile in zip((first, second), tiles)
                    ]
                    above, below = sides(even, *received)
                    plane, exists = (below, PREV_X) if xp == 0 else (above, NEXT_X)
                    planes.append(jnp.where(info[exists] == 1, plane, 0.0))
            at = (xp * channels + c) * TILE
            store_tiles(stack, at, planes)
    total = jnp.dot(matrix[0], stack[:, :512], preferred_element_type=F32)
    sums[...] = total + jnp.dot(matrix[1], stack[:, 512:], preferred_element_type=F32)
    lane = lanes_iota()
    for d in range(3):
        for x in range(rows_x):
            for t in range(4):
                cols = slice(t * LANES, (t + 1) * LANES)

                def piece(k):
                    at = ((k * 3 + d) * rows_x + x) * TILE
                    return sums[at : at + TILE, cols]

                before = jnp.where(lane > 0, pltpu.roll(piece(0), 1, 1), 0.0)
                after = jnp.where(lane < LANES - 1, pltpu.roll(piece(2), LANES - 1, 1), 0.0)
                part[d, x, tile_rows(t)] = piece(1) + before + after


def add_parts(two, info, part, other, logits, brick, *faces):
    rows_x, rows_z = part.shape[1], part.shape[2]
    for d in range(3):
        for x in range(rows_x):
            total = part[d, x] + other[d, x]
            logits[d, x] = total
            brick[d, x] = total.astype(BF16)
            for phase, face in enumerate(faces):
                even = info[EVEN_Z] != phase
                face[d, x] = jnp.where(even, total[rows_z - TILE :], total[:TILE]).astype(BF16)


def up(plane, dim):
    return pltpu.roll(plane, plane.shape[dim] - 1, dim)


def down(plane, dim):
    return pltpu.roll(plane, 1, dim)


def prepare(colours, two, info, planted, slope, likelihoods, first, second, *refs):
    faces, edges_a, edges_b = refs[: 1 + two], refs[1 + two : 2 + 2 * two], refs[2 + 2 * two : 3 + 3 * two]
    v0, free, field = refs[3 + 3 * two :]
    labels, rows_x, _, _ = slope.shape
    channels = 2 * labels
    even = info[EVEN_X] == 1

    def grown(index, source, l, tile):
        received = [
            jnp.concatenate([ref[index].astype(F32), tile(*ends_z(info, tiles, source, l))], axis=0)
            for ref, tiles in ((first, edges_a), (second, edges_b))
        ]
        return sides(even, *received)

    for x in range(rows_x):
        for l in range(labels):
            ends = ends_z(info, faces, x, l)
            rhs, full = fields(planted[x], likelihoods[l, x], slope[l, x], colours, info[COLOUR] + l)
            rhs = jnp.concatenate([rhs, rhs_tile(*ends)], axis=0)
            field[l, x + 1] = jnp.concatenate([full, full_tile(*ends)], axis=0)
            above, below = grown(channels + l * rows_x + x, x, l, rhs_tile)
            for at, plane in ((x + HALO, rhs), (x, below), (x + HALO + rows_x, above)):
                open_cell = plane < SEED / 2
                v0[l, at] = jnp.where(open_cell, plane, 0.0)
                if l == 0:
                    free[at] = jnp.where(open_cell, 1.0, 0.0)
    for l in range(labels):
        base = 2 * labels + labels * rows_x + 2 * l
        field[l, 0] = grown(base + 1, rows_x - 1, l, full_tile)[1]
        for r in range(2):
            field[l, rows_x + 1 + r] = grown(base + r, r, l, full_tile)[0]


def krylov(size_x, size_z, two, info, v0, free, logits, mine, other, *refs):
    faces, mine_edges, other_edges = (refs[n * (1 + two) : (n + 1) * (1 + two)] for n in range(3))
    v1, v2, slope_out, dots_out, weight, dots = refs[3 * (1 + two) :]
    labels, _, rows, _ = v0.shape
    rows_x, rows_z = logits.shape[1:3]
    is_up = info[UP] == 1
    z = rows_iota(rows)
    z = info[FIRST_Z] + jnp.where(z < rows_z + HALO, z, z - rows)
    inside_z = (z >= 0) & (z < size_z)
    in_z = jnp.where(inside_z, 1.0, 0.0)
    next_z = jnp.where(inside_z & (z < size_z - 1), 1.0, 0.0)
    in_zy = jnp.where(lanes_iota(rows) < LANES - 1, in_z, 0.0)
    for at in range(1, rows_x + 2 * HALO - 1):
        x = at - HALO
        place = info[FIRST_X] + x
        inside = (place >= 0) & (place < size_x)
        in_x = jnp.where(inside, 1.0, 0.0)
        next_x = jnp.where(inside & (place < size_x - 1), 1.0, 0.0)
        for d in range(3):
            def grown(plane, tiles, source):
                return jnp.concatenate([plane, rhs_tile(*ends_z(info, tiles, d, source))], axis=0)

            if 0 <= x < rows_x:
                plane = grown(logits[d, x], faces, x)
            else:
                source = x % rows_x
                here = grown(mine[d, source].astype(F32), mine_edges, source)
                there = grown(other[d, source].astype(F32), other_edges, source)
                plane = jnp.where(is_up, there, here) if x < 0 else jnp.where(is_up, here, there)
            squashed = 1.0 / (1.0 + jnp.exp(-plane))
            valid = (in_z * next_x, next_z * in_x, in_zy * in_x)[d]
            edge_weight = (0.05 + squashed) * valid
            weight[d, at] = edge_weight
            if d > 0:
                weight[2 + d, at] = down(edge_weight, d - 1)
            if -1 <= x <= rows_x:
                slope_out[d, x + 1] = squashed * (1.0 - squashed) * valid

    def label(l, carry):
        def operate(v, start, stop):
            flow_before = weight[0, start - 1] * (v[l, start - 1] - v[l, start])
            for at in range(start, stop):
                here = v[l, at]
                flow = weight[0, at] * (here - v[l, at + 1])
                result = flow - flow_before
                for dim in range(2):
                    result = result + weight[1 + dim, at] * (here - up(here, dim))
                    result = result + weight[3 + dim, at] * (here - down(here, dim))
                yield at, here, free[at] * result
                flow_before = flow

        for at, here, result in operate(v0, 2, rows_x + 2 * HALO - 1):
            v1[l, at] = result * (1.0 / SPREAD) - here
        for at, here, result in operate(v1, 3, rows_x + 2 * HALO - 2):
            v2[l, at] = result * (2.0 / SPREAD) - 2.0 * here - v0[l, at]
        sums = [jnp.zeros((TILE, LANES), F32)] * 6
        for at, here, result in operate(v2, HALO, HALO + rows_x):
            a, b = v0[l, at], v1[l, at]
            for n, product in enumerate((a * a, a * b, b * b, b * here, here * here, here * result)):
                for t in range(rows_z // TILE):
                    sums[n] = sums[n] + product[tile_rows(t)]
        for n in range(6):
            dots[pl.ds(n * labels + l, 1), :] = jnp.sum(sums[n], axis=0, keepdims=True)
        return carry

    lax.fori_loop(0, labels, label, 0)
    total = jnp.sum(dots[...], axis=1, keepdims=True)
    tile = jnp.zeros((TILE, LANES), F32)
    for n in range(6):
        column = total[tile_rows(n // 2)]
        column = jnp.broadcast_to(column, (TILE, LANES))
        tile = jnp.where(lanes_iota() == n, pltpu.roll(column, 4, 0) if n % 2 else column, tile)
    for n in range(dots_out.shape[0]):
        dots_out[n] = tile


def steps(g00, g01, g11, g12, g22, k22):
    g02 = 2.0 * g11 - g00
    k00 = SPREAD * (g00 + g01)
    k01 = SPREAD * (g01 + g11)
    k02 = SPREAD * (g02 + g12)
    k11 = SPREAD * (g11 + 0.5 * (g12 + g01))
    k12 = SPREAD * (g12 + 0.5 * (g22 + g02))
    alpha = g00 / k00
    c0 = alpha
    r0 = 1.0 - alpha * SPREAD
    r1 = -alpha * SPREAD
    rr = r0 * r0 * g00 + 2.0 * r0 * r1 * g01 + r1 * r1 * g11
    beta = rr / g00
    p0, p1 = r0 + beta, r1
    alpha = rr / (p0 * p0 * k00 + 2.0 * p0 * p1 * k01 + p1 * p1 * k11)
    c0, c1 = c0 + alpha * p0, alpha * p1
    r0 = r0 - alpha * SPREAD * (p0 + 0.5 * p1)
    r1 = r1 - alpha * SPREAD * (p0 + p1)
    r2 = -alpha * SPREAD * 0.5 * p1
    rr_next = r0 * r0 * g00 + r1 * r1 * g11 + r2 * r2 * g22
    rr_next = rr_next + 2.0 * (r0 * r1 * g01 + r0 * r2 * g02 + r1 * r2 * g12)
    beta = rr_next / rr
    p0, p1, p2 = r0 + beta * p0, r1 + beta * p1, r2
    curve = p0 * p0 * k00 + p1 * p1 * k11 + p2 * p2 * k22
    curve = curve + 2.0 * (p0 * p1 * k01 + p0 * p2 * k02 + p1 * p2 * k12)
    alpha = rr_next / curve
    return c0 + alpha * p0, c1 + alpha * p1, alpha * p2


def edges(info, parts, v0, v1, v2, field, out, lam):
    labels, _, rows, _ = v0.shape
    rows_x = out.shape[1] - 2
    total = jnp.sum(parts[...], axis=0)
    grams = [jnp.broadcast_to(total[:, n : n + 1], (TILE, LANES)) for n in range(6)]
    c0, c1, c2 = steps(*grams)
    for l in range(labels):
        s0, s1, s2 = (jnp.broadcast_to(c[l : l + 1], (rows, LANES)) for c in (c0, c1, c2))
        for at in range(rows_x + 3):
            source = at + HALO - 1
            lam[l, at] = s0 * v0[l, source] + s1 * v1[l, source] + s2 * v2[l, source]
    for at in range(rows_x + 2):
        sums = [jnp.zeros((rows, LANES), F32)] * 3
        for l in range(labels):
            a, b = lam[l, at], field[l, at]
            sums[0] = sums[0] - (a - lam[l, at + 1]) * (b - field[l, at + 1])
            sums[1] = sums[1] - (a - up(a, 0)) * (b - up(b, 0))
            sums[2] = sums[2] - (a - up(a, 1)) * (b - up(b, 1))
        for d in range(3):
            out[d, at] = sums[d]


def logit_grads(edge, other, slope, xp):
    lane = lanes_iota(edge.shape[2])
    shifted = [[], [], []]
    for d in range(3):
        plane = ((edge[d, xp] + other[d, xp]) * slope[d, xp]).astype(BF16).astype(F32)
        shifted[0].append(jnp.where(lane < LANES - 1, up(plane, 1), 0.0))
        shifted[1].append(plane)
        shifted[2].append(jnp.where(lane > 0, down(plane, 1), 0.0))
    return shifted[0] + shifted[1] + shifted[2]


def filter_sums(info, edge, other, slope, stack, out, own, products, rows_out):
    rows_x = edge.shape[1] - 2
    for x in range(rows_x):
        planes = logit_grads(edge, other, slope, x + 1)
        planes.append(jnp.zeros_like(planes[0]))
        for pair in range(5):
            at = (x * 16 + 2 * pair) * TILE
            for t in range(4):
                both = jnp.concatenate([plane[tile_rows(t)] for plane in planes[2 * pair : 2 * pair + 2]], axis=0)
                own[at : at + 16, t * LANES : (t + 1) * LANES] = both.astype(BF16)
        own[(x * 16 + 10) * TILE : (x + 1) * 16 * TILE, :] = jnp.zeros((6 * TILE, 4 * LANES), BF16)
    for n in range(2):
        products[n] = lax.dot_general(
            own[...], stack[:, 512 * n : 512 * (n + 1)], (((1,), (1,)), ((), ())), preferred_element_type=F32
        )
    rows_out[...] = jnp.zeros_like(rows_out)
    masks = {(h, j, o): band(h, j, o) for o in (-1, 0, 1) for h in range(2) for j in bands(o)}
    for kd in range(9):
        k, d = kd // 3, kd % 3
        for i in range(3):
            for j in range(3):
                total = jnp.zeros((TILE, LANES), F32)
                for o in (-1, 0, 1):
                    if j in bands(o):
                        for x in range(rows_x):
                            at = (x * 16 + kd) * TILE
                            col = (x + i) // 2 * LANES
                            piece = products[abs(o), at : at + TILE, col : col + LANES]
                            total = total + jnp.where(masks[(x + i) % 2, j, o], piece, 0.0)
                row = d * 27 + i * 9 + j * 3 + k
                rows_out[row : row + 1] = jnp.sum(total, axis=0, keepdims=True)
    sums = lax.dot_general(
        jnp.where(((lanes_iota() >> 3) & 7) == rows_iota(), 1.0, 0.0),
        rows_out[...],
        (((1,), (1,)), ((), ())),
        precision=lax.Precision.HIGHEST,
        preferred_element_type=F32,
    )
    for n in range(out.shape[0]):
        out[n] = sums


def image_sums(info, edge, other, slope, matrix, out, grads, sums):
    for xp in range(edge.shape[1]):
        planes = logit_grads(edge, other, slope, xp)
        planes += [jnp.zeros_like(planes[0])] * 7
        for pair in range(8):
            store_tiles(grads, (xp * 16 + 2 * pair) * TILE, planes[2 * pair : 2 * pair + 2])
    total = jnp.dot(matrix[0], grads[:, :512], preferred_element_type=F32)
    sums[...] = total + jnp.dot(matrix[1], grads[:, 512:], preferred_element_type=F32)
    channels, rows_x, rows_z, _ = out.shape
    for c in range(channels):
        for x in range(rows_x):
            at = (c * rows_x + x) * TILE
            for t in range(0, rows_z // TILE, 2):
                both = [sums[at : at + TILE, s * LANES : (s + 1) * LANES] for s in (t, t + 1)]
                out[c, x, t * TILE : (t + 2) * TILE] = jnp.concatenate(both, axis=0).astype(BF16)


def local(image, filt, planted, likelihoods, slope):
    channels = image.shape[0]
    labels, rows_x, rows_z, rows_y = likelihoods.shape
    if (channels, labels, rows_x, rows_z, rows_y) != (8, 4, HALO, 4 * TILE, LANES):
        raise ValueError("brick size")
    lab, xy, gz = lax.axis_index("lab"), lax.axis_index("xy"), lax.axis_index("gz")
    colours = labels * lax.axis_size("lab")
    size_x, size_z = rows_x * lax.axis_size("xy"), rows_z * lax.axis_size("gz")
    rows = rows_z + TILE
    two = lax.axis_size("gz") > 2
    phases = range(1 + two)
    members = lax.axis_size("xy") * lax.axis_size("gz")
    info = jnp.stack(
        [
            1 - xy % 2,
            1 - gz % 2,
            xy * rows_x,
            gz * rows_z,
            lab * labels,
            1 - (xy + lab) % 2,
            jnp.minimum(xy, 1),
            jnp.minimum(lax.axis_size("xy") - 1 - xy, 1),
            jnp.minimum(gz, 1),
            jnp.minimum(lax.axis_size("gz") - 1 - gz, 1),
        ]
    ).astype(jnp.int32)

    inputs = (image, planted, likelihoods, slope)
    planes = channels + labels * rows_x + 2 * labels
    brick = shaped((planes, rows_z, LANES), BF16)
    taps = jnp.transpose(filt, (0, 2, 3, 4, 1))
    matrix, back_matrix, image, planted, likelihoods, slope, *packed = call(
        functools.partial(pack, colours, two),
        [shaped((2, 288, 384), BF16), shaped((2, 256, 768), BF16)]
        + [shaped(a.shape, a.dtype) for a in inputs]
        + [shaped((rows_x, labels, TILE, LANES), BF16)] * (1 + two)
        + [brick, brick],
        info,
        *(pltpu.with_memory_space_constraint(a, pltpu.HBM) for a in (taps, *inputs)),
        scratch=[
            pltpu.VMEM(taps.shape, BF16),
            pltpu.VMEM((112, LANES), F32),
            pltpu.SemaphoreType.DMA((5,)),
        ],
        name="pack",
        space=pltpu.HBM,
    )
    send_a, send_b = packed[1 + two :]
    faces = [z_swap(packed[phase], phase) for phase in phases]
    edges_a = [diagonal_swap(packed[phase], 0, phase) for phase in phases]
    edges_b = [diagonal_swap(packed[phase], 1, phase) for phase in phases]
    second = x_swap(send_b, 1)
    first = x_swap(send_a, 0)
    received = (first, second, *faces, *edges_a, *edges_b)

    part, stack = call(
        functools.partial(convolve, two),
        [shaped((3, rows_x, rows_z, LANES), F32), shaped((384, 1024), BF16)],
        info,
        image,
        *received,
        matrix,
        scratch=[pltpu.VMEM((288, 512), F32)],
        name="convolve",
    )
    logits, own, *sends = call(
        functools.partial(add_parts, two),
        [shaped(part.shape, F32), shaped(part.shape, BF16)]
        + [shaped((3, rows_x, TILE, LANES), BF16)] * (1 + two),
        info,
        part,
        lab_swap(part),
        name="add_parts",
    )
    mine = split_swap(own)
    mine_edges = [split_diagonal_swap(sends[phase], phase) for phase in phases]
    logit_faces = [z_swap(sends[phase], phase) for phase in phases]
    mine, mine_edges, logit_faces = lax.optimization_barrier((mine, mine_edges, logit_faces))
    other = lab_swap(mine)
    other_edges = [lab_swap(block) for block in mine_edges]
    extended = (labels, rows_x + 2 * HALO, rows, LANES)
    ring = shaped((3, rows_x + 2, rows, LANES), F32)
    v0, free, field = call(
        functools.partial(prepare, colours, two),
        [shaped(extended, F32), shaped(extended[1:], F32), shaped((labels, rows_x + 3, rows, LANES), F32)],
        info,
        planted,
        slope,
        likelihoods,
        *received,
        name="prepare",
    )
    v1, v2, squash_slope, dots = call(
        functools.partial(krylov, size_x, size_z, two),
        [shaped(extended, F32)] * 2 + [ring, shaped((members, TILE, LANES), F32)],
        info,
        v0,
        free,
        logits,
        mine,
        other,
        *logit_faces,
        *mine_edges,
        *other_edges,
        scratch=[pltpu.VMEM((5,) + extended[1:], F32), pltpu.VMEM((6 * labels, LANES), F32)],
        name="krylov",
    )
    edge = call(
        edges,
        ring,
        info,
        everyones(dots, ("xy", "gz")),
        v0,
        v1,
        v2,
        field,
        scratch=[pltpu.VMEM((labels, rows_x + 3, rows, LANES), F32)],
        name="edges",
    )
    other_edge = lab_swap(edge)
    sums = call(
        filter_sums,
        shaped((members, TILE, LANES), F32),
        info,
        edge,
        other_edge,
        squash_slope,
        stack,
        scratch=[
            pltpu.VMEM((512, 512), BF16),
            pltpu.VMEM((2, 512, 384), F32),
            pltpu.VMEM((LANES, LANES), F32),
        ],
        name="filter_sums",
    )
    grad_image = call(
        image_sums,
        shaped(image.shape, BF16),
        info,
        edge,
        other_edge,
        squash_slope,
        back_matrix,
        scratch=[pltpu.VMEM((768, 1024), BF16), pltpu.VMEM((256, 512), F32)],
        flops=10_000_000,
        name="image_sums",
    )
    grad_filter = jnp.sum(everyones(sums, ("xy", "gz")), axis=0)
    grad_filter = grad_filter[:, :81].reshape(channels, 3, 27)
    return grad_image, jnp.transpose(grad_filter, (1, 0, 2)).reshape(3, channels, 3, 3, 3)


def solution(mesh):
    return jax.shard_map(
        local,
        mesh=mesh,
        in_specs=(
            P("lab", ("crops", "xy"), "gz", None),
            P(),
            P(("crops", "xy"), "gz", None),
            P("lab", ("crops", "xy"), "gz", None),
            P("lab", ("crops", "xy"), "gz", None),
        ),
        out_specs=(P("lab", ("crops", "xy"), "gz", None), P("crops", "lab", None, None, None)),
        check_vma=False,
    )
```

```python
import functools

import jax
import jax.numpy as jnp
from jax import lax
from jax.experimental import pallas as pl
from jax.experimental.pallas import tpu as pltpu
from jax.sharding import PartitionSpec as P

HALO = 4
SEED = 64.0
SPREAD = 6.3
TILE = 8
LANES = 128
BF16, F32 = jnp.bfloat16, jnp.float32
EVEN_X, EVEN_Z, FIRST_X, FIRST_Z, COLOUR, UP, PREV_X, NEXT_X, PREV_Z, NEXT_Z = range(10)


SWAP_AXES = ("xy", "gz", "lab")


def mate(place, phase, count):
    other = place + 1 if (place - phase) % 2 == 0 else place - 1
    return other if phase <= min(place, other) and max(place, other) < count else None


def swap(block, partner):
    sizes = [lax.axis_size(axis) for axis in SWAP_AXES]
    devices = [(x, z, lab) for x in range(sizes[0]) for z in range(sizes[1]) for lab in range(sizes[2])]
    pairs = {}
    for device in devices:
        if partner(*device) is not None:
            pairs[device] = partner(*device)
    for other_of in (lambda x, z, lab: (x, z, lab ^ 1), lambda x, z, lab: (x, z ^ 1, lab)):
        for device in devices:
            other = other_of(*device)
            if device not in pairs and other in devices and other not in pairs:
                pairs[device], pairs[other] = other, device

    def flat(x, z, lab):
        return (x * sizes[1] + z) * sizes[2] + lab

    return lax.ppermute(block, SWAP_AXES, [(flat(*src), flat(*dst)) for src, dst in sorted(pairs.items())])


def x_swap(block, phase):
    count = lax.axis_size("xy")

    def partner(x, z, lab):
        other = mate(x, phase, count)
        return None if other is None else (other, z, lab)

    return swap(block, partner)


def z_swap(block, phase):
    count = lax.axis_size("gz")

    def partner(x, z, lab):
        other = mate(z, phase, count)
        return None if other is None else (x, other, lab)

    return swap(block, partner)


def diagonal_swap(block, x_phase, z_phase):
    counts = lax.axis_size("xy"), lax.axis_size("gz")

    def partner(x, z, lab):
        others = mate(x, x_phase, counts[0]), mate(z, z_phase, counts[1])
        return None if None in others else (*others, lab)

    return swap(block, partner)


def lab_swap(block):
    return lax.ppermute(block, "lab", [(0, 1), (1, 0)])


def split_swap(block):
    count = lax.axis_size("xy")

    def partner(x, z, lab):
        other = mate(x, lab % 2, count)
        return None if other is None else (other, z, lab)

    return swap(block, partner)


def split_diagonal_swap(block, z_phase):
    counts = lax.axis_size("xy"), lax.axis_size("gz")

    def partner(x, z, lab):
        others = mate(x, lab % 2, counts[0]), mate(z, z_phase, counts[1])
        return None if None in others else (*others, lab)

    return swap(block, partner)


def everyones(copies, axes):
    return lax.all_to_all(copies, axes, 0, 0)


def call(kernel, outs, *ins, scratch=(), flops=1_000_000, name=None, space=pltpu.VMEM):
    specs = [pl.BlockSpec(memory_space=pltpu.SMEM)]
    specs += [pl.BlockSpec(memory_space=space)] * (len(ins) - 1)
    bytes_moved = sum(a.size * a.dtype.itemsize for a in ins)
    return pl.pallas_call(
        kernel,
        out_shape=outs,
        in_specs=specs,
        out_specs=jax.tree.map(lambda _: pl.BlockSpec(memory_space=pltpu.VMEM), outs),
        scratch_shapes=list(scratch),
        compiler_params=pltpu.CompilerParams(vmem_limit_bytes=40 * 2**20),
        cost_estimate=pl.CostEstimate(flops=flops, bytes_accessed=bytes_moved, transcendentals=0),
        name=name,
    )(*ins)


def shaped(shape, dtype):
    return jax.ShapeDtypeStruct(shape, dtype)


def rows_iota(rows=TILE):
    return lax.broadcasted_iota(jnp.int32, (rows, LANES), 0)


def lanes_iota(rows=TILE):
    return lax.broadcasted_iota(jnp.int32, (rows, LANES), 1)


def fields(planted, likelihood, slope, colours, colour):
    free = planted >= colours
    member = jnp.where(planted == colour, 1.0, 0.0)
    return jnp.where(free, slope, SEED), jnp.where(free, likelihood, member)


def pack(
    colours,
    two,
    info,
    filt_in,
    image_in,
    planted_in,
    likelihoods_in,
    slope_in,
    wide_out,
    back_out,
    image,
    planted,
    likelihoods,
    slope,
    *refs,
):
    faces, (send_a, send_b, filt, taps, sems) = refs[: 1 + two], refs[1 + two :]
    pairs = (
        (planted_in, planted),
        (slope_in, slope),
        (likelihoods_in, likelihoods),
        (image_in, image),
        (filt_in, filt),
    )
    copies = [pltpu.make_async_copy(src, dst, sems.at[n]) for n, (src, dst) in enumerate(pairs)]
    for copy in reversed(copies):
        copy.start()
    copies[4].wait()
    spread_filter(info, filt, taps, wide_out, back_out)
    labels, rows_x, rows_z, _ = likelihoods.shape
    channels = image.shape[0]
    last, first = slice(rows_z - TILE, rows_z), slice(0, TILE)
    even = info[EVEN_X] == 1
    high, low = jnp.where(even, rows_x - 1, 0), jnp.where(even, 0, rows_x - 1)
    copies[0].wait()
    copies[1].wait()
    for x in range(rows_x):
        for l in range(labels):
            rhs = jnp.where(planted[x] >= colours, slope[l, x], SEED).astype(BF16)
            send_a[channels + l * rows_x + x] = rhs
            send_b[channels + l * rows_x + x] = rhs
    copies[2].wait()
    for l in range(labels):
        for send, at in ((send_a, high), (send_b, low)):
            for r in range(2):
                x = jnp.where(at == 0, 0, rows_x - 2) + r
                _, full = fields(planted[x], likelihoods[l, x], slope[l, x], colours, info[COLOUR] + l)
                send[channels + labels * rows_x + 2 * l + r] = full.astype(BF16)
    copies[3].wait()
    for c in range(channels):
        send_a[c] = image[c, high]
        send_b[c] = image[c, low]
    for phase, out in enumerate(faces):
        even = info[EVEN_Z] != phase
        place = (rows_iota() + jnp.where(even, 0, 4)) & 7

        def channel(c, x):
            return jnp.where(even, image[c, x, last].astype(F32), image[c, x, first].astype(F32))

        def turned(tile, for_even, for_odd):
            return jnp.where(even, pltpu.roll(tile, for_even, 0), pltpu.roll(tile, for_odd, 0))

        for x in range(rows_x):
            seeds = jnp.where(even, planted[x, last], planted[x, first])
            for l in range(labels):
                ends = [jnp.where(even, ref[l, x, last], ref[l, x, first]) for ref in (likelihoods, slope)]
                rhs, full = fields(seeds, *ends, colours, info[COLOUR] + l)
                first_channel = turned(channel(2 * l, x), 3, 6)
                second_channel = turned(channel(2 * l + 1, x), 4, 7)
                rest = jnp.where(place == 2, first_channel, second_channel)
                rest = jnp.where(place < 2, turned(full, 2, 4), rest)
                out[x, l] = jnp.where(place >= 4, rhs, rest).astype(BF16)


def sides(even, first, second):
    if second is None:
        return jnp.where(even, first, 0.0), jnp.where(even, 0.0, first)
    return jnp.where(even, first, second), jnp.where(even, second, first)


def ends_z(info, tiles, x, l):
    both = [ref[x, l].astype(F32) for ref in tiles]
    return sides(info[EVEN_Z] == 1, both[0], both[1] if len(both) > 1 else None)


def rhs_tile(above, below):
    return jnp.where(rows_iota() < 4, above, below)


def full_tile(above, below):
    return jnp.where(rows_iota() < 4, pltpu.roll(above, 4, 0), pltpu.roll(below, 6, 0))


def image_tile(info, above, below, c):
    up, down = (2, 5) if c % 2 == 0 else (1, 4)
    above = jnp.where(info[NEXT_Z] == 1, above, 0.0)
    below = jnp.where(info[PREV_Z] == 1, below, 0.0)
    return jnp.where(rows_iota() < 4, pltpu.roll(above, up, 0), pltpu.roll(below, down, 0))


def band(half, j, o, transposed=False):
    z, lane = rows_iota(), lanes_iota()
    other = lane & 7
    at = (z + 1 - other - 8 * o) if transposed else (other + 8 * o - z + 1)
    mask = at == j
    if half is not None:
        mask = mask & ((lane >> 6) == half)
    return mask


def bands(o, transposed=False):
    if o == 0:
        return (0, 1, 2)
    return (0,) if (o < 0) != transposed else (2,)


def spread_filter(info, filt, taps, wide_out, back_out):
    taps[...] = jnp.zeros_like(taps)
    for d in range(3):
        for i in range(3):
            for j in range(3):
                at = (d * 9 + i * 3 + j) * 4
                taps[at : at + 3, : filt.shape[-1]] = filt[d, i, j].astype(F32)
    lane = lanes_iota(LANES)
    channel = rows_iota(LANES) - 2 * info[COLOUR]
    all_taps = taps[...].astype(BF16)
    by_channel = jnp.where(channel == ((lane >> 3) & 7), 1.0, 0.0).astype(BF16)
    own = jnp.dot(
        all_taps, jnp.where(channel == lane, 1.0, 0.0).astype(BF16), preferred_element_type=F32
    ).astype(BF16)
    wide = jnp.dot(all_taps, by_channel, preferred_element_type=F32)
    tap, edge = rows_iota(taps.shape[0]), lanes_iota(taps.shape[0]) >> 3
    shift = jnp.where(edge >= 3, 1, 0) + jnp.where(edge >= 6, 1, 0)
    first_tap = jnp.where(edge < 9, (edge - 3 * shift) * 36 + shift, -LANES)
    places = [jnp.where(tap == first_tap + 4 * ij, 1.0, 0.0).astype(BF16) for ij in range(9)]
    back = [
        lax.dot_general(own, place, (((0,), (0,)), ((), ())), preferred_element_type=F32) for place in places
    ]
    zero = jnp.zeros((TILE, LANES), F32)
    for at_out, distances in enumerate(((0,), (-1, 1))):
        cases = [(o, j) for o in distances for j in bands(o)]
        masks = {(h, j): band(h, j, o) for h in range(2) for o, j in cases}
        for kd in range(9):
            for pair in range(2):
                for block in range(3):
                    tiles = []
                    for x in (2 * pair, 2 * pair + 1):
                        tile = zero
                        for i in range(3):
                            if (x + i) // 2 == block:
                                for _, j in cases:
                                    row = (kd % 3 * 9 + i * 3 + j) * 4 + kd // 3
                                    value = jnp.broadcast_to(wide[row : row + 1], (TILE, LANES))
                                    tile = jnp.where(masks[(x + i) % 2, j], value, tile)
                        tiles.append(tile)
                    at = (kd * 4 + 2 * pair) * TILE
                    wide_out[at_out, at : at + 16, block * LANES : (block + 1) * LANES] = jnp.concatenate(
                        tiles, axis=0
                    ).astype(BF16)
        cases = [(o, j) for o in distances for j in bands(o, True)]
        masks = {j: band(None, j, o, True) for o, j in cases}
        for c in range(8):
            for pair in range(2):
                for block in range(6):
                    tiles = []
                    for x in (2 * pair, 2 * pair + 1):
                        tile = zero
                        i = x + 2 - block
                        if 0 <= i < 3:
                            for _, j in cases:
                                value = jnp.broadcast_to(back[i * 3 + j][c : c + 1], (TILE, LANES))
                                tile = jnp.where(masks[j], value, tile)
                        tiles.append(tile)
                    at = (c * 4 + 2 * pair) * TILE
                    back_out[at_out, at : at + 16, block * LANES : (block + 1) * LANES] = jnp.concatenate(
                        tiles, axis=0
                    ).astype(BF16)


def store_tiles(out, at, planes):
    for t in range(4):
        both = jnp.concatenate([plane[tile_rows(t)] for plane in planes], axis=0)
        out[at : at + 16, t * LANES : (t + 1) * LANES] = both.astype(BF16)
        both = [jnp.where(rows_iota() < 4, plane[tile_rows(t + 1)], plane[tile_rows(t - 1)]) for plane in planes]
        both = jnp.concatenate(both, axis=0)
        out[at : at + 16, (t + 4) * LANES : (t + 5) * LANES] = both.astype(BF16)


def tile_rows(t):
    at = (4 if t < 0 else t) * TILE
    return slice(at, at + TILE)


def convolve(two, info, image, first, second, *refs):
    faces, edges_a, edges_b = refs[: 1 + two], refs[1 + two : 2 + 2 * two], refs[2 + 2 * two : 3 + 3 * two]
    matrix, part, stack, sums = refs[3 + 3 * two :]
    channels, rows_x = image.shape[0], image.shape[1]
    even = info[EVEN_X] == 1
    for xp in range(rows_x + 2):
        for c in range(0, channels, 2):
            planes = []
            if 0 < xp <= rows_x:
                ends = [ends_z(info, faces, xp - 1, c // 2)]
            else:
                ends = [ends_z(info, tiles, rows_x - 1 if xp == 0 else 0, c // 2) for tiles in (edges_a, edges_b)]
            for ch in (c, c + 1):
                tiles = [image_tile(info, *pair, ch) for pair in ends]
                if 0 < xp <= rows_x:
                    planes.append(jnp.concatenate([image[ch, xp - 1].astype(F32), tiles[0]], axis=0))
                else:
                    received = [
                        jnp.concatenate([ref[ch].astype(F32), tile], axis=0)
                        for ref, tile in zip((first, second), tiles)
                    ]
                    above, below = sides(even, *received)
                    plane, exists = (below, PREV_X) if xp == 0 else (above, NEXT_X)
                    planes.append(jnp.where(info[exists] == 1, plane, 0.0))
            at = (xp * channels + c) * TILE
            store_tiles(stack, at, planes)
    total = jnp.dot(matrix[0], stack[:, :512], preferred_element_type=F32)
    sums[...] = total + jnp.dot(matrix[1], stack[:, 512:], preferred_element_type=F32)
    lane = lanes_iota()
    for d in range(3):
        for x in range(rows_x):
            for t in range(4):
                cols = slice(t * LANES, (t + 1) * LANES)

                def piece(k):
                    at = ((k * 3 + d) * rows_x + x) * TILE
                    return sums[at : at + TILE, cols]

                before = jnp.where(lane > 0, pltpu.roll(piece(0), 1, 1), 0.0)
                after = jnp.where(lane < LANES - 1, pltpu.roll(piece(2), LANES - 1, 1), 0.0)
                part[d, x, tile_rows(t)] = (piece(1) + before + after).astype(BF16)


def add_parts(two, info, part, other, logits, brick, *faces):
    rows_x, rows_z = part.shape[1], part.shape[2]
    for d in range(3):
        for x in range(rows_x):
            total = part[d, x].astype(F32) + other[d, x].astype(F32)
            logits[d, x] = total
            brick[d, x] = total.astype(BF16)
            for phase, face in enumerate(faces):
                even = info[EVEN_Z] != phase
                face[d, x] = jnp.where(even, total[rows_z - TILE :], total[:TILE]).astype(BF16)


def up(plane, dim):
    return pltpu.roll(plane, plane.shape[dim] - 1, dim)


def down(plane, dim):
    return pltpu.roll(plane, 1, dim)


def prepare(colours, two, info, planted, slope, likelihoods, first, second, *refs):
    faces, edges_a, edges_b = refs[: 1 + two], refs[1 + two : 2 + 2 * two], refs[2 + 2 * two : 3 + 3 * two]
    v0, free, field = refs[3 + 3 * two :]
    labels, rows_x, _, _ = slope.shape
    channels = 2 * labels
    even = info[EVEN_X] == 1

    def grown(index, source, l, tile):
        received = [
            jnp.concatenate([ref[index].astype(F32), tile(*ends_z(info, tiles, source, l))], axis=0)
            for ref, tiles in ((first, edges_a), (second, edges_b))
        ]
        return sides(even, *received)

    for x in range(rows_x):
        for l in range(labels):
            ends = ends_z(info, faces, x, l)
            rhs, full = fields(planted[x], likelihoods[l, x], slope[l, x], colours, info[COLOUR] + l)
            rhs = jnp.concatenate([rhs, rhs_tile(*ends)], axis=0)
            field[l, x + 1] = jnp.concatenate([full, full_tile(*ends)], axis=0)
            above, below = grown(channels + l * rows_x + x, x, l, rhs_tile)
            for at, plane in ((x + HALO, rhs), (x, below), (x + HALO + rows_x, above)):
                open_cell = plane < SEED / 2
                v0[l, at] = jnp.where(open_cell, plane, 0.0)
                if l == 0:
                    free[at] = jnp.where(open_cell, 1.0, 0.0)
    for l in range(labels):
        base = 2 * labels + labels * rows_x + 2 * l
        field[l, 0] = grown(base + 1, rows_x - 1, l, full_tile)[1]
        for r in range(2):
            field[l, rows_x + 1 + r] = grown(base + r, r, l, full_tile)[0]


def krylov(size_x, size_z, two, info, v0, free, logits, mine, other, *refs):
    faces, mine_edges, other_edges = (refs[n * (1 + two) : (n + 1) * (1 + two)] for n in range(3))
    v1, v2, slope_out, dots_out, weight, dots = refs[3 * (1 + two) :]
    labels, _, rows, _ = v0.shape
    rows_x, rows_z = logits.shape[1:3]
    is_up = info[UP] == 1
    z = rows_iota(rows)
    z = info[FIRST_Z] + jnp.where(z < rows_z + HALO, z, z - rows)
    inside_z = (z >= 0) & (z < size_z)
    in_z = jnp.where(inside_z, 1.0, 0.0)
    next_z = jnp.where(inside_z & (z < size_z - 1), 1.0, 0.0)
    in_zy = jnp.where(lanes_iota(rows) < LANES - 1, in_z, 0.0)
    for at in range(1, rows_x + 2 * HALO - 1):
        x = at - HALO
        place = info[FIRST_X] + x
        inside = (place >= 0) & (place < size_x)
        in_x = jnp.where(inside, 1.0, 0.0)
        next_x = jnp.where(inside & (place < size_x - 1), 1.0, 0.0)
        for d in range(3):
            def grown(plane, tiles, source):
                return jnp.concatenate([plane, rhs_tile(*ends_z(info, tiles, d, source))], axis=0)

            if 0 <= x < rows_x:
                plane = grown(logits[d, x], faces, x)
            else:
                source = x % rows_x
                here = grown(mine[d, source].astype(F32), mine_edges, source)
                there = grown(other[d, source].astype(F32), other_edges, source)
                plane = jnp.where(is_up, there, here) if x < 0 else jnp.where(is_up, here, there)
            squashed = 1.0 / (1.0 + jnp.exp(-plane))
            valid = (in_z * next_x, next_z * in_x, in_zy * in_x)[d]
            edge_weight = (0.05 + squashed) * valid
            weight[d, at] = edge_weight
            if d > 0:
                weight[2 + d, at] = down(edge_weight, d - 1)
            if -1 <= x <= rows_x:
                slope_out[d, x + 1] = squashed * (1.0 - squashed) * valid

    def label(l, carry):
        def operate(v, start, stop):
            flow_before = weight[0, start - 1] * (v[l, start - 1] - v[l, start])
            for at in range(start, stop):
                here = v[l, at]
                flow = weight[0, at] * (here - v[l, at + 1])
                result = flow - flow_before
                for dim in range(2):
                    result = result + weight[1 + dim, at] * (here - up(here, dim))
                    result = result + weight[3 + dim, at] * (here - down(here, dim))
                yield at, here, free[at] * result
                flow_before = flow

        for at, here, result in operate(v0, 2, rows_x + 2 * HALO - 1):
            v1[l, at] = result * (1.0 / SPREAD) - here
        for at, here, result in operate(v1, 3, rows_x + 2 * HALO - 2):
            v2[l, at] = result * (2.0 / SPREAD) - 2.0 * here - v0[l, at]
        sums = [jnp.zeros((TILE, LANES), F32)] * 6
        for at, here, result in operate(v2, HALO, HALO + rows_x):
            a, b = v0[l, at], v1[l, at]
            for n, product in enumerate((a * a, a * b, b * b, b * here, here * here, here * result)):
                for t in range(rows_z // TILE):
                    sums[n] = sums[n] + product[tile_rows(t)]
        for n in range(6):
            dots[pl.ds(n * labels + l, 1), :] = jnp.sum(sums[n], axis=0, keepdims=True)
        return carry

    lax.fori_loop(0, labels, label, 0)
    total = jnp.sum(dots[...], axis=1, keepdims=True)
    tile = jnp.zeros((TILE, LANES), F32)
    for n in range(6):
        column = total[tile_rows(n // 2)]
        column = jnp.broadcast_to(column, (TILE, LANES))
        tile = jnp.where(lanes_iota() == n, pltpu.roll(column, 4, 0) if n % 2 else column, tile)
    for n in range(dots_out.shape[0]):
        dots_out[n] = tile


def steps(g00, g01, g11, g12, g22, k22):
    g02 = 2.0 * g11 - g00
    k00 = SPREAD * (g00 + g01)
    k01 = SPREAD * (g01 + g11)
    k02 = SPREAD * (g02 + g12)
    k11 = SPREAD * (g11 + 0.5 * (g12 + g01))
    k12 = SPREAD * (g12 + 0.5 * (g22 + g02))
    alpha = g00 / k00
    c0 = alpha
    r0 = 1.0 - alpha * SPREAD
    r1 = -alpha * SPREAD
    rr = r0 * r0 * g00 + 2.0 * r0 * r1 * g01 + r1 * r1 * g11
    beta = rr / g00
    p0, p1 = r0 + beta, r1
    alpha = rr / (p0 * p0 * k00 + 2.0 * p0 * p1 * k01 + p1 * p1 * k11)
    c0, c1 = c0 + alpha * p0, alpha * p1
    r0 = r0 - alpha * SPREAD * (p0 + 0.5 * p1)
    r1 = r1 - alpha * SPREAD * (p0 + p1)
    r2 = -alpha * SPREAD * 0.5 * p1
    rr_next = r0 * r0 * g00 + r1 * r1 * g11 + r2 * r2 * g22
    rr_next = rr_next + 2.0 * (r0 * r1 * g01 + r0 * r2 * g02 + r1 * r2 * g12)
    beta = rr_next / rr
    p0, p1, p2 = r0 + beta * p0, r1 + beta * p1, r2
    curve = p0 * p0 * k00 + p1 * p1 * k11 + p2 * p2 * k22
    curve = curve + 2.0 * (p0 * p1 * k01 + p0 * p2 * k02 + p1 * p2 * k12)
    alpha = rr_next / curve
    return c0 + alpha * p0, c1 + alpha * p1, alpha * p2


def edges(info, parts, v0, v1, v2, field, out, lam):
    labels, _, rows, _ = v0.shape
    rows_x = out.shape[1] - 2
    total = jnp.sum(parts[...], axis=0)
    grams = [jnp.broadcast_to(total[:, n : n + 1], (TILE, LANES)) for n in range(6)]
    c0, c1, c2 = steps(*grams)
    for l in range(labels):
        s0, s1, s2 = (jnp.broadcast_to(c[l : l + 1], (rows, LANES)) for c in (c0, c1, c2))
        for at in range(rows_x + 3):
            source = at + HALO - 1
            lam[l, at] = s0 * v0[l, source] + s1 * v1[l, source] + s2 * v2[l, source]
    for at in range(rows_x + 2):
        sums = [jnp.zeros((rows, LANES), F32)] * 3
        for l in range(labels):
            a, b = lam[l, at], field[l, at]
            sums[0] = sums[0] - (a - lam[l, at + 1]) * (b - field[l, at + 1])
            sums[1] = sums[1] - (a - up(a, 0)) * (b - up(b, 0))
            sums[2] = sums[2] - (a - up(a, 1)) * (b - up(b, 1))
        for d in range(3):
            out[d, at] = sums[d]


def logit_grads(edge, other, slope, xp):
    lane = lanes_iota(edge.shape[2])
    shifted = [[], [], []]
    for d in range(3):
        plane = ((edge[d, xp] + other[d, xp]) * slope[d, xp]).astype(BF16).astype(F32)
        shifted[0].append(jnp.where(lane < LANES - 1, up(plane, 1), 0.0))
        shifted[1].append(plane)
        shifted[2].append(jnp.where(lane > 0, down(plane, 1), 0.0))
    return shifted[0] + shifted[1] + shifted[2]


def filter_sums(info, edge, other, slope, stack, out, own, products, rows_out):
    rows_x = edge.shape[1] - 2
    for x in range(rows_x):
        planes = logit_grads(edge, other, slope, x + 1)
        planes.append(jnp.zeros_like(planes[0]))
        for pair in range(5):
            at = (x * 16 + 2 * pair) * TILE
            for t in range(4):
                both = jnp.concatenate([plane[tile_rows(t)] for plane in planes[2 * pair : 2 * pair + 2]], axis=0)
                own[at : at + 16, t * LANES : (t + 1) * LANES] = both.astype(BF16)
        own[(x * 16 + 10) * TILE : (x + 1) * 16 * TILE, :] = jnp.zeros((6 * TILE, 4 * LANES), BF16)
    for n in range(2):
        products[n] = lax.dot_general(
            own[...], stack[:, 512 * n : 512 * (n + 1)], (((1,), (1,)), ((), ())), preferred_element_type=F32
        )
    rows_out[...] = jnp.zeros_like(rows_out)
    masks = {(h, j, o): band(h, j, o) for o in (-1, 0, 1) for h in range(2) for j in bands(o)}
    for kd in range(9):
        k, d = kd // 3, kd % 3
        for i in range(3):
            for j in range(3):
                total = jnp.zeros((TILE, LANES), F32)
                for o in (-1, 0, 1):
                    if j in bands(o):
                        for x in range(rows_x):
                            at = (x * 16 + kd) * TILE
                            col = (x + i) // 2 * LANES
                            piece = products[abs(o), at : at + TILE, col : col + LANES]
                            total = total + jnp.where(masks[(x + i) % 2, j, o], piece, 0.0)
                row = d * 27 + i * 9 + j * 3 + k
                rows_out[row : row + 1] = jnp.sum(total, axis=0, keepdims=True)
    sums = lax.dot_general(
        jnp.where(((lanes_iota() >> 3) & 7) == rows_iota(), 1.0, 0.0),
        rows_out[...],
        (((1,), (1,)), ((), ())),
        precision=lax.Precision.HIGHEST,
        preferred_element_type=F32,
    )
    for n in range(out.shape[0]):
        out[n] = sums


def image_sums(info, edge, other, slope, matrix, out, grads, sums):
    for xp in range(edge.shape[1]):
        planes = logit_grads(edge, other, slope, xp)
        planes += [jnp.zeros_like(planes[0])] * 7
        for pair in range(8):
            store_tiles(grads, (xp * 16 + 2 * pair) * TILE, planes[2 * pair : 2 * pair + 2])
    total = jnp.dot(matrix[0], grads[:, :512], preferred_element_type=F32)
    sums[...] = total + jnp.dot(matrix[1], grads[:, 512:], preferred_element_type=F32)
    channels, rows_x, rows_z, _ = out.shape
    for c in range(channels):
        for x in range(rows_x):
            at = (c * rows_x + x) * TILE
            for t in range(0, rows_z // TILE, 2):
                both = [sums[at : at + TILE, s * LANES : (s + 1) * LANES] for s in (t, t + 1)]
                out[c, x, t * TILE : (t + 2) * TILE] = jnp.concatenate(both, axis=0).astype(BF16)


def local(image, filt, planted, likelihoods, slope):
    channels = image.shape[0]
    labels, rows_x, rows_z, rows_y = likelihoods.shape
    if (channels, labels, rows_x, rows_z, rows_y) != (8, 4, HALO, 4 * TILE, LANES):
        raise ValueError("brick size")
    lab, xy, gz = lax.axis_index("lab"), lax.axis_index("xy"), lax.axis_index("gz")
    colours = labels * lax.axis_size("lab")
    size_x, size_z = rows_x * lax.axis_size("xy"), rows_z * lax.axis_size("gz")
    rows = rows_z + TILE
    two = lax.axis_size("gz") > 2
    phases = range(1 + two)
    members = lax.axis_size("xy") * lax.axis_size("gz")
    info = jnp.stack(
        [
            1 - xy % 2,
            1 - gz % 2,
            xy * rows_x,
            gz * rows_z,
            lab * labels,
            1 - (xy + lab) % 2,
            jnp.minimum(xy, 1),
            jnp.minimum(lax.axis_size("xy") - 1 - xy, 1),
            jnp.minimum(gz, 1),
            jnp.minimum(lax.axis_size("gz") - 1 - gz, 1),
        ]
    ).astype(jnp.int32)

    inputs = (image, planted, likelihoods, slope)
    planes = channels + labels * rows_x + 2 * labels
    brick = shaped((planes, rows_z, LANES), BF16)
    taps = jnp.transpose(filt, (0, 2, 3, 4, 1))
    matrix, back_matrix, image, planted, likelihoods, slope, *packed = call(
        functools.partial(pack, colours, two),
        [shaped((2, 288, 384), BF16), shaped((2, 256, 768), BF16)]
        + [shaped(a.shape, a.dtype) for a in inputs]
        + [shaped((rows_x, labels, TILE, LANES), BF16)] * (1 + two)
        + [brick, brick],
        info,
        *(pltpu.with_memory_space_constraint(a, pltpu.HBM) for a in (taps, *inputs)),
        scratch=[
            pltpu.VMEM(taps.shape, BF16),
            pltpu.VMEM((112, LANES), F32),
            pltpu.SemaphoreType.DMA((5,)),
        ],
        name="pack",
        space=pltpu.HBM,
    )
    send_a, send_b = packed[1 + two :]
    faces = [z_swap(packed[phase], phase) for phase in phases]
    edges_a = [diagonal_swap(packed[phase], 0, phase) for phase in phases]
    edges_b = [diagonal_swap(packed[phase], 1, phase) for phase in phases]
    second = x_swap(send_b, 1)
    first = x_swap(send_a, 0)
    received = (first, second, *faces, *edges_a, *edges_b)

    part, stack = call(
        functools.partial(convolve, two),
        [shaped((3, rows_x, rows_z, LANES), BF16), shaped((384, 1024), BF16)],
        info,
        image,
        *received,
        matrix,
        scratch=[pltpu.VMEM((288, 512), F32)],
        name="convolve",
    )
    logits, own, *sends = call(
        functools.partial(add_parts, two),
        [shaped(part.shape, F32), shaped(part.shape, BF16)]
        + [shaped((3, rows_x, TILE, LANES), BF16)] * (1 + two),
        info,
        part,
        lab_swap(part),
        name="add_parts",
    )
    mine = split_swap(own)
    mine_edges = [split_diagonal_swap(sends[phase], phase) for phase in phases]
    logit_faces = [z_swap(sends[phase], phase) for phase in phases]
    mine, mine_edges, logit_faces = lax.optimization_barrier((mine, mine_edges, logit_faces))
    other = lab_swap(mine)
    other_edges = [lab_swap(block) for block in mine_edges]
    extended = (labels, rows_x + 2 * HALO, rows, LANES)
    ring = shaped((3, rows_x + 2, rows, LANES), F32)
    v0, free, field = call(
        functools.partial(prepare, colours, two),
        [shaped(extended, F32), shaped(extended[1:], F32), shaped((labels, rows_x + 3, rows, LANES), F32)],
        info,
        planted,
        slope,
        likelihoods,
        *received,
        name="prepare",
    )
    v1, v2, squash_slope, dots = call(
        functools.partial(krylov, size_x, size_z, two),
        [shaped(extended, F32)] * 2 + [ring, shaped((members, TILE, LANES), F32)],
        info,
        v0,
        free,
        logits,
        mine,
        other,
        *logit_faces,
        *mine_edges,
        *other_edges,
        scratch=[pltpu.VMEM((5,) + extended[1:], F32), pltpu.VMEM((6 * labels, LANES), F32)],
        name="krylov",
    )
    edge = call(
        edges,
        ring,
        info,
        everyones(dots, ("xy", "gz")),
        v0,
        v1,
        v2,
        field,
        scratch=[pltpu.VMEM((labels, rows_x + 3, rows, LANES), F32)],
        name="edges",
    )
    other_edge = lab_swap(edge)
    sums = call(
        filter_sums,
        shaped((members, TILE, LANES), F32),
        info,
        edge,
        other_edge,
        squash_slope,
        stack,
        scratch=[
            pltpu.VMEM((512, 512), BF16),
            pltpu.VMEM((2, 512, 384), F32),
            pltpu.VMEM((LANES, LANES), F32),
        ],
        name="filter_sums",
    )
    grad_image = call(
        image_sums,
        shaped(image.shape, BF16),
        info,
        edge,
        other_edge,
        squash_slope,
        back_matrix,
        scratch=[pltpu.VMEM((768, 1024), BF16), pltpu.VMEM((256, 512), F32)],
        flops=10_000_000,
        name="image_sums",
    )
    grad_filter = jnp.sum(everyones(sums, ("xy", "gz")), axis=0)
    grad_filter = grad_filter[:, :81].reshape(channels, 3, 27)
    return grad_image, jnp.transpose(grad_filter, (1, 0, 2)).reshape(3, channels, 3, 3, 3)


def solution(mesh):
    return jax.shard_map(
        local,
        mesh=mesh,
        in_specs=(
            P("lab", ("crops", "xy"), "gz", None),
            P(),
            P(("crops", "xy"), "gz", None),
            P("lab", ("crops", "xy"), "gz", None),
            P("lab", ("crops", "xy"), "gz", None),
        ),
        out_specs=(P("lab", ("crops", "xy"), "gz", None), P("crops", "lab", None, None, None)),
        check_vma=False,
    )
```
